32 devices in a mesh: groups: 2 (over y), tm: 4 (over x, core), rows: 4 (over z).
Axes of the slice: x: 2, y: 2, z: 4, core: 2. Of those that a mesh axis runs over, the one named last changes fastest.
Arguments:
- starts: float32 [8, 256, 4096], P(('groups', 'tm'), 'rows'), parts along dimension 0, may hold values from -1.2 to 1.2
- drive: float32 [256, 4096], P('rows'), may hold values from -0.6 to 0.6
Outputs:
- ends: float32 [8, 256, 4096], P(('groups', 'tm'), 'rows'), parts along dimension 0
The draws below stay inside these ranges and needn't reach their ends.
There are 2 independent parts, one for each index of `groups`. The reference program is written for one: setup_inputs(seed, part) draws one part's arguments, and reference() takes and returns one part's arrays. A program takes and returns all parts, laid end to end along the dimension named above; an argument that names none is the same for every part. Nothing has to cross between parts.
All inputs are finite; a program needn't handle non-finite values.
Results may differ from the reference program's by a relative error of at most 0.00002.
Values sent between devices are 32-bit elements; how exact they have to be, the bound alone decides.
No kernel may reach another device: no remote copies, remote signals or barrier semaphores. Data moves between devices by JAX's collectives and lax.ppermute only.
A program may use at most 64 MiB of HBM per device.

```python
import jax
import jax.numpy as jnp

NY = 4096
FINE = 3
SLICES = 4
NX = 256


def levels(rng, dims, cuts, least, high):
    loudness = 1.0
    for position, parts in cuts:
        draws = jax.random.uniform(jax.random.fold_in(jax.random.fold_in(rng, 6), position), (parts,), jnp.float32, least / len(cuts), high / len(cuts))
        loudness = loudness * jnp.repeat(jnp.exp(draws), dims[position] // parts).reshape((-1,) + (1,) * (len(dims) - 1 - position))
    return loudness


def setup_inputs(seed: int = 0, part: int = 0) -> dict:
    splits = jax.random.split(jax.random.key(seed), 3)
    own_keys = jax.random.split(jax.random.fold_in(splits[2], part), 3)
    starts = jnp.clip(jax.random.uniform(own_keys[0], (SLICES, NX, NY), jnp.float32, -1.2, 1.2) * levels(own_keys[0], (SLICES, NX, NY), ((0, 4), (1, 4)), -0.4, 0.0), -1.2, 1.2)
    drive = jnp.clip(jax.random.uniform(splits[1], (NX, NY), jnp.float32, -0.6, 0.6) * levels(splits[1], (NX, NY), ((0, 4),), -0.4, 0.0), -0.6, 0.6)
    return {"starts": starts, "drive": drive}


diffusion = 2.0
step_fine = 0.1


def neighbour_sum(padded):
    centre = padded[1:-1]
    return padded[2:] + padded[:-2] + jnp.roll(centre, 1, axis=1) + jnp.roll(centre, -1, axis=1)


def fine_update(padded, drive):
    centre = padded[1:-1]
    nsum = neighbour_sum(padded)
    return centre + step_fine * (diffusion * (nsum - 4.0 * centre) + centre - centre * centre * centre + drive)


def coarse_update(padded, drive, coarse_step):
    centre = padded[1:-1]
    nsum = neighbour_sum(padded)
    return (centre + coarse_step * (diffusion * nsum + centre - centre * centre * centre + drive)) / (1.0 + 4.0 * diffusion * coarse_step)


def pad_rows(field):
    return jnp.pad(field, ((1, 1), (0, 0)))


def reference(starts, drive):
    coarse_step = FINE * step_fine
    ends = []
    current = starts[0]
    for slice_id in range(SLICES):
        fine_field = starts[slice_id]
        for step in range(FINE):
            fine_field = fine_update(pad_rows(fine_field), drive)
        delta = fine_field - coarse_update(pad_rows(starts[slice_id]), drive, coarse_step)
        current = coarse_update(pad_rows(current), drive, coarse_step) + delta
        ends.append(current)
    return jnp.stack(ends)
```

```python
import jax
import jax.numpy as jnp
from jax import lax
from jax.sharding import PartitionSpec as P

FINE = 3
WIDE = 8


diffusion = 2.0
step_fine = 0.1
coarse_step = FINE * step_fine

AXES = ("groups", "tm", "rows")


def routed(block, route):
    groups, slices, rows = (lax.axis_size(a) for a in AXES)
    pairs = []
    for g in range(groups):
        for t in range(slices):
            for r in range(rows):
                to_t, to_r = route(t, r)
                pairs.append(((g * slices + t) * rows + r, (g * slices + to_t) * rows + to_r))
    return lax.ppermute(block, AXES, pairs)


def partner(t, r):
    return t ^ 1, r


def outward(slices, rows):
    def route(t, r):
        to_r = r + 1 if t & 1 else r - 1
        if 0 <= to_r < rows:
            return t ^ 1, to_r
        other = t ^ 2
        return (other, r) if other < slices else (t, r)

    return route


def stage_swap(stage, slices):
    def route(t, r):
        chip = t // 2
        if chip == stage:
            return t + 2, r
        if chip == stage + 1:
            return t - 2, r
        return t, r

    return route


def neighbour_sum(field):
    return (
        jnp.roll(field, 1, axis=0)
        + jnp.roll(field, -1, axis=0)
        + jnp.roll(field, 1, axis=1)
        + jnp.roll(field, -1, axis=1)
    )


def fine_update(v, drive, inside):
    nsum = neighbour_sum(v)
    new = v + step_fine * (diffusion * (nsum - 4.0 * v) + v - v * v * v + drive)
    return jnp.where(inside, new, 0.0)


def coarse_update(v, drive, inside):
    nsum = neighbour_sum(v)
    new = (v + coarse_step * (diffusion * nsum + v - v * v * v + drive)) / (
        1.0 + 4.0 * diffusion * coarse_step
    )
    return jnp.where(inside, new, 0.0)


def on_device(starts, drive):
    own = starts[0]
    height = own.shape[0]
    half = height // 2
    slices, rows = lax.axis_size("tm"), lax.axis_size("rows")
    chips = slices // 2
    t, r = lax.axis_index("tm"), lax.axis_index("rows")
    core, chip = t % 2, t // 2
    first = core == 0
    away = outward(slices, rows)

    other = routed(own, partner)
    s_a = jnp.where(first, own, other)
    s_b = jnp.where(first, other, own)

    edge = core * (height - WIDE)
    near = core * (half - WIDE)

    def cut(field, start, size):
        return lax.dynamic_slice_in_dim(field, start, size, axis=0)

    sent = jnp.concatenate([cut(f, edge, WIDE) for f in (s_a, s_b, drive)])
    got = routed(sent, away)

    def window(field, place):
        body = cut(field, near, half + WIDE)
        side = got[place * WIDE : (place + 1) * WIDE]
        return jnp.where(
            first, jnp.concatenate([side, body]), jnp.concatenate([body, side])
        )

    w_a, w_b, w_d = (window(f, i) for i, f in enumerate((s_a, s_b, drive)))
    span = half + 2 * WIDE
    row = r * height + core * half - WIDE + lax.broadcasted_iota(jnp.int32, (span, 1), 0)
    inside = (row >= 0) & (row < rows * height)
    w_a = jnp.where(inside, w_a, 0.0)
    w_b = jnp.where(inside, w_b, 0.0)

    def fine(v):
        for _ in range(FINE):
            v = fine_update(v, w_d, inside)
        return v

    d_a = fine(w_a) - coarse_update(w_a, w_d, inside)
    d_b = fine(w_b) - coarse_update(w_b, w_d, inside)

    def chain(v):
        e_a = coarse_update(v, w_d, inside) + d_a
        e_b = coarse_update(e_a, w_d, inside) + d_b
        return e_a, e_b

    def extended(v):
        inner = routed(cut(v, jnp.where(first, WIDE + half - 2, WIDE), 2), partner)
        outer = routed(cut(v, jnp.where(first, WIDE, WIDE + half - 2), 2), away)
        body = v[WIDE : WIDE + half]
        above = jnp.where(first, outer, inner)
        below = jnp.where(first, inner, outer)
        return jnp.concatenate([above, body, below])

    e_a, e_b = chain(w_a)
    for stage in range(chips - 1):
        moved = e_b[WIDE - 2 : WIDE + half + 2] if stage == 0 else extended(e_b)
        arrived = routed(moved, stage_swap(stage, slices))
        current = jnp.pad(arrived, ((WIDE - 2, WIDE - 2), (0, 0)))
        current = jnp.where(inside, current, 0.0)
        n_a, n_b = chain(current)
        here = chip == stage + 1
        e_a = jnp.where(here, n_a, e_a)
        e_b = jnp.where(here, n_b, e_b)

    e_a, e_b = e_a[WIDE : WIDE + half], e_b[WIDE : WIDE + half]
    back = routed(jnp.where(first, e_b, e_a), partner)
    top = jnp.where(first, e_a, back)
    low = jnp.where(first, back, e_b)
    return jnp.concatenate([top, low])[None]


def solution(mesh):
    in_specs = (P(("groups", "tm"), "rows", None), P("rows", None))
    out_specs = P(("groups", "tm"), "rows", None)
    return jax.shard_map(
        on_device, mesh=mesh, in_specs=in_specs, out_specs=out_specs, check_vma=False
    )
```

```python
import functools

import jax
import jax.numpy as jnp
from jax import lax
from jax.experimental import pallas as pl
from jax.experimental.pallas import tpu as pltpu
from jax.sharding import PartitionSpec as P

FINE = 3
WIDE = 8
CUT = 4


diffusion = 2.0
step_fine = 0.1
coarse_step = FINE * step_fine
damping = 1.0 + 4.0 * diffusion * coarse_step

AXES = ("groups", "tm", "rows")


def routed(block, route):
    groups, slices, rows = (lax.axis_size(a) for a in AXES)
    pairs = []
    for g in range(groups):
        for t in range(slices):
            for r in range(rows):
                to_g, to_t, to_r = route(g, t, r)
                source = (g * slices + t) * rows + r
                pairs.append((source, (to_g * slices + to_t) * rows + to_r))
    return lax.ppermute(block, AXES, pairs)


def partner(g, t, r):
    return g, t ^ 1, r


def outward(groups, rows):
    def route(g, t, r):
        to_r = r + 1 if t & 1 else r - 1
        if 0 <= to_r < rows:
            return g, t ^ 1, to_r
        other = g ^ 1
        return (other, t, r) if other < groups else (g, t, r)

    return route


def stage_swap(stage):
    def route(g, t, r):
        chip = t // 2
        if chip == stage:
            return g, t + 2, r
        if chip == stage + 1:
            return g, t - 2, r
        return g, t, r

    return route


def around(v):
    height, width = v.shape
    return (pltpu.roll(v, 1, 0) + pltpu.roll(v, height - 1, 0)) + (
        pltpu.roll(v, 1, 1) + pltpu.roll(v, width - 1, 1)
    )


def fine_of(v, nsum, drive):
    return (
        step_fine * diffusion * nsum
        + v * ((1.0 + step_fine - 4.0 * step_fine * diffusion) - step_fine * (v * v))
        + step_fine * drive
    )


def coarse_of(v, nsum, drive):
    scale = coarse_step / damping
    return (
        scale * diffusion * nsum
        + v * ((1.0 + coarse_step) / damping - scale * (v * v))
        + scale * drive
    )


def compute(kernel, outs, args, **kwargs):
    shapes = [jax.ShapeDtypeStruct(o, jnp.float32) for o in outs]
    vmem = pl.BlockSpec(memory_space=pltpu.VMEM)
    return pl.pallas_call(
        kernel,
        out_shape=shapes,
        in_specs=[vmem] * len(args),
        out_specs=[vmem] * len(outs),
        compiler_params=pltpu.CompilerParams(vmem_limit_bytes=12 << 20),
        **kwargs,
    )(*args)


def first_pass(a, b, drive, inside=None):
    def kept(v):
        return v if inside is None else jnp.where(inside, v, 0.0)

    def delta(v):
        nsum = around(v)
        coarse = coarse_of(v, nsum, drive)
        fine = kept(fine_of(v, nsum, drive))
        for _ in range(FINE - 1):
            fine = kept(fine_of(fine, around(fine), drive))
        return kept(coarse), kept(fine - coarse)

    coarse_a, d_a = delta(a)
    _, d_b = delta(b)
    e_a = coarse_a + d_a
    e_b = kept(coarse_of(e_a, around(e_a), drive) + d_b)
    return d_a, d_b, e_b


def chain(current, d_a, d_b, drive, inside=None):
    e_a = coarse_of(current, around(current), drive) + d_a
    if inside is not None:
        e_a = jnp.where(inside, e_a, 0.0)
    e_b = coarse_of(e_a, around(e_a), drive) + d_b
    return e_a, e_b


def picked(first, own, other):
    return jnp.where(first, own, other), jnp.where(first, other, own)


def tiles(ref, kind, start, count):
    height = ref.shape[0] // 4
    return ref[pl.ds(kind * height + 8 * start, 8 * count), :]


def put(ref, kind, start, value):
    height = ref.shape[0] // 4
    ref[pl.ds(kind * height + 8 * start, value.shape[0]), :] = value


def mixed(upper, lower):
    row = lax.broadcasted_iota(jnp.int32, upper.shape, 0)
    return jnp.where(row < CUT, upper, lower)


def inner_kernel(half, own, other, drive, sent, state, edge):
    core = lax.axis_index("tm") % 2
    first = core == 0
    height = 2 * half
    row = pl.multiple_of(half - 16 + 8 * core, 8)
    a, b = picked(first, own[pl.ds(row, 24), :], other[pl.ds(row, 24), :])
    d = drive[pl.ds(row, 24), :]
    d_a, d_b, e_b = first_pass(a, b, d)
    sent[...] = pltpu.roll(e_b, 24 - CUT, 0)[:16]
    for kind, v in enumerate((d_a, d_b, d, a)):
        put(state, kind, 0, v)
    row = pl.multiple_of((height - WIDE) * core, 8)
    a, b = picked(first, own[pl.ds(row, 8), :], other[pl.ds(row, 8), :])
    edge[0:8, :] = a
    edge[8:16, :] = b
    edge[16:24, :] = drive[pl.ds(row, 8), :]


def middle_kernel(half, own, other, drive, inner, sent, state):
    core = lax.axis_index("tm") % 2
    first = core == 0
    row = pl.multiple_of((half + 8) * core, 8)
    a, b = picked(first, own[pl.ds(row, 24), :], other[pl.ds(row, 24), :])
    d = drive[pl.ds(row, 24), :]
    d_a, d_b, e_b = first_pass(a, b, d)
    sent[...] = pltpu.roll(e_b, 24 - CUT, 0)[:16]
    fields = (d_a, d_b, d, a)

    @pl.when(first)
    def _():
        for kind, v in enumerate(fields):
            put(state, kind, 0, v[:16])
            put(state, kind, 2, mixed(v[16:], tiles(inner, kind, 0, 1)))
            put(state, kind, 3, tiles(inner, kind, 1, 1))

    @pl.when(core == 1)
    def _():
        for kind, v in enumerate(fields):
            put(state, kind, 0, tiles(inner, kind, 1, 1))
            put(state, kind, 1, mixed(tiles(inner, kind, 2, 1), v[:8]))
            put(state, kind, 2, v[8:])


def at_edge(core):
    r, rows = lax.axis_index("rows"), lax.axis_size("rows")
    return ((core == 0) & (r == 0)) | ((core == 1) & (r == rows - 1))


def outer_kernel(half, own, other, drive, got, middle, sent, state):
    core = lax.axis_index("tm") % 2
    first = core == 0
    height = 2 * half
    row = pl.multiple_of((height - WIDE) * core, 8)
    a, b = picked(first, own[pl.ds(row, 8), :], other[pl.ds(row, 8), :])
    near = (a, b, drive[pl.ds(row, 8), :])
    far = [got[8 * i : 8 * i + 8, :] for i in range(3)]
    upper = [jnp.where(first, f, n) for f, n in zip(far, near)]
    lower = [jnp.where(first, n, f) for f, n in zip(far, near)]
    a, b, d = (jnp.concatenate(p) for p in zip(upper, lower))
    tile = lax.broadcasted_iota(jnp.int32, a.shape, 0) // 8
    inside = ~(at_edge(core) & (tile == core))
    a, b = jnp.where(inside, a, 0.0), jnp.where(inside, b, 0.0)
    d_a, d_b, e_b = first_pass(a, b, d, inside)
    sent[...] = pltpu.roll(e_b, 16 - CUT, 0)[:8]
    fields = (d_a, d_b, d, a)

    @pl.when(first)
    def _():
        for kind, v in enumerate(fields):
            put(state, kind, 0, v[:8])
            put(state, kind, 1, mixed(v[8:], tiles(middle, kind, 0, 1)))
            put(state, kind, 2, tiles(middle, kind, 1, 1))

    @pl.when(core == 1)
    def _():
        for kind, v in enumerate(fields):
            put(state, kind, 0, tiles(middle, kind, 2, 1))
            put(state, kind, 1, mixed(tiles(middle, kind, 3, 1), v[:8]))
            put(state, kind, 2, v[8:])


def finish(current, state, low, high, keep, send, inside=None):
    first = lax.axis_index("tm") % 2 == 0
    count = state.shape[0] // 32
    chip = lax.axis_index("tm") // 2
    d_a, d_b, d, a = (tiles(state, kind, 0, count) for kind in range(4))
    current = jnp.where(chip == 0, a, current)
    e_a, e_b = chain(current, d_a, d_b, d, inside)
    kept, sent = picked(first, e_a[low:high], e_b[low:high])
    keep[...] = kept
    send[...] = sent


def inner_end(arrived, state, keep, send):
    v = arrived[...]
    current = pltpu.roll(jnp.concatenate([v, v[:8]]), CUT, 0)
    finish(current, state, 8, 16, keep, send)


def middle_end(inner, middle, state, keep, send, current):
    core = lax.axis_index("tm") % 2

    @pl.when(core == 0)
    def _():
        current[...] = pltpu.roll(jnp.concatenate([middle[...], inner[...]]), CUT, 0)

    @pl.when(core == 1)
    def _():
        current[...] = pltpu.roll(jnp.concatenate([inner[...], middle[...]]), 32 - CUT, 0)

    finish(current[...], state, 8, 24, keep, send)


def outer_end(middle, outer, state, keep, send, current):
    core = lax.axis_index("tm") % 2

    @pl.when(core == 0)
    def _():
        current[...] = pltpu.roll(jnp.concatenate([outer[...], middle[...]]), CUT, 0)

    @pl.when(core == 1)
    def _():
        current[...] = pltpu.roll(jnp.concatenate([middle[...], outer[...]]), 24 - CUT, 0)

    tile = lax.broadcasted_iota(jnp.int32, current.shape, 0) // 8
    inside = ~(at_edge(core) & (tile == 2 * core))
    finish(current[...], state, 8, 16, keep, send, inside)


def joined_kernel(half, *refs):
    pieces, out, sems = refs[:6], refs[6], refs[7]
    core = lax.axis_index("tm") % 2
    copies = []
    for i, piece in enumerate(pieces):
        upper = (half - 8, 8, 0)[i % 3]
        lower = (half, half + 8, 2 * half - 8)[i % 3]
        where_upper = core == 0 if i < 3 else core == 1
        row = pl.multiple_of(jnp.where(where_upper, upper, lower), 8)
        copy = pltpu.make_async_copy(
            piece, out.at[0, pl.ds(row, piece.shape[0]), :], sems.at[i]
        )
        copy.start()
        copies.append(copy)
    for copy in copies:
        copy.wait()


def after(value, earlier):
    return lax.optimization_barrier((value, earlier))[0]


def masked_update(update, v, drive, inside):
    wide = (
        jnp.roll(v, 1, axis=0) + jnp.roll(v, -1, axis=0)
    ) + (jnp.roll(v, 1, axis=1) + jnp.roll(v, -1, axis=1))
    return jnp.where(inside, update(v, wide, drive), 0.0)


def long_chain(own, drive):
    height = own.shape[0]
    half = height // 2
    groups, slices, rows = (lax.axis_size(a) for a in AXES)
    t, r = lax.axis_index("tm"), lax.axis_index("rows")
    core, chip = t % 2, t // 2
    first = core == 0
    away = outward(groups, rows)

    def cut(field, start, size):
        return lax.dynamic_slice_in_dim(field, start, size, axis=0)

    other = routed(own, partner)
    s_a, s_b = picked(first, own, other)
    edge = core * (height - WIDE)
    got = routed(jnp.concatenate([cut(f, edge, WIDE) for f in (s_a, s_b, drive)]), away)

    def sided(body, outer, inner):
        return jnp.where(
            first,
            jnp.concatenate([outer, body, inner]),
            jnp.concatenate([inner, body, outer]),
        )

    def window(field, place):
        body = cut(field, core * half, half)
        inner = cut(field, jnp.where(first, half, half - WIDE), WIDE)
        return sided(body, got[place * WIDE : (place + 1) * WIDE], inner)

    w_a, w_b, w_d = (window(f, i) for i, f in enumerate((s_a, s_b, drive)))
    row = lax.broadcasted_iota(jnp.int32, (half + 2 * WIDE, 1), 0)
    row = row + r * height + core * half - WIDE
    inside = (row >= 0) & (row < rows * height)
    w_a, w_b = jnp.where(inside, w_a, 0.0), jnp.where(inside, w_b, 0.0)

    def delta(v):
        fine = v
        for _ in range(FINE):
            fine = masked_update(fine_of, fine, w_d, inside)
        return fine - masked_update(coarse_of, v, w_d, inside)

    d_a, d_b = delta(w_a), delta(w_b)

    def both(v):
        e_a = masked_update(coarse_of, v, w_d, inside) + d_a
        return e_a, masked_update(coarse_of, e_a, w_d, inside) + d_b

    def extended(v):
        last = WIDE + half - 2
        inner = routed(cut(v, jnp.where(first, last, WIDE), 2), partner)
        outer = routed(cut(v, jnp.where(first, WIDE, last), 2), away)
        return sided(v[WIDE : WIDE + half], outer, inner)

    e_a, e_b = both(w_a)
    for stage in range(slices // 2 - 1):
        moved = e_b[WIDE - 2 : WIDE + half + 2] if stage == 0 else extended(e_b)
        arrived = routed(moved, stage_swap(stage))
        current = jnp.pad(arrived, ((WIDE - 2, WIDE - 2), (0, 0)))
        n_a, n_b = both(jnp.where(inside, current, 0.0))
        here = chip == stage + 1
        e_a, e_b = jnp.where(here, n_a, e_a), jnp.where(here, n_b, e_b)

    kept, sent = picked(first, e_a[WIDE : WIDE + half], e_b[WIDE : WIDE + half])
    back = routed(sent, partner)
    return jnp.concatenate(picked(first, kept, back))[None]


def on_device(starts, drive):
    own = starts[0]
    if lax.axis_size("tm") != 4:
        return long_chain(own, drive)
    height, width = own.shape
    half = height // 2
    groups, rows = lax.axis_size("groups"), lax.axis_size("rows")

    other = routed(own, partner)
    sent_1, state_1, edge = compute(
        functools.partial(inner_kernel, half),
        [(16, width), (4 * 24, width), (24, width)],
        (own, other, drive),
        name="inner",
    )
    here_1 = routed(sent_1, stage_swap(0))
    got = routed(edge, outward(groups, rows))
    sent_2, state_2 = compute(
        functools.partial(middle_kernel, half),
        [(16, width), (4 * 32, width)],
        (own, other, drive, state_1),
        name="middle",
    )
    here_2 = routed(sent_2, stage_swap(0))
    sent_3, state_3 = compute(
        functools.partial(outer_kernel, half),
        [(8, width), (4 * 24, width)],
        (own, other, drive, got, state_2),
        name="outer",
    )
    here_3 = routed(sent_3, stage_swap(0))

    keep_1, send_1 = compute(
        inner_end, [(8, width)] * 2, (here_1, after(state_1, sent_3)), name="inner_end"
    )
    back_1 = routed(send_1, partner)
    keep_2, send_2 = compute(
        middle_end,
        [(16, width)] * 2,
        (here_1, here_2, state_2),
        scratch_shapes=[pltpu.VMEM((32, width), jnp.float32)],
        name="middle_end",
    )
    back_2 = routed(send_2, partner)
    keep_3, send_3 = compute(
        outer_end,
        [(8, width)] * 2,
        (here_2, here_3, state_3),
        scratch_shapes=[pltpu.VMEM((24, width), jnp.float32)],
        name="outer_end",
    )
    back_3 = routed(send_3, partner)
    pieces = (keep_1, keep_2, keep_3, back_1, back_2, back_3)
    return pl.pallas_call(
        functools.partial(joined_kernel, half),
        out_shape=jax.ShapeDtypeStruct((1, height, width), jnp.float32),
        in_specs=[pl.BlockSpec(memory_space=pltpu.VMEM)] * 6,
        out_specs=pl.BlockSpec(memory_space=pl.ANY),
        scratch_shapes=[pltpu.SemaphoreType.DMA((6,))],
        compiler_params=pltpu.CompilerParams(vmem_limit_bytes=12 << 20),
        name="joined",
    )(*pieces)


def solution(mesh):
    in_specs = (P(("groups", "tm"), "rows", None), P("rows", None))
    out_specs = P(("groups", "tm"), "rows", None)
    return jax.shard_map(
        on_device, mesh=mesh, in_specs=in_specs, out_specs=out_specs, check_vma=False
    )
```

```python
import functools

import jax
import jax.numpy as jnp
from jax import lax
from jax.experimental import pallas as pl
from jax.experimental.pallas import tpu as pltpu
from jax.sharding import PartitionSpec as P


FINE = 3
WIDE = 8
CUT = 4


diffusion = 2.0
step_fine = 0.1
coarse_step = FINE * step_fine
damping = 1.0 + 4.0 * diffusion * coarse_step

AXES = ("groups", "tm", "rows")


def routed(block, route):
    groups, slices, rows = (lax.axis_size(a) for a in AXES)
    pairs = []
    for g in range(groups):
        for t in range(slices):
            for r in range(rows):
                to_g, to_t, to_r = route(g, t, r)
                source = (g * slices + t) * rows + r
                pairs.append((source, (to_g * slices + to_t) * rows + to_r))
    return lax.ppermute(block, AXES, pairs)


def partner(g, t, r):
    return g, t ^ 1, r


def outward(groups, rows):
    def route(g, t, r):
        to_r = r + 1 if t & 1 else r - 1
        if 0 <= to_r < rows:
            return g, t ^ 1, to_r
        other = g ^ 1
        return (other, t, r) if other < groups else (g, t, r)

    return route


def stage_swap(stage):
    def route(g, t, r):
        chip = t // 2
        if chip == stage:
            return g, t + 2, r
        if chip == stage + 1:
            return g, t - 2, r
        return g, t, r

    return route


def around(v):
    height, width = v.shape
    return (pltpu.roll(v, 1, 0) + pltpu.roll(v, height - 1, 0)) + (
        pltpu.roll(v, 1, 1) + pltpu.roll(v, width - 1, 1)
    )


def fine_of(v, nsum, drive):
    return (
        step_fine * diffusion * nsum
        + v * ((1.0 + step_fine - 4.0 * step_fine * diffusion) - step_fine * (v * v))
        + step_fine * drive
    )


def coarse_of(v, nsum, drive):
    scale = coarse_step / damping
    return (
        scale * diffusion * nsum
        + v * ((1.0 + coarse_step) / damping - scale * (v * v))
        + scale * drive
    )


def compute(kernel, outs, args, **kwargs):
    shapes = [jax.ShapeDtypeStruct(o, jnp.float32) for o in outs]
    vmem = pl.BlockSpec(memory_space=pltpu.VMEM)
    return pl.pallas_call(
        kernel,
        out_shape=shapes,
        in_specs=[vmem] * len(args),
        out_specs=[vmem] * len(outs),
        compiler_params=pltpu.CompilerParams(vmem_limit_bytes=16 << 20),
        **kwargs,
    )(*args)


def same(v):
    return v


def start_of(v, drive, kept=same):
    nsum = around(v)
    coarse = kept(coarse_of(v, nsum, drive))
    fine = kept(fine_of(v, nsum, drive))
    for _ in range(FINE - 1):
        fine = kept(fine_of(fine, around(fine), drive))
    return fine, coarse


def ends_of(first, mine, theirs, drive, kept=same):
    f_a, f_b = picked(first, mine[0], theirs[0])
    g_a, g_b = picked(first, mine[1], theirs[1])
    e_a = g_a + (f_a - g_a)
    e_b = kept(coarse_of(e_a, around(e_a), drive)) + (f_b - g_b)
    return e_a, e_b


def chain(current, d_a, d_b, drive, kept=same):
    e_a = kept(coarse_of(current, around(current), drive)) + d_a
    e_b = kept(coarse_of(e_a, around(e_a), drive)) + d_b
    return e_a, e_b


def picked(first, own, other):
    return jnp.where(first, own, other), jnp.where(first, other, own)


def field(ref, kind, kinds, start, size):
    height = ref.shape[0] // kinds
    return ref.at[pl.ds(pl.multiple_of(kind * height + start, 8), size), :]


def mixed(upper, lower):
    row = lax.broadcasted_iota(jnp.int32, upper.shape, 0)
    return jnp.where(row < CUT, upper, lower)


def place():
    t = lax.axis_index("tm")
    return t % 2, t // 2


def at_edge(core):
    r, rows = lax.axis_index("rows"), lax.axis_size("rows")
    return ((core == 0) & (r == 0)) | ((core == 1) & (r == rows - 1))


def inner_row(half, core):
    return pl.multiple_of(half - 16 + 8 * core, 8)


def middle_row(half, core):
    return pl.multiple_of((half + 8) * core, 8)


def outer_row(half, core):
    return pl.multiple_of((2 * half - WIDE) * core, 8)


def load_kernel(half, starts, drive, own, held, inner, middle, sems):
    core, chip = place()
    copies = []
    for i, (row, size) in enumerate(((half - 16, 32), (0, half - 16), (half + 16, half - 16))):
        rows = pl.ds(row, size)
        pair = (
            pltpu.make_async_copy(starts.at[0, rows, :], own.at[rows, :], sems.at[2 * i]),
            pltpu.make_async_copy(drive.at[rows, :], held.at[rows, :], sems.at[2 * i + 1]),
        )
        for copy in pair:
            copy.start()
        copies.append(pair)

    def window(row, into):
        @pl.when(chip == 0)
        def _():
            fine, coarse = start_of(own[pl.ds(row, 24), :], held[pl.ds(row, 24), :])
            into[0:24, :] = fine
            into[24:48, :] = coarse

    for copy in copies[0]:
        copy.wait()
    window(inner_row(half, core), inner)
    for copy in (*copies[1], *copies[2]):
        copy.wait()
    window(middle_row(half, core), middle)


def inner_kernel(half, own, other, drive, mine, sent, ends, edge):
    core, chip = place()
    first = core == 0

    @pl.when(chip == 0)
    def _():
        rows = pl.ds(inner_row(half, core), 24)
        d = drive[rows, :]
        theirs = start_of(other[rows, :], d)
        e_a, e_b = ends_of(first, (mine[0:24, :], mine[24:48, :]), theirs, d)
        sent[...] = pltpu.roll(e_b, 24 - CUT, 0)[:16]
        ends[0:24, :] = e_a
        ends[24:48, :] = e_b

    rows = pl.ds(outer_row(half, core), 8)
    a, b = picked(first, own[rows, :], other[rows, :])
    edge[0:8, :] = a
    edge[8:16, :] = b
    edge[16:24, :] = drive[rows, :]


def middle_kernel(half, own, other, drive, mine, sent, ends, state):
    core, chip = place()
    first = core == 0

    @pl.when(chip == 0)
    def _():
        rows = pl.ds(middle_row(half, core), 24)
        d = drive[rows, :]
        theirs = start_of(other[rows, :], d)
        e_a, e_b = ends_of(first, (mine[0:24, :], mine[24:48, :]), theirs, d)
        sent[...] = pltpu.roll(e_b, 24 - CUT, 0)[:16]
        ends[0:24, :] = e_a
        ends[24:48, :] = e_b

    @pl.when(chip > 0)
    def _():
        size = half + WIDE
        rows = pl.ds(pl.multiple_of((half - WIDE) * core, 8), size)
        d = drive[rows, :]
        state[2 * size : 3 * size, :] = d
        for mine_first, ref in ((True, own), (False, other)):
            fine, coarse = start_of(ref[rows, :], d)
            kind = jnp.where(first == mine_first, 0, 1)
            field(state, kind, 3, 0, size)[...] = fine - coarse


def outer_kernel(half, own, other, drive, got, inner_state, sent, ends, state):
    core, chip = place()
    first = core == 0
    rows = pl.ds(outer_row(half, core), 8)
    a, b = picked(first, own[rows, :], other[rows, :])
    near = (a, b, drive[rows, :])
    far = [got[8 * i : 8 * i + 8, :] for i in range(3)]
    upper = [jnp.where(first, f, n) for f, n in zip(far, near)]
    lower = [jnp.where(first, n, f) for f, n in zip(far, near)]
    a, b, d = (jnp.concatenate(p) for p in zip(upper, lower))
    tile = lax.broadcasted_iota(jnp.int32, a.shape, 0) // 8
    inside = ~(at_edge(core) & (tile == core))

    def kept(v):
        return jnp.where(inside, v, 0.0)

    f_a, g_a = start_of(kept(a), d, kept)
    f_b, g_b = start_of(kept(b), d, kept)

    @pl.when(chip == 0)
    def _():
        e_a = g_a + (f_a - g_a)
        e_b = kept(coarse_of(e_a, around(e_a), d)) + (f_b - g_b)
        sent[...] = pltpu.roll(e_b, 16 - CUT, 0)[:8]
        ends[0:16, :] = e_a
        ends[16:32, :] = e_b

    size = half + WIDE
    fields = (f_a - g_a, f_b - g_b, d)

    @pl.when((chip > 0) & first)
    def _():
        for kind, v in enumerate(fields):
            before = field(inner_state, kind, 3, 0, 16)[...]
            field(state, kind, 3, 0, 8)[...] = v[:8]
            field(state, kind, 3, 8, 8)[...] = mixed(v[8:], before[:8])
            field(state, kind, 3, 16, 8)[...] = before[8:]

    @pl.when((chip > 0) & (core == 1))
    def _():
        for kind, v in enumerate(fields):
            before = field(inner_state, kind, 3, size - 16, 16)[...]
            field(state, kind, 3, 0, 8)[...] = before[:8]
            field(state, kind, 3, 8, 8)[...] = mixed(before[8:], v[:8])
            field(state, kind, 3, 16, 8)[...] = v[8:]


def put_ends(first, e_a, e_b, keep, send):
    kept, sent = picked(first, e_a, e_b)
    keep[...] = kept
    send[...] = sent


def inner_end(half, arrived, state, ends, keep, send):
    core, chip = place()
    first = core == 0

    @pl.when(chip == 0)
    def _():
        put_ends(first, ends[8:16, :], ends[32:40, :], keep, send)

    @pl.when(chip > 0)
    def _():
        v = arrived[...]
        current = pltpu.roll(jnp.concatenate([v, v[:8]]), CUT, 0)
        row = (half - 16) * (1 - core)
        d_a, d_b, d = (field(state, kind, 3, row, 24)[...] for kind in range(3))
        e_a, e_b = chain(current, d_a, d_b, d)
        put_ends(first, e_a[8:16], e_b[8:16], keep, send)


def middle_end(inner, middle, state, inner_ends, ends, keep, send, current):
    core, chip = place()
    first = core == 0

    def known(kind):
        near = field(inner_ends, kind, 2, 16 * core, 8)[...]
        rows = [field(ends, kind, 2, 8 * i, 8)[...] for i in range(3)]
        upper = jnp.where(first, rows[1], mixed(near, rows[0]))
        lower = jnp.where(first, mixed(rows[2], near), rows[1])
        return jnp.concatenate([upper, lower])

    @pl.when(chip == 0)
    def _():
        put_ends(first, known(0), known(1), keep, send)

    @pl.when((chip > 0) & first)
    def _():
        current[...] = pltpu.roll(jnp.concatenate([middle[...], inner[...]]), CUT, 0)

    @pl.when((chip > 0) & (core == 1))
    def _():
        current[...] = pltpu.roll(jnp.concatenate([inner[...], middle[...]]), 32 - CUT, 0)

    @pl.when(chip > 0)
    def _():
        d_a, d_b, d = (field(state, kind, 3, 8 * core, 32)[...] for kind in range(3))
        e_a, e_b = chain(current[...], d_a, d_b, d)
        put_ends(first, e_a[8:24], e_b[8:24], keep, send)


def outer_end(middle, outer, state, middle_ends, ends, keep, send, current):
    core, chip = place()
    first = core == 0

    def known(kind):
        near = field(middle_ends, kind, 2, 16 * core, 8)[...]
        far = field(ends, kind, 2, 8 * (1 - core), 8)[...]
        return jnp.where(first, mixed(far, near), mixed(near, far))

    @pl.when(chip == 0)
    def _():
        put_ends(first, known(0), known(1), keep, send)

    @pl.when((chip > 0) & first)
    def _():
        current[...] = pltpu.roll(jnp.concatenate([outer[...], middle[...]]), CUT, 0)

    @pl.when((chip > 0) & (core == 1))
    def _():
        current[...] = pltpu.roll(jnp.concatenate([middle[...], outer[...]]), 24 - CUT, 0)

    @pl.when(chip > 0)
    def _():
        d_a, d_b, d = (field(state, kind, 3, 0, 24)[...] for kind in range(3))
        tile = lax.broadcasted_iota(jnp.int32, d.shape, 0) // 8
        inside = ~(at_edge(core) & (tile == 2 * core))
        e_a = coarse_of(current[...], around(current[...]), d) + d_a
        e_a = jnp.where(inside, e_a, 0.0)
        e_b = coarse_of(e_a, around(e_a), d) + d_b
        put_ends(first, e_a[8:16], e_b[8:16], keep, send)


def write_kernel(half, order, *refs):
    count = len(order)
    pieces, out, sems = refs[:count], refs[-2], refs[-1]
    core, _ = place()
    copies = []
    for i, (mine, part) in enumerate(order):
        upper = (half - 8, 8, 0)[part]
        lower = (half, half + 8, 2 * half - 8)[part]
        row = pl.multiple_of(jnp.where((core == 0) == mine, upper, lower), 8)
        piece = pieces[i]
        copy = pltpu.make_async_copy(
            piece, out.at[0, pl.ds(row, piece.shape[0]), :], sems.at[i]
        )
        copy.start()
        copies.append(copy)
    for copy in copies:
        copy.wait()


def written(half, order, pieces, shape, into=None):
    vmem, anywhere = pl.BlockSpec(memory_space=pltpu.VMEM), pl.BlockSpec(memory_space=pl.ANY)
    count = len(pieces)
    extra = () if into is None else (into,)
    return pl.pallas_call(
        functools.partial(write_kernel, half, order),
        out_shape=jax.ShapeDtypeStruct(shape, jnp.float32),
        in_specs=[vmem] * count + [anywhere] * len(extra),
        out_specs=anywhere,
        input_output_aliases={count: 0} if extra else {},
        scratch_shapes=[pltpu.SemaphoreType.DMA((count,))],
        compiler_params=pltpu.CompilerParams(vmem_limit_bytes=16 << 20),
    )(*pieces, *extra)


def after(value, earlier):
    return lax.optimization_barrier((value, earlier))[0]


def masked_update(update, v, drive, inside):
    wide = (
        jnp.roll(v, 1, axis=0) + jnp.roll(v, -1, axis=0)
    ) + (jnp.roll(v, 1, axis=1) + jnp.roll(v, -1, axis=1))
    return jnp.where(inside, update(v, wide, drive), 0.0)


def long_chain(own, drive):
    height = own.shape[0]
    half = height // 2
    groups, slices, rows = (lax.axis_size(a) for a in AXES)
    t, r = lax.axis_index("tm"), lax.axis_index("rows")
    core, chip = t % 2, t // 2
    first = core == 0
    away = outward(groups, rows)

    def cut(field, start, size):
        return lax.dynamic_slice_in_dim(field, start, size, axis=0)

    other = routed(own, partner)
    s_a, s_b = picked(first, own, other)
    edge = core * (height - WIDE)
    got = routed(jnp.concatenate([cut(f, edge, WIDE) for f in (s_a, s_b, drive)]), away)

    def sided(body, outer, inner):
        return jnp.where(
            first,
            jnp.concatenate([outer, body, inner]),
            jnp.concatenate([inner, body, outer]),
        )

    def window(field, place):
        body = cut(field, core * half, half)
        inner = cut(field, jnp.where(first, half, half - WIDE), WIDE)
        return sided(body, got[place * WIDE : (place + 1) * WIDE], inner)

    w_a, w_b, w_d = (window(f, i) for i, f in enumerate((s_a, s_b, drive)))
    row = lax.broadcasted_iota(jnp.int32, (half + 2 * WIDE, 1), 0)
    row = row + r * height + core * half - WIDE
    inside = (row >= 0) & (row < rows * height)
    w_a, w_b = jnp.where(inside, w_a, 0.0), jnp.where(inside, w_b, 0.0)

    def delta(v):
        fine = v
        for _ in range(FINE):
            fine = masked_update(fine_of, fine, w_d, inside)
        return fine - masked_update(coarse_of, v, w_d, inside)

    d_a, d_b = delta(w_a), delta(w_b)

    def both(v):
        e_a = masked_update(coarse_of, v, w_d, inside) + d_a
        return e_a, masked_update(coarse_of, e_a, w_d, inside) + d_b

    def extended(v):
        last = WIDE + half - 2
        inner = routed(cut(v, jnp.where(first, last, WIDE), 2), partner)
        outer = routed(cut(v, jnp.where(first, WIDE, last), 2), away)
        return sided(v[WIDE : WIDE + half], outer, inner)

    e_a, e_b = both(w_a)
    for stage in range(slices // 2 - 1):
        moved = e_b[WIDE - 2 : WIDE + half + 2] if stage == 0 else extended(e_b)
        arrived = routed(moved, stage_swap(stage))
        current = jnp.pad(arrived, ((WIDE - 2, WIDE - 2), (0, 0)))
        n_a, n_b = both(jnp.where(inside, current, 0.0))
        here = chip == stage + 1
        e_a, e_b = jnp.where(here, n_a, e_a), jnp.where(here, n_b, e_b)

    kept, sent = picked(first, e_a[WIDE : WIDE + half], e_b[WIDE : WIDE + half])
    back = routed(sent, partner)
    return jnp.concatenate(picked(first, kept, back))[None]


def on_device(starts, drive):
    own = starts[0]
    if lax.axis_size("tm") != 4:
        return long_chain(own, drive)
    return two_chips(starts, drive)


def two_chips(starts, drive):
    _, height, width = starts.shape
    half = height // 2
    groups, rows = lax.axis_size("groups"), lax.axis_size("rows")
    vmem, anywhere = pl.BlockSpec(memory_space=pltpu.VMEM), pl.BlockSpec(memory_space=pl.ANY)

    other = routed(starts[0], partner)
    own, held, mine_1, mine_2 = pl.pallas_call(
        functools.partial(load_kernel, half),
        out_shape=[
            jax.ShapeDtypeStruct((size, width), jnp.float32)
            for size in (height, height, 48, 48)
        ],
        in_specs=[anywhere] * 2,
        out_specs=[vmem] * 4,
        scratch_shapes=[pltpu.SemaphoreType.DMA((6,))],
        compiler_params=pltpu.CompilerParams(vmem_limit_bytes=16 << 20),
        cost_estimate=pl.CostEstimate(
            flops=60 * 48 * width, bytes_accessed=16 * height * width, transcendentals=0
        ),
        name="load",
    )(starts, drive)
    sent_1, ends_1, edge = compute(
        functools.partial(inner_kernel, half),
        [(16, width), (48, width), (24, width)],
        (own, other, held, mine_1),
        name="inner",
    )
    here_1 = routed(sent_1, stage_swap(0))
    got = routed(edge, outward(groups, rows))
    sent_2, ends_2, state = compute(
        functools.partial(middle_kernel, half),
        [(16, width), (48, width), (3 * (half + WIDE), width)],
        (own, other, held, mine_2),
        name="middle",
    )
    here_2 = routed(sent_2, stage_swap(0))
    sent_3, ends_3, state_3 = compute(
        functools.partial(outer_kernel, half),
        [(8, width), (32, width), (3 * 24, width)],
        (own, other, held, got, state),
        name="outer",
    )
    here_3 = routed(sent_3, stage_swap(0))

    keep_1, send_1 = compute(
        functools.partial(inner_end, half),
        [(8, width)] * 2,
        (here_1, state, after(ends_1, sent_3)),
        name="inner_end",
    )
    back_1 = routed(send_1, partner)
    keep_2, send_2 = compute(
        middle_end,
        [(16, width)] * 2,
        (here_1, here_2, state, ends_1, after(ends_2, keep_1)),
        scratch_shapes=[pltpu.VMEM((32, width), jnp.float32)],
        name="middle_end",
    )
    back_2 = routed(send_2, partner)
    out = written(half, ((True, 0), (True, 1), (False, 0)), (keep_1, keep_2, back_1), starts.shape)
    out, ends_3 = lax.optimization_barrier((out, ends_3))
    keep_3, send_3 = compute(
        outer_end,
        [(8, width)] * 2,
        (here_2, here_3, state_3, ends_2, ends_3),
        scratch_shapes=[pltpu.VMEM((24, width), jnp.float32)],
        name="outer_end",
    )
    back_3 = routed(send_3, partner)
    return written(
        half, ((False, 1), (True, 2), (False, 2)), (back_2, keep_3, back_3), starts.shape, into=out
    )


def solution(mesh):
    in_specs = (P(("groups", "tm"), "rows", None), P("rows", None))
    out_specs = P(("groups", "tm"), "rows", None)
    return jax.shard_map(
        on_device, mesh=mesh, in_specs=in_specs, out_specs=out_specs, check_vma=False
    )
```

```python
import functools

import jax
import jax.numpy as jnp
from jax import lax
from jax.experimental import pallas as pl
from jax.experimental.pallas import tpu as pltpu
from jax.sharding import PartitionSpec as P


FINE = 3
WIDE = 8
CUT = 4


diffusion = 2.0
step_fine = 0.1
coarse_step = FINE * step_fine
damping = 1.0 + 4.0 * diffusion * coarse_step

AXES = ("groups", "tm", "rows")


def routed(block, route):
    groups, slices, rows = (lax.axis_size(a) for a in AXES)
    pairs = []
    for g in range(groups):
        for t in range(slices):
            for r in range(rows):
                to_g, to_t, to_r = route(g, t, r)
                source = (g * slices + t) * rows + r
                pairs.append((source, (to_g * slices + to_t) * rows + to_r))
    return lax.ppermute(block, AXES, pairs)


def partner(g, t, r):
    return g, t ^ 1, r


def outward(groups, rows):
    def route(g, t, r):
        to_r = r + 1 if t & 1 else r - 1
        if 0 <= to_r < rows:
            return g, t ^ 1, to_r
        other = g ^ 1
        return (other, t, r) if other < groups else (g, t, r)

    return route


def stage_swap(stage):
    def route(g, t, r):
        chip = t // 2
        if chip == stage:
            return g, t + 2, r
        if chip == stage + 1:
            return g, t - 2, r
        return g, t, r

    return route


def around(v):
    height, width = v.shape
    return (pltpu.roll(v, 1, 0) + pltpu.roll(v, height - 1, 0)) + (
        pltpu.roll(v, 1, 1) + pltpu.roll(v, width - 1, 1)
    )


def fine_of(v, nsum, drive):
    return (
        step_fine * diffusion * nsum
        + v * ((1.0 + step_fine - 4.0 * step_fine * diffusion) - step_fine * (v * v))
        + step_fine * drive
    )


def coarse_of(v, nsum, drive):
    scale = coarse_step / damping
    return (
        scale * diffusion * nsum
        + v * ((1.0 + coarse_step) / damping - scale * (v * v))
        + scale * drive
    )


def compute(kernel, outs, args, **kwargs):
    shapes = [jax.ShapeDtypeStruct(o, jnp.float32) for o in outs]
    vmem = pl.BlockSpec(memory_space=pltpu.VMEM)
    return pl.pallas_call(
        kernel,
        out_shape=shapes,
        in_specs=[vmem] * len(args),
        out_specs=[vmem] * len(outs),
        compiler_params=pltpu.CompilerParams(vmem_limit_bytes=16 << 20),
        **kwargs,
    )(*args)


def same(v):
    return v


def start_of(v, drive, kept=same):
    nsum = around(v)
    coarse = kept(coarse_of(v, nsum, drive))
    fine = kept(fine_of(v, nsum, drive))
    for _ in range(FINE - 1):
        fine = kept(fine_of(fine, around(fine), drive))
    return fine, coarse


def ends_of(first, mine, theirs, drive, kept=same):
    f_a, f_b = picked(first, mine[0], theirs[0])
    g_a, g_b = picked(first, mine[1], theirs[1])
    e_a = g_a + (f_a - g_a)
    e_b = kept(coarse_of(e_a, around(e_a), drive)) + (f_b - g_b)
    return e_a, e_b


def chain(current, d_a, d_b, drive, kept=same):
    e_a = kept(coarse_of(current, around(current), drive)) + d_a
    e_b = kept(coarse_of(e_a, around(e_a), drive)) + d_b
    return e_a, e_b


def picked(first, own, other):
    return jnp.where(first, own, other), jnp.where(first, other, own)


def field(ref, kind, kinds, start, size):
    height = ref.shape[0] // kinds
    return ref.at[pl.ds(pl.multiple_of(kind * height + start, 8), size), :]


def mixed(upper, lower):
    row = lax.broadcasted_iota(jnp.int32, upper.shape, 0)
    return jnp.where(row < CUT, upper, lower)


def place():
    t = lax.axis_index("tm")
    return t % 2, t // 2


def at_edge(core):
    r, rows = lax.axis_index("rows"), lax.axis_size("rows")
    return ((core == 0) & (r == 0)) | ((core == 1) & (r == rows - 1))


def inner_row(half, core):
    return pl.multiple_of(half - 16 + 8 * core, 8)


def middle_row(half, core):
    return pl.multiple_of((half + 8) * core, 8)


def outer_row(half, core):
    return pl.multiple_of((2 * half - WIDE) * core, 8)


def load_kernel(half, starts, drive, own, held, inner, middle, sems):
    core, chip = place()
    copies = []
    for i, (row, size) in enumerate(((half - 16, 32), (0, half - 16), (half + 16, half - 16))):
        rows = pl.ds(row, size)
        pair = (
            pltpu.make_async_copy(starts.at[0, rows, :], own.at[rows, :], sems.at[2 * i]),
            pltpu.make_async_copy(drive.at[rows, :], held.at[rows, :], sems.at[2 * i + 1]),
        )
        for copy in pair:
            copy.start()
        copies.append(pair)

    def window(row, into):
        @pl.when(chip == 0)
        def _():
            fine, coarse = start_of(own[pl.ds(row, 24), :], held[pl.ds(row, 24), :])
            into[0:24, :] = fine
            into[24:48, :] = coarse

    for copy in copies[0]:
        copy.wait()
    window(inner_row(half, core), inner)
    for copy in (*copies[1], *copies[2]):
        copy.wait()
    window(middle_row(half, core), middle)


def inner_kernel(half, own, other, drive, mine, sent, ends, edge):
    core, chip = place()
    first = core == 0

    @pl.when(chip == 0)
    def _():
        rows = pl.ds(inner_row(half, core), 24)
        d = drive[rows, :]
        theirs = start_of(other[rows, :], d)
        e_a, e_b = ends_of(first, (mine[0:24, :], mine[24:48, :]), theirs, d)
        sent[...] = pltpu.roll(e_b, 24 - CUT, 0)[:16]
        ends[0:24, :] = e_a
        ends[24:48, :] = e_b

    rows = pl.ds(outer_row(half, core), 8)
    a, b = picked(first, own[rows, :], other[rows, :])
    edge[0:8, :] = a
    edge[8:16, :] = b
    edge[16:24, :] = drive[rows, :]


def middle_kernel(half, own, other, drive, mine, sent, ends):
    core, chip = place()
    first = core == 0

    @pl.when(chip == 0)
    def _():
        rows = pl.ds(middle_row(half, core), 24)
        d = drive[rows, :]
        theirs = start_of(other[rows, :], d)
        e_a, e_b = ends_of(first, (mine[0:24, :], mine[24:48, :]), theirs, d)
        sent[...] = pltpu.roll(e_b, 24 - CUT, 0)[:16]
        ends[0:24, :] = e_a
        ends[24:48, :] = e_b


def state_kernel(half, own, other, drive, state):
    core, chip = place()
    first = core == 0

    @pl.when(chip > 0)
    def _():
        size = half + WIDE
        rows = pl.ds(pl.multiple_of((half - WIDE) * core, 8), size)
        d = drive[rows, :]
        state[2 * size : 3 * size, :] = d
        for mine_first, ref in ((True, own), (False, other)):
            fine, coarse = start_of(ref[rows, :], d)
            kind = jnp.where(first == mine_first, 0, 1)
            field(state, kind, 3, 0, size)[...] = fine - coarse


def outer_kernel(half, own, other, drive, got, inner_state, sent, ends, state):
    core, chip = place()
    first = core == 0
    rows = pl.ds(outer_row(half, core), 8)
    a, b = picked(first, own[rows, :], other[rows, :])
    near = (a, b, drive[rows, :])
    far = [got[8 * i : 8 * i + 8, :] for i in range(3)]
    upper = [jnp.where(first, f, n) for f, n in zip(far, near)]
    lower = [jnp.where(first, n, f) for f, n in zip(far, near)]
    a, b, d = (jnp.concatenate(p) for p in zip(upper, lower))
    tile = lax.broadcasted_iota(jnp.int32, a.shape, 0) // 8
    inside = ~(at_edge(core) & (tile == core))

    def kept(v):
        return jnp.where(inside, v, 0.0)

    f_a, g_a = start_of(kept(a), d, kept)
    f_b, g_b = start_of(kept(b), d, kept)

    @pl.when(chip == 0)
    def _():
        e_a = g_a + (f_a - g_a)
        e_b = kept(coarse_of(e_a, around(e_a), d)) + (f_b - g_b)
        sent[...] = pltpu.roll(e_b, 16 - CUT, 0)[:8]
        ends[0:16, :] = e_a
        ends[16:32, :] = e_b

    size = half + WIDE
    fields = (f_a - g_a, f_b - g_b, d)

    @pl.when((chip > 0) & first)
    def _():
        for kind, v in enumerate(fields):
            before = field(inner_state, kind, 3, 0, 16)[...]
            field(state, kind, 3, 0, 8)[...] = v[:8]
            field(state, kind, 3, 8, 8)[...] = mixed(v[8:], before[:8])
            field(state, kind, 3, 16, 8)[...] = before[8:]

    @pl.when((chip > 0) & (core == 1))
    def _():
        for kind, v in enumerate(fields):
            before = field(inner_state, kind, 3, size - 16, 16)[...]
            field(state, kind, 3, 0, 8)[...] = before[:8]
            field(state, kind, 3, 8, 8)[...] = mixed(before[8:], v[:8])
            field(state, kind, 3, 16, 8)[...] = v[8:]


def put_ends(first, e_a, e_b, keep, send):
    kept, sent = picked(first, e_a, e_b)
    keep[...] = kept
    send[...] = sent


def inner_end(half, arrived, state, ends, keep, send):
    core, chip = place()
    first = core == 0

    @pl.when(chip == 0)
    def _():
        put_ends(first, ends[8:16, :], ends[32:40, :], keep, send)

    @pl.when(chip > 0)
    def _():
        v = arrived[...]
        current = pltpu.roll(jnp.concatenate([v, v[:8]]), CUT, 0)
        row = (half - 16) * (1 - core)
        d_a, d_b, d = (field(state, kind, 3, row, 24)[...] for kind in range(3))
        e_a, e_b = chain(current, d_a, d_b, d)
        put_ends(first, e_a[8:16], e_b[8:16], keep, send)


def middle_end(inner, middle, state, inner_ends, ends, keep, send, current):
    core, chip = place()
    first = core == 0

    def known(kind):
        near = field(inner_ends, kind, 2, 16 * core, 8)[...]
        rows = [field(ends, kind, 2, 8 * i, 8)[...] for i in range(3)]
        upper = jnp.where(first, rows[1], mixed(near, rows[0]))
        lower = jnp.where(first, mixed(rows[2], near), rows[1])
        return jnp.concatenate([upper, lower])

    @pl.when(chip == 0)
    def _():
        put_ends(first, known(0), known(1), keep, send)

    @pl.when((chip > 0) & first)
    def _():
        current[...] = pltpu.roll(jnp.concatenate([middle[...], inner[...]]), CUT, 0)

    @pl.when((chip > 0) & (core == 1))
    def _():
        current[...] = pltpu.roll(jnp.concatenate([inner[...], middle[...]]), 32 - CUT, 0)

    @pl.when(chip > 0)
    def _():
        d_a, d_b, d = (field(state, kind, 3, 8 * core, 32)[...] for kind in range(3))
        e_a, e_b = chain(current[...], d_a, d_b, d)
        put_ends(first, e_a[8:24], e_b[8:24], keep, send)


def outer_end(middle, outer, state, middle_ends, ends, keep, send, current):
    core, chip = place()
    first = core == 0

    def known(kind):
        near = field(middle_ends, kind, 2, 16 * core, 8)[...]
        far = field(ends, kind, 2, 8 * (1 - core), 8)[...]
        return jnp.where(first, mixed(far, near), mixed(near, far))

    @pl.when(chip == 0)
    def _():
        put_ends(first, known(0), known(1), keep, send)

    @pl.when((chip > 0) & first)
    def _():
        current[...] = pltpu.roll(jnp.concatenate([outer[...], middle[...]]), CUT, 0)

    @pl.when((chip > 0) & (core == 1))
    def _():
        current[...] = pltpu.roll(jnp.concatenate([middle[...], outer[...]]), 24 - CUT, 0)

    @pl.when(chip > 0)
    def _():
        d_a, d_b, d = (field(state, kind, 3, 0, 24)[...] for kind in range(3))
        tile = lax.broadcasted_iota(jnp.int32, d.shape, 0) // 8
        inside = ~(at_edge(core) & (tile == 2 * core))
        e_a = coarse_of(current[...], around(current[...]), d) + d_a
        e_a = jnp.where(inside, e_a, 0.0)
        e_b = coarse_of(e_a, around(e_a), d) + d_b
        put_ends(first, e_a[8:16], e_b[8:16], keep, send)


def write_kernel(half, order, *refs):
    count = len(order)
    pieces, out, sems = refs[:count], refs[-2], refs[-1]
    core, _ = place()
    copies = []
    for i, (mine, part) in enumerate(order):
        upper = (half - 8, 8, 0)[part]
        lower = (half, half + 8, 2 * half - 8)[part]
        row = pl.multiple_of(jnp.where((core == 0) == mine, upper, lower), 8)
        piece = pieces[i]
        copy = pltpu.make_async_copy(
            piece, out.at[0, pl.ds(row, piece.shape[0]), :], sems.at[i]
        )
        copy.start()
        copies.append(copy)
    for copy in copies:
        copy.wait()


def written(half, order, pieces, shape, into=None):
    vmem, anywhere = pl.BlockSpec(memory_space=pltpu.VMEM), pl.BlockSpec(memory_space=pl.ANY)
    count = len(pieces)
    extra = () if into is None else (into,)
    return pl.pallas_call(
        functools.partial(write_kernel, half, order),
        out_shape=jax.ShapeDtypeStruct(shape, jnp.float32),
        in_specs=[vmem] * count + [anywhere] * len(extra),
        out_specs=anywhere,
        input_output_aliases={count: 0} if extra else {},
        scratch_shapes=[pltpu.SemaphoreType.DMA((count,))],
        compiler_params=pltpu.CompilerParams(vmem_limit_bytes=16 << 20),
    )(*pieces, *extra)


def after(value, earlier):
    return lax.optimization_barrier((value, earlier))[0]


def masked_update(update, v, drive, inside):
    wide = (
        jnp.roll(v, 1, axis=0) + jnp.roll(v, -1, axis=0)
    ) + (jnp.roll(v, 1, axis=1) + jnp.roll(v, -1, axis=1))
    return jnp.where(inside, update(v, wide, drive), 0.0)


def long_chain(own, drive):
    height = own.shape[0]
    half = height // 2
    groups, slices, rows = (lax.axis_size(a) for a in AXES)
    t, r = lax.axis_index("tm"), lax.axis_index("rows")
    core, chip = t % 2, t // 2
    first = core == 0
    away = outward(groups, rows)

    def cut(field, start, size):
        return lax.dynamic_slice_in_dim(field, start, size, axis=0)

    other = routed(own, partner)
    s_a, s_b = picked(first, own, other)
    edge = core * (height - WIDE)
    got = routed(jnp.concatenate([cut(f, edge, WIDE) for f in (s_a, s_b, drive)]), away)

    def sided(body, outer, inner):
        return jnp.where(
            first,
            jnp.concatenate([outer, body, inner]),
            jnp.concatenate([inner, body, outer]),
        )

    def window(field, place):
        body = cut(field, core * half, half)
        inner = cut(field, jnp.where(first, half, half - WIDE), WIDE)
        return sided(body, got[place * WIDE : (place + 1) * WIDE], inner)

    w_a, w_b, w_d = (window(f, i) for i, f in enumerate((s_a, s_b, drive)))
    row = lax.broadcasted_iota(jnp.int32, (half + 2 * WIDE, 1), 0)
    row = row + r * height + core * half - WIDE
    inside = (row >= 0) & (row < rows * height)
    w_a, w_b = jnp.where(inside, w_a, 0.0), jnp.where(inside, w_b, 0.0)

    def delta(v):
        fine = v
        for _ in range(FINE):
            fine = masked_update(fine_of, fine, w_d, inside)
        return fine - masked_update(coarse_of, v, w_d, inside)

    d_a, d_b = delta(w_a), delta(w_b)

    def both(v):
        e_a = masked_update(coarse_of, v, w_d, inside) + d_a
        return e_a, masked_update(coarse_of, e_a, w_d, inside) + d_b

    def extended(v):
        last = WIDE + half - 2
        inner = routed(cut(v, jnp.where(first, last, WIDE), 2), partner)
        outer = routed(cut(v, jnp.where(first, WIDE, last), 2), away)
        return sided(v[WIDE : WIDE + half], outer, inner)

    e_a, e_b = both(w_a)
    for stage in range(slices // 2 - 1):
        moved = e_b[WIDE - 2 : WIDE + half + 2] if stage == 0 else extended(e_b)
        arrived = routed(moved, stage_swap(stage))
        current = jnp.pad(arrived, ((WIDE - 2, WIDE - 2), (0, 0)))
        n_a, n_b = both(jnp.where(inside, current, 0.0))
        here = chip == stage + 1
        e_a, e_b = jnp.where(here, n_a, e_a), jnp.where(here, n_b, e_b)

    kept, sent = picked(first, e_a[WIDE : WIDE + half], e_b[WIDE : WIDE + half])
    back = routed(sent, partner)
    return jnp.concatenate(picked(first, kept, back))[None]


def on_device(starts, drive):
    own = starts[0]
    if lax.axis_size("tm") != 4:
        return long_chain(own, drive)
    return two_chips(starts, drive)


def two_chips(starts, drive):
    _, height, width = starts.shape
    half = height // 2
    groups, rows = lax.axis_size("groups"), lax.axis_size("rows")
    vmem = pl.BlockSpec(memory_space=pltpu.VMEM)

    other = routed(starts[0], partner)
    own, held, mine_1, mine_2 = pl.pallas_call(
        functools.partial(load_kernel, half),
        out_shape=[
            jax.ShapeDtypeStruct((size, width), jnp.float32)
            for size in (height, height, 48, 48)
        ],
        in_specs=[pl.BlockSpec(memory_space=pltpu.HBM)] * 2,
        out_specs=[vmem] * 4,
        scratch_shapes=[pltpu.SemaphoreType.DMA((6,))],
        compiler_params=pltpu.CompilerParams(vmem_limit_bytes=50 << 20),
        cost_estimate=pl.CostEstimate(
            flops=60 * 48 * width, bytes_accessed=16 * height * width, transcendentals=0
        ),
        name="load",
    )(starts, drive)
    sent_1, ends_1, edge = compute(
        functools.partial(inner_kernel, half),
        [(16, width), (48, width), (24, width)],
        (own, other, held, mine_1),
        name="inner",
    )
    here_1 = routed(sent_1, stage_swap(0))
    got = routed(edge, outward(groups, rows))
    sent_2, ends_2 = compute(
        functools.partial(middle_kernel, half),
        [(16, width), (48, width)],
        (own, other, held, mine_2),
        name="middle",
    )
    here_2 = routed(sent_2, stage_swap(0))
    (state,) = compute(
        functools.partial(state_kernel, half),
        [(3 * (half + WIDE), width)],
        (own, other, after(held, sent_2)),
        name="state",
    )
    sent_3, ends_3, state_3 = compute(
        functools.partial(outer_kernel, half),
        [(8, width), (32, width), (3 * 24, width)],
        (own, other, held, got, state),
        name="outer",
    )
    here_3 = routed(sent_3, stage_swap(0))

    keep_1, send_1 = compute(
        functools.partial(inner_end, half),
        [(8, width)] * 2,
        (here_1, state, after(ends_1, sent_3)),
        name="inner_end",
    )
    back_1 = routed(send_1, partner)
    keep_2, send_2 = compute(
        middle_end,
        [(16, width)] * 2,
        (here_1, here_2, state, ends_1, after(ends_2, keep_1)),
        scratch_shapes=[pltpu.VMEM((32, width), jnp.float32)],
        name="middle_end",
    )
    back_2 = routed(send_2, partner)
    out = written(half, ((True, 0), (True, 1), (False, 0)), (keep_1, keep_2, back_1), starts.shape)
    out, ends_3 = lax.optimization_barrier((out, ends_3))
    keep_3, send_3 = compute(
        outer_end,
        [(8, width)] * 2,
        (here_2, here_3, state_3, ends_2, ends_3),
        scratch_shapes=[pltpu.VMEM((24, width), jnp.float32)],
        name="outer_end",
    )
    back_3 = routed(send_3, partner)
    return written(
        half, ((False, 1), (True, 2), (False, 2)), (back_2, keep_3, back_3), starts.shape, into=out
    )


def solution(mesh):
    in_specs = (P(("groups", "tm"), "rows", None), P("rows", None))
    out_specs = P(("groups", "tm"), "rows", None)
    return jax.shard_map(
        on_device, mesh=mesh, in_specs=in_specs, out_specs=out_specs, check_vma=False
    )
```

```python
import functools

import jax
import jax.numpy as jnp
from jax import lax
from jax.experimental import pallas as pl
from jax.experimental.pallas import tpu as pltpu
from jax.sharding import PartitionSpec as P


FINE = 3
WIDE = 8
CUT = 4


diffusion = 2.0
step_fine = 0.1
coarse_step = FINE * step_fine
damping = 1.0 + 4.0 * diffusion * coarse_step

AXES = ("groups", "tm", "rows")


def routed(block, route):
    groups, slices, rows = (lax.axis_size(a) for a in AXES)
    pairs = []
    for g in range(groups):
        for t in range(slices):
            for r in range(rows):
                to_g, to_t, to_r = route(g, t, r)
                source = (g * slices + t) * rows + r
                pairs.append((source, (to_g * slices + to_t) * rows + to_r))
    return lax.ppermute(block, AXES, pairs)


def partner(g, t, r):
    return g, t ^ 1, r


def outward(groups, rows):
    def route(g, t, r):
        to_r = r + 1 if t & 1 else r - 1
        if 0 <= to_r < rows:
            return g, t ^ 1, to_r
        other = g ^ 1
        return (other, t, r) if other < groups else (g, t, r)

    return route


def stage_swap(stage):
    def route(g, t, r):
        chip = t // 2
        if chip == stage:
            return g, t + 2, r
        if chip == stage + 1:
            return g, t - 2, r
        return g, t, r

    return route


def around(v):
    height, width = v.shape
    return (pltpu.roll(v, 1, 0) + pltpu.roll(v, height - 1, 0)) + (
        pltpu.roll(v, 1, 1) + pltpu.roll(v, width - 1, 1)
    )


def fine_of(v, nsum, drive):
    return (
        step_fine * diffusion * nsum
        + v * ((1.0 + step_fine - 4.0 * step_fine * diffusion) - step_fine * (v * v))
        + step_fine * drive
    )


def coarse_of(v, nsum, drive):
    scale = coarse_step / damping
    return (
        scale * diffusion * nsum
        + v * ((1.0 + coarse_step) / damping - scale * (v * v))
        + scale * drive
    )


def compute(kernel, outs, args, **kwargs):
    shapes = [jax.ShapeDtypeStruct(o, jnp.float32) for o in outs]
    vmem = pl.BlockSpec(memory_space=pltpu.VMEM)
    return pl.pallas_call(
        kernel,
        out_shape=shapes,
        in_specs=[vmem] * len(args),
        out_specs=[vmem] * len(outs),
        compiler_params=pltpu.CompilerParams(vmem_limit_bytes=16 << 20),
        **kwargs,
    )(*args)


def same(v):
    return v


def start_of(v, drive, kept=same):
    nsum = around(v)
    coarse = kept(coarse_of(v, nsum, drive))
    fine = kept(fine_of(v, nsum, drive))
    for _ in range(FINE - 1):
        fine = kept(fine_of(fine, around(fine), drive))
    return fine, coarse


def ends_of(first, mine, theirs, drive, kept=same):
    f_a, f_b = picked(first, mine[0], theirs[0])
    g_a, g_b = picked(first, mine[1], theirs[1])
    e_a = g_a + (f_a - g_a)
    e_b = kept(coarse_of(e_a, around(e_a), drive)) + (f_b - g_b)
    return e_a, e_b


def chain(current, d_a, d_b, drive, kept=same):
    e_a = kept(coarse_of(current, around(current), drive)) + d_a
    e_b = kept(coarse_of(e_a, around(e_a), drive)) + d_b
    return e_a, e_b


def picked(first, own, other):
    return jnp.where(first, own, other), jnp.where(first, other, own)


def field(ref, kind, kinds, start, size):
    height = ref.shape[0] // kinds
    return ref.at[pl.ds(pl.multiple_of(kind * height + start, 8), size), :]


def mixed(upper, lower):
    row = lax.broadcasted_iota(jnp.int32, upper.shape, 0)
    return jnp.where(row < CUT, upper, lower)


def sublane(v):
    return lax.broadcasted_iota(jnp.int32, v.shape, 0)


def folded(v):
    width = v.shape[1]
    half, quarter = width // 2, width // 4
    four = mixed(v[:, :half], pltpu.roll(v[:, half:], 4, 0))
    row = sublane(four[:, :quarter])
    two = pltpu.roll(v[:, :quarter], 4, 0)
    for i, shift in ((1, 6), (2, 0), (3, 2)):
        part = v[:, i * quarter : (i + 1) * quarter]
        part = pltpu.roll(part, shift, 0) if shift else part
        two = jnp.where(row < 2 * i, two, part)
    return jnp.concatenate([four, two], axis=1)


def unfolded(v):
    half = v.shape[1] * 2 // 3
    four, two = v[:, :half], v[:, half:]
    low = [pltpu.roll(two, 4, 0), pltpu.roll(two, 2, 0), two, pltpu.roll(two, 6, 0)]
    return mixed(
        jnp.concatenate([four, pltpu.roll(four, 4, 0)], axis=1),
        jnp.concatenate(low, axis=1),
    )


def place():
    t = lax.axis_index("tm")
    return t % 2, t // 2


def at_edge(core):
    r, rows = lax.axis_index("rows"), lax.axis_size("rows")
    return ((core == 0) & (r == 0)) | ((core == 1) & (r == rows - 1))


def inner_row(half, core):
    return pl.multiple_of(half - 16 + 8 * core, 8)


def middle_row(half, core):
    return pl.multiple_of((half + 8) * core, 8)


def outer_row(half, core):
    return pl.multiple_of((2 * half - WIDE) * core, 8)


def load_kernel(half, starts, drive, own, held, inner, sems):
    core, chip = place()
    copies = []
    for i, (row, size) in enumerate(((half - 16, 32), (0, half - 16), (half + 16, half - 16))):
        rows = pl.ds(row, size)
        pair = (
            pltpu.make_async_copy(starts.at[0, rows, :], own.at[rows, :], sems.at[2 * i]),
            pltpu.make_async_copy(drive.at[rows, :], held.at[rows, :], sems.at[2 * i + 1]),
        )
        for copy in pair:
            copy.start()
        copies.append(pair)

    for copy in copies[0]:
        copy.wait()

    @pl.when(chip == 0)
    def _():
        rows = pl.ds(inner_row(half, core), 24)
        fine, coarse = start_of(own[rows, :], held[rows, :])
        inner[0:24, :] = fine
        inner[24:48, :] = coarse

    for copy in (*copies[1], *copies[2]):
        copy.wait()


def inner_kernel(half, side, own, other, drive, mine, sent, ends, edge=None):
    core, chip = place()
    first = core == 0
    width = drive.shape[1]
    mid = width // 2

    def columns(ref, rows):
        if side == 0:
            parts = ref[rows, width - 128 :], ref[rows, : mid + 128]
        else:
            parts = ref[rows, mid - 128 :], ref[rows, :128]
        return jnp.concatenate(parts, axis=1)

    @pl.when(chip == 0)
    def _():
        rows = pl.ds(inner_row(half, core), 24)
        d = columns(drive, rows)
        theirs = start_of(columns(other, rows), d)
        known = columns(mine, pl.ds(0, 24)), columns(mine, pl.ds(24, 24))
        e_a, e_b = ends_of(first, known, theirs, d)
        e_a, e_b = e_a[:, 128:-128], e_b[:, 128:-128]
        frame = pltpu.roll(e_b, 24 - CUT, 0)
        whole, part = picked(first, frame[:8], frame[8:16])
        part = jnp.where(first, part, pltpu.roll(part, 6, 0))
        sent[...] = jnp.concatenate([whole, folded(part)], axis=1)
        ends[0:24, :] = e_a
        ends[24:48, :] = e_b

    if edge is not None:
        rows = pl.ds(outer_row(half, core), 8)
        a, b = picked(first, own[rows, :], other[rows, :])
        edge[0:8, :] = a
        edge[8:16, :] = b
        edge[16:24, :] = drive[rows, :]


def middle_kernel(half, own, other, drive, sent, ends):
    core, chip = place()
    first = core == 0

    @pl.when(chip == 0)
    def _():
        rows = pl.ds(middle_row(half, core), 24)
        d = drive[rows, :]
        mine, theirs = start_of(own[rows, :], d), start_of(other[rows, :], d)
        e_a, e_b = ends_of(first, mine, theirs, d)
        sent[...] = pltpu.roll(e_b, 24 - CUT, 0)[:16]
        ends[0:24, :] = e_a
        ends[24:48, :] = e_b


def state_kernel(half, own, other, drive, state):
    core, chip = place()
    first = core == 0

    @pl.when(chip > 0)
    def _():
        size = half + WIDE
        rows = pl.ds(pl.multiple_of((half - WIDE) * core, 8), size)
        d = drive[rows, :]
        state[2 * size : 3 * size, :] = d
        for mine_first, ref in ((True, own), (False, other)):
            fine, coarse = start_of(ref[rows, :], d)
            kind = jnp.where(first == mine_first, 0, 1)
            field(state, kind, 3, 0, size)[...] = fine - coarse


def outer_kernel(half, own, other, drive, got, inner_state, sent, ends, state):
    core, chip = place()
    first = core == 0
    rows = pl.ds(outer_row(half, core), 8)
    a, b = picked(first, own[rows, :], other[rows, :])
    near = (a, b, drive[rows, :])
    far = [got[8 * i : 8 * i + 8, :] for i in range(3)]
    upper = [jnp.where(first, f, n) for f, n in zip(far, near)]
    lower = [jnp.where(first, n, f) for f, n in zip(far, near)]
    a, b, d = (jnp.concatenate(p) for p in zip(upper, lower))
    tile = lax.broadcasted_iota(jnp.int32, a.shape, 0) // 8
    inside = ~(at_edge(core) & (tile == core))

    def kept(v):
        return jnp.where(inside, v, 0.0)

    f_a, g_a = start_of(kept(a), d, kept)
    f_b, g_b = start_of(kept(b), d, kept)

    @pl.when(chip == 0)
    def _():
        e_a = g_a + (f_a - g_a)
        e_b = kept(coarse_of(e_a, around(e_a), d)) + (f_b - g_b)
        frame = pltpu.roll(e_b, 16 - CUT, 0)[:8]
        sent[...] = folded(jnp.where(first, pltpu.roll(frame, 6, 0), frame))
        ends[0:16, :] = e_a
        ends[16:32, :] = e_b

    size = half + WIDE
    fields = (f_a - g_a, f_b - g_b, d)

    @pl.when((chip > 0) & first)
    def _():
        for kind, v in enumerate(fields):
            before = field(inner_state, kind, 3, 0, 16)[...]
            field(state, kind, 3, 0, 8)[...] = v[:8]
            field(state, kind, 3, 8, 8)[...] = mixed(v[8:], before[:8])
            field(state, kind, 3, 16, 8)[...] = before[8:]

    @pl.when((chip > 0) & (core == 1))
    def _():
        for kind, v in enumerate(fields):
            before = field(inner_state, kind, 3, size - 16, 16)[...]
            field(state, kind, 3, 0, 8)[...] = before[:8]
            field(state, kind, 3, 8, 8)[...] = mixed(before[8:], v[:8])
            field(state, kind, 3, 16, 8)[...] = v[8:]


def put_ends(first, e_a, e_b, keep, send):
    kept, sent = picked(first, e_a, e_b)
    keep[...] = kept
    send[...] = sent


def inner_end(
    half, left, right, state, ends_left, ends_right, middle, outer, keep, send, frame
):
    core, chip = place()
    first = core == 0
    mid = ends_left.shape[1]

    @pl.when(chip == 0)
    def _():
        def rows(kind, tile):
            into = pl.ds(24 * kind + 8 * tile, 8)
            return jnp.concatenate([ends_left[into, :], ends_right[into, :]], axis=1)

        def known(kind):
            lower = [rows(kind, i) for i in range(3)]
            upper = [field(middle, kind, 2, 8 * i, 8)[...] for i in range(3)]
            last = [field(outer, kind, 2, 8 * i, 8)[...] for i in range(2)]
            return jnp.concatenate(
                [
                    lower[1],
                    jnp.where(first, upper[1], mixed(lower[2], upper[0])),
                    jnp.where(first, mixed(upper[2], lower[0]), upper[1]),
                    jnp.where(first, mixed(last[1], upper[0]), mixed(upper[2], last[0])),
                ]
            )

        kept, sent = picked(first, known(0), known(1))
        keep[...] = kept
        send[...] = sent

    @pl.when(chip > 0)
    def _():
        parts = left[...], right[...]
        whole = jnp.concatenate([p[:, :mid] for p in parts], axis=1)
        part = jnp.concatenate([unfolded(p[:, mid:]) for p in parts], axis=1)
        part = jnp.where(first, part, pltpu.roll(part, 2, 0))
        top, low = picked(first, whole, part)
        frame[0:8, :] = top
        frame[8:16, :] = low
        current = pltpu.roll(jnp.concatenate([top, low, low]), CUT, 0)
        row = (half - 16) * (1 - core)
        d_a, d_b, d = (field(state, kind, 3, row, 24)[...] for kind in range(3))
        e_a, e_b = chain(current, d_a, d_b, d)
        kept, sent = picked(first, e_a[8:16], e_b[8:16])
        keep[0:8, :] = kept
        send[0:8, :] = sent


def put_ends(first, e_a, e_b, keep, send):
    kept, sent = picked(first, e_a, e_b)
    keep[...] = kept
    send[...] = sent


def middle_end(inner, middle, state, keep, send, current):
    core, chip = place()
    first = core == 0

    @pl.when((chip > 0) & first)
    def _():
        current[...] = pltpu.roll(jnp.concatenate([middle[...], inner[...]]), CUT, 0)

    @pl.when((chip > 0) & (core == 1))
    def _():
        current[...] = pltpu.roll(jnp.concatenate([inner[...], middle[...]]), 32 - CUT, 0)

    @pl.when(chip > 0)
    def _():
        d_a, d_b, d = (field(state, kind, 3, 8 * core, 32)[...] for kind in range(3))
        e_a, e_b = chain(current[...], d_a, d_b, d)
        put_ends(first, e_a[8:24], e_b[8:24], keep, send)


def outer_end(middle, outer, state, keep, send, current):
    core, chip = place()
    first = core == 0

    @pl.when((chip > 0) & first)
    def _():
        part = pltpu.roll(unfolded(outer[...]), 2, 0)
        current[...] = pltpu.roll(jnp.concatenate([part, middle[...]]), CUT, 0)

    @pl.when((chip > 0) & (core == 1))
    def _():
        part = unfolded(outer[...])
        current[...] = pltpu.roll(jnp.concatenate([middle[...], part]), 24 - CUT, 0)

    @pl.when(chip > 0)
    def _():
        d_a, d_b, d = (field(state, kind, 3, 0, 24)[...] for kind in range(3))
        tile = lax.broadcasted_iota(jnp.int32, d.shape, 0) // 8
        inside = ~(at_edge(core) & (tile == 2 * core))
        e_a = coarse_of(current[...], around(current[...]), d) + d_a
        e_a = jnp.where(inside, e_a, 0.0)
        e_b = coarse_of(e_a, around(e_a), d) + d_b
        put_ends(first, e_a[8:16], e_b[8:16], keep, send)


def write_kernel(half, last, *refs):
    count = 3
    pieces, out, sems = refs[:count], refs[-2], refs[-1]
    core, chip = place()

    def copy_all(order):
        copies = []
        for i, (mine, part, source, begin, size) in enumerate(order):
            upper = (half - 8, 8, 0)[part]
            lower = (half, half + 8, 2 * half - 8)[part]
            row = pl.multiple_of(jnp.where((core == 0) == mine, upper, lower), 8)
            copy = pltpu.make_async_copy(
                pieces[source].at[pl.ds(begin, size), :],
                out.at[0, pl.ds(row, size), :],
                sems.at[i],
            )
            copy.start()
            copies.append(copy)
        for copy in copies:
            copy.wait()

    parts = ((0, 0, 8), (1, 8, half - 16), (2, half - 8, 8))
    if last:

        @pl.when(chip > 0)
        def _():
            copy_all(((False, 1, 0, 0, half - 16), (True, 2, 1, 0, 8), (False, 2, 2, 0, 8)))

    else:

        @pl.when(chip == 0)
        def _():
            copy_all(
                [(mine, part, source, *rows) for mine, source in ((True, 0), (False, 2)) for part, *rows in parts]
            )

        @pl.when(chip > 0)
        def _():
            copy_all(((True, 0, 0, 0, 8), (True, 1, 1, 0, half - 16), (False, 0, 2, 0, 8)))


def written(half, pieces, shape, into=None):
    vmem, anywhere = pl.BlockSpec(memory_space=pltpu.VMEM), pl.BlockSpec(memory_space=pl.ANY)
    extra = () if into is None else (into,)
    return pl.pallas_call(
        functools.partial(write_kernel, half, into is not None),
        out_shape=jax.ShapeDtypeStruct(shape, jnp.float32),
        in_specs=[vmem] * 3 + [anywhere] * len(extra),
        out_specs=anywhere,
        input_output_aliases={3: 0} if extra else {},
        scratch_shapes=[pltpu.SemaphoreType.DMA((6,))],
        compiler_params=pltpu.CompilerParams(vmem_limit_bytes=16 << 20),
    )(*pieces, *extra)


def after(value, earlier):
    return lax.optimization_barrier((value, earlier))[0]


def masked_update(update, v, drive, inside):
    wide = (
        jnp.roll(v, 1, axis=0) + jnp.roll(v, -1, axis=0)
    ) + (jnp.roll(v, 1, axis=1) + jnp.roll(v, -1, axis=1))
    return jnp.where(inside, update(v, wide, drive), 0.0)


def long_chain(own, drive):
    height = own.shape[0]
    half = height // 2
    groups, slices, rows = (lax.axis_size(a) for a in AXES)
    t, r = lax.axis_index("tm"), lax.axis_index("rows")
    core, chip = t % 2, t // 2
    first = core == 0
    away = outward(groups, rows)

    def cut(field, start, size):
        return lax.dynamic_slice_in_dim(field, start, size, axis=0)

    other = routed(own, partner)
    s_a, s_b = picked(first, own, other)
    edge = core * (height - WIDE)
    got = routed(jnp.concatenate([cut(f, edge, WIDE) for f in (s_a, s_b, drive)]), away)

    def sided(body, outer, inner):
        return jnp.where(
            first,
            jnp.concatenate([outer, body, inner]),
            jnp.concatenate([inner, body, outer]),
        )

    def window(field, place):
        body = cut(field, core * half, half)
        inner = cut(field, jnp.where(first, half, half - WIDE), WIDE)
        return sided(body, got[place * WIDE : (place + 1) * WIDE], inner)

    w_a, w_b, w_d = (window(f, i) for i, f in enumerate((s_a, s_b, drive)))
    row = lax.broadcasted_iota(jnp.int32, (half + 2 * WIDE, 1), 0)
    row = row + r * height + core * half - WIDE
    inside = (row >= 0) & (row < rows * height)
    w_a, w_b = jnp.where(inside, w_a, 0.0), jnp.where(inside, w_b, 0.0)

    def delta(v):
        fine = v
        for _ in range(FINE):
            fine = masked_update(fine_of, fine, w_d, inside)
        return fine - masked_update(coarse_of, v, w_d, inside)

    d_a, d_b = delta(w_a), delta(w_b)

    def both(v):
        e_a = masked_update(coarse_of, v, w_d, inside) + d_a
        return e_a, masked_update(coarse_of, e_a, w_d, inside) + d_b

    def extended(v):
        last = WIDE + half - 2
        inner = routed(cut(v, jnp.where(first, last, WIDE), 2), partner)
        outer = routed(cut(v, jnp.where(first, WIDE, last), 2), away)
        return sided(v[WIDE : WIDE + half], outer, inner)

    e_a, e_b = both(w_a)
    for stage in range(slices // 2 - 1):
        moved = e_b[WIDE - 2 : WIDE + half + 2] if stage == 0 else extended(e_b)
        arrived = routed(moved, stage_swap(stage))
        current = jnp.pad(arrived, ((WIDE - 2, WIDE - 2), (0, 0)))
        n_a, n_b = both(jnp.where(inside, current, 0.0))
        here = chip == stage + 1
        e_a, e_b = jnp.where(here, n_a, e_a), jnp.where(here, n_b, e_b)

    kept, sent = picked(first, e_a[WIDE : WIDE + half], e_b[WIDE : WIDE + half])
    back = routed(sent, partner)
    return jnp.concatenate(picked(first, kept, back))[None]


def on_device(starts, drive):
    own = starts[0]
    if lax.axis_size("tm") != 4:
        return long_chain(own, drive)
    return two_chips(starts, drive)


def two_chips(starts, drive):
    _, height, width = starts.shape
    half = height // 2
    groups, rows = lax.axis_size("groups"), lax.axis_size("rows")
    vmem = pl.BlockSpec(memory_space=pltpu.VMEM)

    other = routed(starts[0], partner)
    own, held, mine = pl.pallas_call(
        functools.partial(load_kernel, half),
        out_shape=[
            jax.ShapeDtypeStruct((size, width), jnp.float32) for size in (height, height, 48)
        ],
        in_specs=[pl.BlockSpec(memory_space=pltpu.HBM)] * 2,
        out_specs=[vmem] * 3,
        scratch_shapes=[pltpu.SemaphoreType.DMA((6,))],
        compiler_params=pltpu.CompilerParams(vmem_limit_bytes=51 << 20),
        cost_estimate=pl.CostEstimate(
            flops=60 * 24 * width, bytes_accessed=16 * height * width, transcendentals=0
        ),
        name="load",
    )(starts, drive)
    mid = width // 2
    packed = mid * 7 // 4
    sent_l, ends_l = compute(
        functools.partial(inner_kernel, half, 0), [(8, packed), (48, mid)], (own, other, held, mine)
    )
    here_l = routed(sent_l, stage_swap(0))
    sent_r, ends_r, edge = compute(
        functools.partial(inner_kernel, half, 1),
        [(8, packed), (48, mid), (24, width)],
        (own, other, held, after(mine, sent_l)),
    )
    here_r = routed(sent_r, stage_swap(0))
    got = routed(edge, outward(groups, rows))
    sent_2, ends_2 = compute(
        functools.partial(middle_kernel, half),
        [(16, width), (48, width)],
        (own, other, after(held, sent_r)),
    )
    here_2 = routed(sent_2, stage_swap(0))
    (state,) = compute(
        functools.partial(state_kernel, half),
        [(3 * (half + WIDE), width)],
        (own, other, after(held, sent_2)),
    )
    sent_3, ends_3, state_3 = compute(
        functools.partial(outer_kernel, half),
        [(8, width * 3 // 4), (32, width), (3 * 24, width)],
        (own, other, held, got, state),
    )
    here_3 = routed(sent_3, stage_swap(0))

    keep_1, send_1, frame = compute(
        functools.partial(inner_end, half),
        [(half, width), (half, width), (16, width)],
        (here_l, here_r, state, ends_l, ends_r, ends_2, ends_3),
    )
    back_1 = routed(send_1, partner)
    keep_2, send_2 = compute(
        middle_end,
        [(half - 16, width)] * 2,
        (frame, here_2, state),
        scratch_shapes=[pltpu.VMEM((32, width), jnp.float32)],
    )
    back_2 = routed(send_2, partner)
    out = written(half, (keep_1, keep_2, back_1), starts.shape)
    out, state_3 = lax.optimization_barrier((out, state_3))
    keep_3, send_3 = compute(
        outer_end,
        [(8, width)] * 2,
        (here_2, here_3, state_3),
        scratch_shapes=[pltpu.VMEM((24, width), jnp.float32)],
    )
    back_3 = routed(send_3, partner)
    return written(half, (back_2, keep_3, back_3), starts.shape, into=out)


def solution(mesh):
    in_specs = (P(("groups", "tm"), "rows", None), P("rows", None))
    out_specs = P(("groups", "tm"), "rows", None)
    return jax.shard_map(
        on_device, mesh=mesh, in_specs=in_specs, out_specs=out_specs, check_vma=False
    )
```

```python
import functools

import jax
import jax.numpy as jnp
from jax import lax
from jax.experimental import pallas as pl
from jax.experimental.pallas import tpu as pltpu
from jax.sharding import PartitionSpec as P


FINE = 3
WIDE = 8
CUT = 4


diffusion = 2.0
step_fine = 0.1
coarse_step = FINE * step_fine
damping = 1.0 + 4.0 * diffusion * coarse_step

AXES = ("groups", "tm", "rows")


def routed(block, route):
    groups, slices, rows = (lax.axis_size(a) for a in AXES)
    pairs = []
    for g in range(groups):
        for t in range(slices):
            for r in range(rows):
                to_g, to_t, to_r = route(g, t, r)
                source = (g * slices + t) * rows + r
                pairs.append((source, (to_g * slices + to_t) * rows + to_r))
    return lax.ppermute(block, AXES, pairs)


def partner(g, t, r):
    return g, t ^ 1, r


def outward(groups, rows):
    def route(g, t, r):
        to_r = r + 1 if t & 1 else r - 1
        if 0 <= to_r < rows:
            return g, t ^ 1, to_r
        other = g ^ 1
        return (other, t, r) if other < groups else (g, t, r)

    return route


def stage_swap(stage):
    def route(g, t, r):
        chip = t // 2
        if chip == stage:
            return g, t + 2, r
        if chip == stage + 1:
            return g, t - 2, r
        return g, t, r

    return route


def around(v):
    height, width = v.shape
    return (pltpu.roll(v, 1, 0) + pltpu.roll(v, height - 1, 0)) + (
        pltpu.roll(v, 1, 1) + pltpu.roll(v, width - 1, 1)
    )


def fine_of(v, nsum, drive):
    return (
        step_fine * diffusion * nsum
        + v * ((1.0 + step_fine - 4.0 * step_fine * diffusion) - step_fine * (v * v))
        + step_fine * drive
    )


def coarse_of(v, nsum, drive):
    scale = coarse_step / damping
    return (
        scale * diffusion * nsum
        + v * ((1.0 + coarse_step) / damping - scale * (v * v))
        + scale * drive
    )


def compute(kernel, outs, args, **kwargs):
    shapes = [jax.ShapeDtypeStruct(o, jnp.float32) for o in outs]
    vmem = pl.BlockSpec(memory_space=pltpu.VMEM)
    return pl.pallas_call(
        kernel,
        out_shape=shapes,
        in_specs=[vmem] * len(args),
        out_specs=[vmem] * len(outs),
        compiler_params=pltpu.CompilerParams(vmem_limit_bytes=16 << 20),
        **kwargs,
    )(*args)


def same(v):
    return v


def start_of(v, drive, kept=same):
    nsum = around(v)
    coarse = kept(coarse_of(v, nsum, drive))
    fine = kept(fine_of(v, nsum, drive))
    for _ in range(FINE - 1):
        fine = kept(fine_of(fine, around(fine), drive))
    return fine, coarse


def ends_of(first, mine, theirs, drive, kept=same):
    f_a, f_b = picked(first, mine[0], theirs[0])
    g_a, g_b = picked(first, mine[1], theirs[1])
    e_a = g_a + (f_a - g_a)
    e_b = kept(coarse_of(e_a, around(e_a), drive)) + (f_b - g_b)
    return e_a, e_b


def chain(current, d_a, d_b, drive, kept=same):
    e_a = kept(coarse_of(current, around(current), drive)) + d_a
    e_b = kept(coarse_of(e_a, around(e_a), drive)) + d_b
    return e_a, e_b


def picked(first, own, other):
    return jnp.where(first, own, other), jnp.where(first, other, own)


def field(ref, kind, kinds, start, size):
    height = ref.shape[0] // kinds
    return ref.at[pl.ds(pl.multiple_of(kind * height + start, 8), size), :]


def mixed(upper, lower):
    row = lax.broadcasted_iota(jnp.int32, upper.shape, 0)
    return jnp.where(row < CUT, upper, lower)


def sublane(v):
    return lax.broadcasted_iota(jnp.int32, v.shape, 0)


def folded(v):
    width = v.shape[1]
    half, quarter = width // 2, width // 4
    four = mixed(v[:, :half], pltpu.roll(v[:, half:], 4, 0))
    row = sublane(four[:, :quarter])
    two = pltpu.roll(v[:, :quarter], 4, 0)
    for i, shift in ((1, 6), (2, 0), (3, 2)):
        part = v[:, i * quarter : (i + 1) * quarter]
        part = pltpu.roll(part, shift, 0) if shift else part
        two = jnp.where(row < 2 * i, two, part)
    return jnp.concatenate([four, two], axis=1)


def unfolded(v):
    half = v.shape[1] * 2 // 3
    four, two = v[:, :half], v[:, half:]
    low = [pltpu.roll(two, 4, 0), pltpu.roll(two, 2, 0), two, pltpu.roll(two, 6, 0)]
    return mixed(
        jnp.concatenate([four, pltpu.roll(four, 4, 0)], axis=1),
        jnp.concatenate(low, axis=1),
    )


def place():
    t = lax.axis_index("tm")
    return t % 2, t // 2


def at_edge(core):
    r, rows = lax.axis_index("rows"), lax.axis_size("rows")
    return ((core == 0) & (r == 0)) | ((core == 1) & (r == rows - 1))


def inner_row(half, core):
    return pl.multiple_of(half - 16 + 8 * core, 8)


def middle_row(half, core):
    return pl.multiple_of((half + 8) * core, 8)


def outer_row(half, core):
    return pl.multiple_of((2 * half - WIDE) * core, 8)


def load_kernel(half, starts, drive, own, held, inner, sems):
    core, chip = place()
    copies = []
    for i, (row, size) in enumerate(((half - 16, 32), (0, half - 16), (half + 16, half - 16))):
        rows = pl.ds(row, size)
        pair = (
            pltpu.make_async_copy(starts.at[0, rows, :], own.at[rows, :], sems.at[2 * i]),
            pltpu.make_async_copy(drive.at[rows, :], held.at[rows, :], sems.at[2 * i + 1]),
        )
        for copy in pair:
            copy.start()
        copies.append(pair)

    for copy in copies[0]:
        copy.wait()

    @pl.when(chip == 0)
    def _():
        rows = pl.ds(inner_row(half, core), 24)
        fine, coarse = start_of(own[rows, :], held[rows, :])
        inner[0:24, :] = fine
        inner[24:48, :] = coarse

    for copy in (*copies[1], *copies[2]):
        copy.wait()


def inner_kernel(half, side, own, other, drive, mine, sent, ends, edge=None):
    core, chip = place()
    first = core == 0
    width = drive.shape[1]
    mid = width // 2

    def columns(ref, rows):
        if side == 0:
            parts = ref[rows, width - 128 :], ref[rows, : mid + 128]
        else:
            parts = ref[rows, mid - 128 :], ref[rows, :128]
        return jnp.concatenate(parts, axis=1)

    @pl.when(chip == 0)
    def _():
        rows = pl.ds(inner_row(half, core), 24)
        d = columns(drive, rows)
        theirs = start_of(columns(other, rows), d)
        known = columns(mine, pl.ds(0, 24)), columns(mine, pl.ds(24, 24))
        e_a, e_b = ends_of(first, known, theirs, d)
        e_a, e_b = e_a[:, 128:-128], e_b[:, 128:-128]
        frame = pltpu.roll(e_b, 24 - CUT, 0)
        whole, part = picked(first, frame[:8], frame[8:16])
        part = jnp.where(first, part, pltpu.roll(part, 6, 0))
        sent[...] = jnp.concatenate([whole, folded(part)], axis=1)
        ends[0:24, :] = e_a
        ends[24:48, :] = e_b

    if edge is not None:
        rows = pl.ds(outer_row(half, core), 8)
        a, b = picked(first, own[rows, :], other[rows, :])
        fields = (jnp.where(first, v, pltpu.roll(v, 6, 0)) for v in (a, b, drive[rows, :]))
        edge[...] = jnp.concatenate([folded(v) for v in fields], axis=1)


def middle_kernel(half, own, other, drive, sent, ends, delta):
    core, chip = place()
    first = core == 0

    @pl.when(chip == 0)
    def _():
        rows = pl.ds(middle_row(half, core), 24)
        d = drive[rows, :]
        mine, theirs = start_of(own[rows, :], d), start_of(other[rows, :], d)
        e_a, e_b = ends_of(first, mine, theirs, d)
        sent[...] = pltpu.roll(e_b, 24 - CUT, 0)[:16]
        ends[0:24, :] = e_a
        ends[24:48, :] = e_b

    @pl.when(chip > 0)
    def _():
        rows = receiver_rows(half, core)
        fine, coarse = start_of(own[rows, :], drive[rows, :])
        delta[...] = fine - coarse


def receiver_rows(half, core):
    return pl.ds(pl.multiple_of((half - WIDE) * core, 8), half + WIDE)


def state_kernel(half, other, drive, theirs):
    core, chip = place()

    @pl.when(chip > 0)
    def _():
        rows = receiver_rows(half, core)
        fine, coarse = start_of(other[rows, :], drive[rows, :])
        theirs[...] = fine - coarse


def outer_window(half, own, other, drive, got):
    core, _ = place()
    first = core == 0
    rows = pl.ds(outer_row(half, core), 8)
    a, b = picked(first, own[rows, :], other[rows, :])
    near = (a, b, drive[rows, :])
    size = got.shape[1] // 3
    far = [unfolded(got[:, i * size : (i + 1) * size]) for i in range(3)]
    far = [jnp.where(first, pltpu.roll(v, 2, 0), v) for v in far]
    upper = [jnp.where(first, f, n) for f, n in zip(far, near)]
    lower = [jnp.where(first, n, f) for f, n in zip(far, near)]
    a, b, d = (jnp.concatenate(p) for p in zip(upper, lower))
    inside = ~(at_edge(core) & (sublane(a) // 8 == core))

    def kept(v):
        return jnp.where(inside, v, 0.0)

    return kept(a), kept(b), d, kept


def outer_kernel(half, own, other, drive, got, sent, ends):
    core, chip = place()
    first = core == 0

    @pl.when(chip == 0)
    def _():
        a, b, d, kept = outer_window(half, own, other, drive, got)
        (f_a, g_a), (f_b, g_b) = start_of(a, d, kept), start_of(b, d, kept)
        e_a = g_a + (f_a - g_a)
        e_b = kept(coarse_of(e_a, around(e_a), d)) + (f_b - g_b)
        frame = pltpu.roll(e_b, 16 - CUT, 0)[:8]
        sent[...] = folded(jnp.where(first, pltpu.roll(frame, 6, 0), frame))
        ends[0:16, :] = e_a
        ends[16:32, :] = e_b


def outer_state_kernel(half, own, other, drive, got, mine, theirs, state):
    core, chip = place()
    first = core == 0

    @pl.when(chip > 0)
    def _():
        a, b, d, kept = outer_window(half, own, other, drive, got)
        (f_a, g_a), (f_b, g_b) = start_of(a, d, kept), start_of(b, d, kept)
        rows = pl.ds(pl.multiple_of((half - WIDE) * core, 8), 16)
        before = picked(first, mine[rows, :], theirs[rows, :])
        d_rows = pl.ds(pl.multiple_of((2 * half - 16) * core, 8), 16)
        fields = zip((f_a - g_a, f_b - g_b, d), (*before, drive[d_rows, :]))
        for kind, (v, near) in enumerate(fields):
            top = jnp.where(first, v[:8], near[:8])
            mid = jnp.where(first, mixed(v[8:], near[:8]), mixed(near[8:], v[:8]))
            low = jnp.where(first, near[8:], v[8:])
            state[24 * kind : 24 * kind + 24, :] = jnp.concatenate([top, mid, low])


def inner_end(half, left, right, drive, mine, theirs, keep, send, frame):
    core, chip = place()
    first = core == 0

    @pl.when(chip > 0)
    def _():
        mid = left.shape[1] * 4 // 7
        parts = left[...], right[...]
        whole = jnp.concatenate([p[:, :mid] for p in parts], axis=1)
        part = jnp.concatenate([unfolded(p[:, mid:]) for p in parts], axis=1)
        part = jnp.where(first, part, pltpu.roll(part, 2, 0))
        top, low = picked(first, whole, part)
        frame[0:8, :] = top
        frame[8:16, :] = low
        current = pltpu.roll(jnp.concatenate([top, low, low]), CUT, 0)
        rows = pl.ds(pl.multiple_of((half - 16) * (1 - core), 8), 24)
        d_a, d_b = picked(first, mine[rows, :], theirs[rows, :])
        d = drive[pl.ds(inner_row(half, core), 24), :]
        e_a, e_b = chain(current, d_a, d_b, d)
        put_ends(first, e_a[8:16], e_b[8:16], keep, send)


def gather_kernel(ends_left, ends_right, middle, outer, keep_8, send_8, keep, send):
    core, chip = place()
    first = core == 0

    @pl.when(chip == 0)
    def _():
        def rows(kind, tile):
            into = pl.ds(24 * kind + 8 * tile, 8)
            return jnp.concatenate([ends_left[into, :], ends_right[into, :]], axis=1)

        def known(kind):
            lower = [rows(kind, i) for i in range(3)]
            upper = [field(middle, kind, 2, 8 * i, 8)[...] for i in range(3)]
            last = [field(outer, kind, 2, 8 * i, 8)[...] for i in range(2)]
            return jnp.concatenate(
                [
                    lower[1],
                    jnp.where(first, upper[1], mixed(lower[2], upper[0])),
                    jnp.where(first, mixed(upper[2], lower[0]), upper[1]),
                    jnp.where(first, mixed(last[1], upper[0]), mixed(upper[2], last[0])),
                ]
            )

        put_ends(first, known(0), known(1), keep, send)

    @pl.when(chip > 0)
    def _():
        keep[0:8, :] = keep_8[...]
        send[0:8, :] = send_8[...]


def put_ends(first, e_a, e_b, keep, send):
    kept, sent = picked(first, e_a, e_b)
    keep[...] = kept
    send[...] = sent


def middle_end(half, inner, middle, drive, mine, theirs, keep, send, current):
    core, chip = place()
    first = core == 0

    @pl.when((chip > 0) & first)
    def _():
        current[...] = pltpu.roll(jnp.concatenate([middle[...], inner[...]]), CUT, 0)

    @pl.when((chip > 0) & (core == 1))
    def _():
        current[...] = pltpu.roll(jnp.concatenate([inner[...], middle[...]]), half - CUT, 0)

    @pl.when(chip > 0)
    def _():
        rows = pl.ds(pl.multiple_of(8 * core, 8), half)
        d_a, d_b = picked(first, mine[rows, :], theirs[rows, :])
        d = drive[pl.ds(pl.multiple_of(half * core, 8), half), :]
        e_a, e_b = chain(current[...], d_a, d_b, d)
        put_ends(first, e_a[8 : half - 8], e_b[8 : half - 8], keep, send)


def outer_end(middle, outer, state, keep, send, current):
    core, chip = place()
    first = core == 0

    @pl.when((chip > 0) & first)
    def _():
        part = pltpu.roll(unfolded(outer[...]), 2, 0)
        current[...] = pltpu.roll(jnp.concatenate([part, middle[...]]), CUT, 0)

    @pl.when((chip > 0) & (core == 1))
    def _():
        part = unfolded(outer[...])
        current[...] = pltpu.roll(jnp.concatenate([middle[...], part]), 24 - CUT, 0)

    @pl.when(chip > 0)
    def _():
        d_a, d_b, d = (field(state, kind, 3, 0, 24)[...] for kind in range(3))
        tile = lax.broadcasted_iota(jnp.int32, d.shape, 0) // 8
        inside = ~(at_edge(core) & (tile == 2 * core))
        e_a = coarse_of(current[...], around(current[...]), d) + d_a
        e_a = jnp.where(inside, e_a, 0.0)
        e_b = coarse_of(e_a, around(e_a), d) + d_b
        put_ends(first, e_a[8:16], e_b[8:16], keep, send)


def write_kernel(half, last, *refs):
    count = 3
    pieces, out, sems = refs[:count], refs[-2], refs[-1]
    core, chip = place()

    def copy_all(order):
        copies = []
        for i, (mine, part, source, begin, size) in enumerate(order):
            upper = (half - 8, 8, 0)[part]
            lower = (half, half + 8, 2 * half - 8)[part]
            row = pl.multiple_of(jnp.where((core == 0) == mine, upper, lower), 8)
            copy = pltpu.make_async_copy(
                pieces[source].at[pl.ds(begin, size), :],
                out.at[0, pl.ds(row, size), :],
                sems.at[i],
            )
            copy.start()
            copies.append(copy)
        for copy in copies:
            copy.wait()

    parts = ((0, 0, 8), (1, 8, half - 16), (2, half - 8, 8))
    if last:

        @pl.when(chip > 0)
        def _():
            copy_all(((False, 1, 0, 0, half - 16), (True, 2, 1, 0, 8), (False, 2, 2, 0, 8)))

    else:

        @pl.when(chip == 0)
        def _():
            copy_all(
                [(mine, part, source, *rows) for mine, source in ((True, 0), (False, 2)) for part, *rows in parts]
            )

        @pl.when(chip > 0)
        def _():
            copy_all(((True, 0, 0, 0, 8), (True, 1, 1, 0, half - 16), (False, 0, 2, 0, 8)))


def written(half, pieces, shape, into=None):
    vmem, anywhere = pl.BlockSpec(memory_space=pltpu.VMEM), pl.BlockSpec(memory_space=pl.ANY)
    extra = () if into is None else (into,)
    return pl.pallas_call(
        functools.partial(write_kernel, half, into is not None),
        out_shape=jax.ShapeDtypeStruct(shape, jnp.float32),
        in_specs=[vmem] * 3 + [anywhere] * len(extra),
        out_specs=anywhere,
        input_output_aliases={3: 0} if extra else {},
        scratch_shapes=[pltpu.SemaphoreType.DMA((6,))],
        compiler_params=pltpu.CompilerParams(vmem_limit_bytes=16 << 20),
    )(*pieces, *extra)


def after(value, earlier):
    return lax.optimization_barrier((value, earlier))[0]


def masked_update(update, v, drive, inside):
    wide = (
        jnp.roll(v, 1, axis=0) + jnp.roll(v, -1, axis=0)
    ) + (jnp.roll(v, 1, axis=1) + jnp.roll(v, -1, axis=1))
    return jnp.where(inside, update(v, wide, drive), 0.0)


def long_chain(own, drive):
    height = own.shape[0]
    half = height // 2
    groups, slices, rows = (lax.axis_size(a) for a in AXES)
    t, r = lax.axis_index("tm"), lax.axis_index("rows")
    core, chip = t % 2, t // 2
    first = core == 0
    away = outward(groups, rows)

    def cut(field, start, size):
        return lax.dynamic_slice_in_dim(field, start, size, axis=0)

    other = routed(own, partner)
    s_a, s_b = picked(first, own, other)
    edge = core * (height - WIDE)
    got = routed(jnp.concatenate([cut(f, edge, WIDE) for f in (s_a, s_b, drive)]), away)

    def sided(body, outer, inner):
        return jnp.where(
            first,
            jnp.concatenate([outer, body, inner]),
            jnp.concatenate([inner, body, outer]),
        )

    def window(field, place):
        body = cut(field, core * half, half)
        inner = cut(field, jnp.where(first, half, half - WIDE), WIDE)
        return sided(body, got[place * WIDE : (place + 1) * WIDE], inner)

    w_a, w_b, w_d = (window(f, i) for i, f in enumerate((s_a, s_b, drive)))
    row = lax.broadcasted_iota(jnp.int32, (half + 2 * WIDE, 1), 0)
    row = row + r * height + core * half - WIDE
    inside = (row >= 0) & (row < rows * height)
    w_a, w_b = jnp.where(inside, w_a, 0.0), jnp.where(inside, w_b, 0.0)

    def delta(v):
        fine = v
        for _ in range(FINE):
            fine = masked_update(fine_of, fine, w_d, inside)
        return fine - masked_update(coarse_of, v, w_d, inside)

    d_a, d_b = delta(w_a), delta(w_b)

    def both(v):
        e_a = masked_update(coarse_of, v, w_d, inside) + d_a
        return e_a, masked_update(coarse_of, e_a, w_d, inside) + d_b

    def extended(v):
        last = WIDE + half - 2
        inner = routed(cut(v, jnp.where(first, last, WIDE), 2), partner)
        outer = routed(cut(v, jnp.where(first, WIDE, last), 2), away)
        return sided(v[WIDE : WIDE + half], outer, inner)

    e_a, e_b = both(w_a)
    for stage in range(slices // 2 - 1):
        moved = e_b[WIDE - 2 : WIDE + half + 2] if stage == 0 else extended(e_b)
        arrived = routed(moved, stage_swap(stage))
        current = jnp.pad(arrived, ((WIDE - 2, WIDE - 2), (0, 0)))
        n_a, n_b = both(jnp.where(inside, current, 0.0))
        here = chip == stage + 1
        e_a, e_b = jnp.where(here, n_a, e_a), jnp.where(here, n_b, e_b)

    kept, sent = picked(first, e_a[WIDE : WIDE + half], e_b[WIDE : WIDE + half])
    back = routed(sent, partner)
    return jnp.concatenate(picked(first, kept, back))[None]


def on_device(starts, drive):
    own = starts[0]
    if lax.axis_size("tm") != 4:
        return long_chain(own, drive)
    return two_chips(starts, drive)


def two_chips(starts, drive):
    _, height, width = starts.shape
    half = height // 2
    groups, rows = lax.axis_size("groups"), lax.axis_size("rows")
    vmem = pl.BlockSpec(memory_space=pltpu.VMEM)

    other = routed(starts[0], partner)
    own, held, mine = pl.pallas_call(
        functools.partial(load_kernel, half),
        out_shape=[
            jax.ShapeDtypeStruct((size, width), jnp.float32) for size in (height, height, 48)
        ],
        in_specs=[pl.BlockSpec(memory_space=pltpu.HBM)] * 2,
        out_specs=[vmem] * 3,
        scratch_shapes=[pltpu.SemaphoreType.DMA((6,))],
        compiler_params=pltpu.CompilerParams(vmem_limit_bytes=51 << 20),
        cost_estimate=pl.CostEstimate(
            flops=60 * 24 * width, bytes_accessed=16 * height * width, transcendentals=0
        ),
        name="load",
    )(starts, drive)
    mid = width // 2
    packed = mid * 7 // 4
    sent_l, ends_l = compute(
        functools.partial(inner_kernel, half, 0), [(8, packed), (48, mid)], (own, other, held, mine)
    )
    here_l = routed(sent_l, stage_swap(0))
    sent_r, ends_r, edge = compute(
        functools.partial(inner_kernel, half, 1),
        [(8, packed), (48, mid), (8, width * 9 // 4)],
        (own, other, held, after(mine, sent_l)),
    )
    here_r = routed(sent_r, stage_swap(0))
    got = routed(edge, outward(groups, rows))
    sent_2, ends_2, delta_own = compute(
        functools.partial(middle_kernel, half),
        [(16, width), (48, width), (half + WIDE, width)],
        (own, other, after(held, sent_r)),
    )
    here_2 = routed(sent_2, stage_swap(0))
    (delta_other,) = compute(
        functools.partial(state_kernel, half), [(half + WIDE, width)], (other, after(held, sent_2))
    )
    keep_8, send_8, frame = compute(
        functools.partial(inner_end, half),
        [(8, width), (8, width), (16, width)],
        (here_l, here_r, held, delta_own, delta_other),
    )
    sent_3, ends_3 = compute(
        functools.partial(outer_kernel, half),
        [(8, width * 3 // 4), (32, width)],
        (own, other, after(held, frame), got),
    )
    here_3 = routed(sent_3, stage_swap(0))
    (state_3,) = compute(
        functools.partial(outer_state_kernel, half),
        [(3 * 24, width)],
        (own, other, after(held, sent_3), got, delta_own, delta_other),
    )
    keep_1, send_1 = compute(
        gather_kernel, [(half, width)] * 2, (ends_l, ends_r, ends_2, ends_3, keep_8, send_8)
    )
    back_1 = routed(send_1, partner)
    keep_2, send_2 = compute(
        functools.partial(middle_end, half),
        [(half - 16, width)] * 2,
        (frame, here_2, held, delta_own, after(delta_other, state_3)),
        scratch_shapes=[pltpu.VMEM((half, width), jnp.float32)],
    )
    back_2 = routed(send_2, partner)
    out = written(half, (keep_1, keep_2, back_1), starts.shape)
    out, state_3 = lax.optimization_barrier((out, state_3))
    keep_3, send_3 = compute(
        outer_end,
        [(8, width)] * 2,
        (here_2, here_3, state_3),
        scratch_shapes=[pltpu.VMEM((24, width), jnp.float32)],
    )
    back_3 = routed(send_3, partner)
    return written(half, (back_2, keep_3, back_3), starts.shape, into=out)


def solution(mesh):
    in_specs = (P(("groups", "tm"), "rows", None), P("rows", None))
    out_specs = P(("groups", "tm"), "rows", None)
    return jax.shard_map(
        on_device, mesh=mesh, in_specs=in_specs, out_specs=out_specs, check_vma=False
    )
```

```python
import functools

import jax
import jax.numpy as jnp
from jax import lax
from jax.experimental import pallas as pl
from jax.experimental.pallas import tpu as pltpu
from jax.sharding import PartitionSpec as P


FINE = 3
WIDE = 8
CUT = 4


diffusion = 2.0
step_fine = 0.1
coarse_step = FINE * step_fine
damping = 1.0 + 4.0 * diffusion * coarse_step

AXES = ("groups", "tm", "rows")


def routed(block, route):
    groups, slices, rows = (lax.axis_size(a) for a in AXES)
    pairs = []
    for g in range(groups):
        for t in range(slices):
            for r in range(rows):
                to_g, to_t, to_r = route(g, t, r)
                source = (g * slices + t) * rows + r
                pairs.append((source, (to_g * slices + to_t) * rows + to_r))
    return lax.ppermute(block, AXES, pairs)


def partner(g, t, r):
    return g, t ^ 1, r


def outward(groups, rows):
    def route(g, t, r):
        to_r = r + 1 if t & 1 else r - 1
        if 0 <= to_r < rows:
            return g, t ^ 1, to_r
        other = g ^ 1
        return (other, t, r) if other < groups else (g, t, r)

    return route


def stage_swap(stage):
    def route(g, t, r):
        chip = t // 2
        if chip == stage:
            return g, t + 2, r
        if chip == stage + 1:
            return g, t - 2, r
        return g, t, r

    return route


def around(v):
    height, width = v.shape
    return (pltpu.roll(v, 1, 0) + pltpu.roll(v, height - 1, 0)) + (
        pltpu.roll(v, 1, 1) + pltpu.roll(v, width - 1, 1)
    )


def fine_of(v, nsum, drive):
    return (
        step_fine * diffusion * nsum
        + v * ((1.0 + step_fine - 4.0 * step_fine * diffusion) - step_fine * (v * v))
        + step_fine * drive
    )


def coarse_of(v, nsum, drive):
    scale = coarse_step / damping
    return (
        scale * diffusion * nsum
        + v * ((1.0 + coarse_step) / damping - scale * (v * v))
        + scale * drive
    )


def compute(kernel, outs, args, **kwargs):
    shapes = [jax.ShapeDtypeStruct(o, jnp.float32) for o in outs]
    vmem = pl.BlockSpec(memory_space=pltpu.VMEM)
    return pl.pallas_call(
        kernel,
        out_shape=shapes,
        in_specs=[vmem] * len(args),
        out_specs=[vmem] * len(outs),
        compiler_params=pltpu.CompilerParams(vmem_limit_bytes=16 << 20),
        **kwargs,
    )(*args)


def same(v):
    return v


def start_of(v, drive, kept=same):
    nsum = around(v)
    coarse = kept(coarse_of(v, nsum, drive))
    fine = kept(fine_of(v, nsum, drive))
    for _ in range(FINE - 1):
        fine = kept(fine_of(fine, around(fine), drive))
    return fine, coarse


def ends_of(first, mine, theirs, drive, kept=same):
    f_a, f_b = picked(first, mine[0], theirs[0])
    g_a, g_b = picked(first, mine[1], theirs[1])
    e_a = g_a + (f_a - g_a)
    e_b = kept(coarse_of(e_a, around(e_a), drive)) + (f_b - g_b)
    return e_a, e_b


def chain(current, d_a, d_b, drive, kept=same):
    e_a = kept(coarse_of(current, around(current), drive)) + d_a
    e_b = kept(coarse_of(e_a, around(e_a), drive)) + d_b
    return e_a, e_b


def picked(first, own, other):
    return jnp.where(first, own, other), jnp.where(first, other, own)


def field(ref, kind, kinds, start, size):
    height = ref.shape[0] // kinds
    return ref.at[pl.ds(pl.multiple_of(kind * height + start, 8), size), :]


def mixed(upper, lower):
    row = lax.broadcasted_iota(jnp.int32, upper.shape, 0)
    return jnp.where(row < CUT, upper, lower)


def sublane(v):
    return lax.broadcasted_iota(jnp.int32, v.shape, 0)


def folded(v):
    width = v.shape[1]
    half, quarter = width // 2, width // 4
    four = mixed(v[:, :half], pltpu.roll(v[:, half:], 4, 0))
    row = sublane(four[:, :quarter])
    two = pltpu.roll(v[:, :quarter], 4, 0)
    for i, shift in ((1, 6), (2, 0), (3, 2)):
        part = v[:, i * quarter : (i + 1) * quarter]
        part = pltpu.roll(part, shift, 0) if shift else part
        two = jnp.where(row < 2 * i, two, part)
    return jnp.concatenate([four, two], axis=1)


def unfolded(v):
    half = v.shape[1] * 2 // 3
    four, two = v[:, :half], v[:, half:]
    low = [pltpu.roll(two, 4, 0), pltpu.roll(two, 2, 0), two, pltpu.roll(two, 6, 0)]
    return mixed(
        jnp.concatenate([four, pltpu.roll(four, 4, 0)], axis=1),
        jnp.concatenate(low, axis=1),
    )


def place():
    t = lax.axis_index("tm")
    return t % 2, t // 2


def at_edge(core):
    r, rows = lax.axis_index("rows"), lax.axis_size("rows")
    return ((core == 0) & (r == 0)) | ((core == 1) & (r == rows - 1))


def inner_row(half, core):
    return pl.multiple_of(half - 16 + 8 * core, 8)


def middle_row(half, core):
    return pl.multiple_of((half + 8) * core, 8)


def outer_row(half, core):
    return pl.multiple_of((2 * half - WIDE) * core, 8)


def load_kernel(half, starts, drive, own, held, inner, sems):
    core, chip = place()
    copies = []
    for i, (row, size) in enumerate(((half - 16, 32), (0, half - 16), (half + 16, half - 16))):
        rows = pl.ds(row, size)
        pair = (
            pltpu.make_async_copy(starts.at[0, rows, :], own.at[rows, :], sems.at[2 * i]),
            pltpu.make_async_copy(drive.at[rows, :], held.at[rows, :], sems.at[2 * i + 1]),
        )
        for copy in pair:
            copy.start()
        copies.append(pair)

    for copy in copies[0]:
        copy.wait()

    @pl.when(chip == 0)
    def _():
        rows = pl.ds(inner_row(half, core), 24)
        fine, coarse = start_of(own[rows, :], held[rows, :])
        inner[0:24, :] = fine
        inner[24:48, :] = coarse

    for copy in (*copies[1], *copies[2]):
        copy.wait()


def inner_kernel(half, side, own, other, drive, mine, sent, ends, edge=None):
    core, chip = place()
    first = core == 0
    width = drive.shape[1]
    mid = width // 2

    def columns(ref, rows):
        if side == 0:
            parts = ref[rows, width - 128 :], ref[rows, : mid + 128]
        else:
            parts = ref[rows, mid - 128 :], ref[rows, :128]
        return jnp.concatenate(parts, axis=1)

    @pl.when(chip == 0)
    def _():
        rows = pl.ds(inner_row(half, core), 24)
        d = columns(drive, rows)
        theirs = start_of(columns(other, rows), d)
        known = columns(mine, pl.ds(0, 24)), columns(mine, pl.ds(24, 24))
        e_a, e_b = ends_of(first, known, theirs, d)
        e_a, e_b = e_a[:, 128:-128], e_b[:, 128:-128]
        frame = pltpu.roll(e_b, 24 - CUT, 0)
        whole, part = picked(first, frame[:8], frame[8:16])
        part = jnp.where(first, part, pltpu.roll(part, 6, 0))
        sent[...] = jnp.concatenate([whole, folded(part)], axis=1)
        ends[0:24, :] = e_a
        ends[24:48, :] = e_b

    if edge is not None:
        rows = pl.ds(outer_row(half, core), 8)
        a, b = picked(first, own[rows, :], other[rows, :])
        fields = (jnp.where(first, v, pltpu.roll(v, 6, 0)) for v in (a, b, drive[rows, :]))
        edge[...] = jnp.concatenate([folded(v) for v in fields], axis=1)


def middle_kernel(half, own, other, drive, sent, ends, delta):
    core, chip = place()
    first = core == 0

    @pl.when(chip == 0)
    def _():
        rows = pl.ds(middle_row(half, core), 24)
        d = drive[rows, :]
        mine, theirs = start_of(own[rows, :], d), start_of(other[rows, :], d)
        e_a, e_b = ends_of(first, mine, theirs, d)
        sent[...] = pltpu.roll(e_b, 24 - CUT, 0)[:16]
        ends[0:24, :] = e_a
        ends[24:48, :] = e_b

    @pl.when(chip > 0)
    def _():
        rows = receiver_rows(half, core)
        fine, coarse = start_of(own[rows, :], drive[rows, :])
        delta[...] = fine - coarse


def receiver_rows(half, core):
    return pl.ds(pl.multiple_of((half - WIDE) * core, 8), half + WIDE)


def state_kernel(half, other, drive, theirs):
    core, chip = place()

    @pl.when(chip > 0)
    def _():
        rows = receiver_rows(half, core)
        fine, coarse = start_of(other[rows, :], drive[rows, :])
        theirs[...] = fine - coarse


def outer_window(half, own, other, drive, got):
    core, _ = place()
    first = core == 0
    rows = pl.ds(outer_row(half, core), 8)
    a, b = picked(first, own[rows, :], other[rows, :])
    near = (a, b, drive[rows, :])
    size = got.shape[1] // 3
    far = [unfolded(got[:, i * size : (i + 1) * size]) for i in range(3)]
    far = [jnp.where(first, pltpu.roll(v, 2, 0), v) for v in far]
    upper = [jnp.where(first, f, n) for f, n in zip(far, near)]
    lower = [jnp.where(first, n, f) for f, n in zip(far, near)]
    a, b, d = (jnp.concatenate(p) for p in zip(upper, lower))
    inside = ~(at_edge(core) & (sublane(a) // 8 == core))

    def kept(v):
        return jnp.where(inside, v, 0.0)

    return kept(a), kept(b), d, kept


def outer_kernel(half, own, other, drive, got, mine, theirs, sent, ends, state):
    core, chip = place()
    first = core == 0
    a, b, d, kept = outer_window(half, own, other, drive, got)
    (f_a, g_a), (f_b, g_b) = start_of(a, d, kept), start_of(b, d, kept)

    @pl.when(chip == 0)
    def _():
        e_a = g_a + (f_a - g_a)
        e_b = kept(coarse_of(e_a, around(e_a), d)) + (f_b - g_b)
        frame = pltpu.roll(e_b, 16 - CUT, 0)[:8]
        sent[...] = folded(jnp.where(first, pltpu.roll(frame, 6, 0), frame))
        ends[0:16, :] = e_a
        ends[16:32, :] = e_b

    @pl.when(chip > 0)
    def _():
        rows = pl.ds(pl.multiple_of((half - WIDE) * core, 8), 16)
        before = picked(first, mine[rows, :], theirs[rows, :])
        d_rows = pl.ds(pl.multiple_of((2 * half - 16) * core, 8), 16)
        fields = zip((f_a - g_a, f_b - g_b, d), (*before, drive[d_rows, :]))
        for kind, (v, near) in enumerate(fields):
            top = jnp.where(first, v[:8], near[:8])
            mid = jnp.where(first, mixed(v[8:], near[:8]), mixed(near[8:], v[:8]))
            low = jnp.where(first, near[8:], v[8:])
            state[24 * kind : 24 * kind + 24, :] = jnp.concatenate([top, mid, low])


def inner_end(half, left, right, drive, mine, theirs, keep, send, frame):
    core, chip = place()
    first = core == 0

    @pl.when(chip > 0)
    def _():
        mid = left.shape[1] * 4 // 7
        parts = left[...], right[...]
        whole = jnp.concatenate([p[:, :mid] for p in parts], axis=1)
        part = jnp.concatenate([unfolded(p[:, mid:]) for p in parts], axis=1)
        part = jnp.where(first, part, pltpu.roll(part, 2, 0))
        top, low = picked(first, whole, part)
        frame[0:8, :] = top
        frame[8:16, :] = low
        current = pltpu.roll(jnp.concatenate([top, low, low]), CUT, 0)
        rows = pl.ds(pl.multiple_of((half - 16) * (1 - core), 8), 24)
        d_a, d_b = picked(first, mine[rows, :], theirs[rows, :])
        d = drive[pl.ds(inner_row(half, core), 24), :]
        e_a, e_b = chain(current, d_a, d_b, d)
        put_ends(first, e_a[8:16], e_b[8:16], keep, send)


def gather_kernel(ends_left, ends_right, middle, outer, keep_8, send_8, keep, send):
    core, chip = place()
    first = core == 0

    @pl.when(chip == 0)
    def _():
        def rows(kind, tile):
            into = pl.ds(24 * kind + 8 * tile, 8)
            return jnp.concatenate([ends_left[into, :], ends_right[into, :]], axis=1)

        def known(kind):
            lower = [rows(kind, i) for i in range(3)]
            upper = [field(middle, kind, 2, 8 * i, 8)[...] for i in range(3)]
            last = [field(outer, kind, 2, 8 * i, 8)[...] for i in range(2)]
            return jnp.concatenate(
                [
                    lower[1],
                    jnp.where(first, upper[1], mixed(lower[2], upper[0])),
                    jnp.where(first, mixed(upper[2], lower[0]), upper[1]),
                    jnp.where(first, mixed(last[1], upper[0]), mixed(upper[2], last[0])),
                ]
            )

        put_ends(first, known(0), known(1), keep, send)

    @pl.when(chip > 0)
    def _():
        keep[0:8, :] = keep_8[...]
        send[0:8, :] = send_8[...]


def put_ends(first, e_a, e_b, keep, send):
    kept, sent = picked(first, e_a, e_b)
    keep[...] = kept
    send[...] = sent


def middle_end(half, inner, middle, drive, mine, theirs, keep, send, current):
    core, chip = place()
    first = core == 0

    @pl.when((chip > 0) & first)
    def _():
        current[...] = pltpu.roll(jnp.concatenate([middle[...], inner[...]]), CUT, 0)

    @pl.when((chip > 0) & (core == 1))
    def _():
        current[...] = pltpu.roll(jnp.concatenate([inner[...], middle[...]]), half - CUT, 0)

    @pl.when(chip > 0)
    def _():
        rows = pl.ds(pl.multiple_of(8 * core, 8), half)
        d_a, d_b = picked(first, mine[rows, :], theirs[rows, :])
        d = drive[pl.ds(pl.multiple_of(half * core, 8), half), :]
        e_a, e_b = chain(current[...], d_a, d_b, d)
        put_ends(first, e_a[8 : half - 8], e_b[8 : half - 8], keep, send)


def outer_end(middle, outer, state, keep, send, current):
    core, chip = place()
    first = core == 0

    @pl.when((chip > 0) & first)
    def _():
        part = pltpu.roll(unfolded(outer[...]), 2, 0)
        current[...] = pltpu.roll(jnp.concatenate([part, middle[...]]), CUT, 0)

    @pl.when((chip > 0) & (core == 1))
    def _():
        part = unfolded(outer[...])
        current[...] = pltpu.roll(jnp.concatenate([middle[...], part]), 24 - CUT, 0)

    @pl.when(chip > 0)
    def _():
        d_a, d_b, d = (field(state, kind, 3, 0, 24)[...] for kind in range(3))
        tile = lax.broadcasted_iota(jnp.int32, d.shape, 0) // 8
        inside = ~(at_edge(core) & (tile == 2 * core))
        e_a = coarse_of(current[...], around(current[...]), d) + d_a
        e_a = jnp.where(inside, e_a, 0.0)
        e_b = coarse_of(e_a, around(e_a), d) + d_b
        put_ends(first, e_a[8:16], e_b[8:16], keep, send)


def write_kernel(half, last, *refs):
    pieces, out, sems = refs[: 1 if last else 5], refs[-2], refs[-1]
    core, chip = place()

    def copy_all(order):
        copies = []
        for i, (mine, part, source, begin, size) in enumerate(order):
            upper = (half - 8, 8, 0)[part]
            lower = (half, half + 8, 2 * half - 8)[part]
            row = pl.multiple_of(jnp.where((core == 0) == mine, upper, lower), 8)
            copy = pltpu.make_async_copy(
                pieces[source].at[pl.ds(begin, size), :],
                out.at[0, pl.ds(row, size), :],
                sems.at[i],
            )
            copy.start()
            copies.append(copy)
        for copy in copies:
            copy.wait()

    if last:

        @pl.when(chip > 0)
        def _():
            copy_all(((False, 2, 0, 0, 8),))

    else:
        rest = half - 16

        @pl.when(chip == 0)
        def _():
            parts = ((0, 0, 8), (1, 8, rest), (2, half - 8, 8))
            copy_all(
                [(mine, part, source, *rows) for mine, source in ((True, 0), (False, 1)) for part, *rows in parts]
            )

        @pl.when(chip > 0)
        def _():
            copy_all(
                (
                    (True, 0, 0, 0, 8),
                    (False, 0, 1, 0, 8),
                    (True, 1, 2, 0, rest),
                    (False, 1, 3, 0, rest),
                    (True, 2, 4, 0, 8),
                )
            )


def written(half, pieces, shape, into=None):
    vmem, anywhere = pl.BlockSpec(memory_space=pltpu.VMEM), pl.BlockSpec(memory_space=pl.ANY)
    extra = () if into is None else (into,)
    return pl.pallas_call(
        functools.partial(write_kernel, half, into is not None),
        out_shape=jax.ShapeDtypeStruct(shape, jnp.float32),
        in_specs=[vmem] * len(pieces) + [anywhere] * len(extra),
        out_specs=anywhere,
        input_output_aliases={len(pieces): 0} if extra else {},
        scratch_shapes=[pltpu.SemaphoreType.DMA((6,))],
        compiler_params=pltpu.CompilerParams(vmem_limit_bytes=16 << 20),
    )(*pieces, *extra)


def after(value, earlier):
    return lax.optimization_barrier((value, earlier))[0]


def masked_update(update, v, drive, inside):
    wide = (
        jnp.roll(v, 1, axis=0) + jnp.roll(v, -1, axis=0)
    ) + (jnp.roll(v, 1, axis=1) + jnp.roll(v, -1, axis=1))
    return jnp.where(inside, update(v, wide, drive), 0.0)


def long_chain(own, drive):
    height = own.shape[0]
    half = height // 2
    groups, slices, rows = (lax.axis_size(a) for a in AXES)
    t, r = lax.axis_index("tm"), lax.axis_index("rows")
    core, chip = t % 2, t // 2
    first = core == 0
    away = outward(groups, rows)

    def cut(field, start, size):
        return lax.dynamic_slice_in_dim(field, start, size, axis=0)

    other = routed(own, partner)
    s_a, s_b = picked(first, own, other)
    edge = core * (height - WIDE)
    got = routed(jnp.concatenate([cut(f, edge, WIDE) for f in (s_a, s_b, drive)]), away)

    def sided(body, outer, inner):
        return jnp.where(
            first,
            jnp.concatenate([outer, body, inner]),
            jnp.concatenate([inner, body, outer]),
        )

    def window(field, place):
        body = cut(field, core * half, half)
        inner = cut(field, jnp.where(first, half, half - WIDE), WIDE)
        return sided(body, got[place * WIDE : (place + 1) * WIDE], inner)

    w_a, w_b, w_d = (window(f, i) for i, f in enumerate((s_a, s_b, drive)))
    row = lax.broadcasted_iota(jnp.int32, (half + 2 * WIDE, 1), 0)
    row = row + r * height + core * half - WIDE
    inside = (row >= 0) & (row < rows * height)
    w_a, w_b = jnp.where(inside, w_a, 0.0), jnp.where(inside, w_b, 0.0)

    def delta(v):
        fine = v
        for _ in range(FINE):
            fine = masked_update(fine_of, fine, w_d, inside)
        return fine - masked_update(coarse_of, v, w_d, inside)

    d_a, d_b = delta(w_a), delta(w_b)

    def both(v):
        e_a = masked_update(coarse_of, v, w_d, inside) + d_a
        return e_a, masked_update(coarse_of, e_a, w_d, inside) + d_b

    def extended(v):
        last = WIDE + half - 2
        inner = routed(cut(v, jnp.where(first, last, WIDE), 2), partner)
        outer = routed(cut(v, jnp.where(first, WIDE, last), 2), away)
        return sided(v[WIDE : WIDE + half], outer, inner)

    e_a, e_b = both(w_a)
    for stage in range(slices // 2 - 1):
        moved = e_b[WIDE - 2 : WIDE + half + 2] if stage == 0 else extended(e_b)
        arrived = routed(moved, stage_swap(stage))
        current = jnp.pad(arrived, ((WIDE - 2, WIDE - 2), (0, 0)))
        n_a, n_b = both(jnp.where(inside, current, 0.0))
        here = chip == stage + 1
        e_a, e_b = jnp.where(here, n_a, e_a), jnp.where(here, n_b, e_b)

    kept, sent = picked(first, e_a[WIDE : WIDE + half], e_b[WIDE : WIDE + half])
    back = routed(sent, partner)
    return jnp.concatenate(picked(first, kept, back))[None]


def on_device(starts, drive):
    own = starts[0]
    if lax.axis_size("tm") != 4:
        return long_chain(own, drive)
    return two_chips(starts, drive)


def two_chips(starts, drive):
    _, height, width = starts.shape
    half = height // 2
    groups, rows = lax.axis_size("groups"), lax.axis_size("rows")
    vmem = pl.BlockSpec(memory_space=pltpu.VMEM)

    other = routed(starts[0], partner)
    own, held, mine = pl.pallas_call(
        functools.partial(load_kernel, half),
        out_shape=[
            jax.ShapeDtypeStruct((size, width), jnp.float32) for size in (height, height, 48)
        ],
        in_specs=[pl.BlockSpec(memory_space=pltpu.HBM)] * 2,
        out_specs=[vmem] * 3,
        scratch_shapes=[pltpu.SemaphoreType.DMA((6,))],
        compiler_params=pltpu.CompilerParams(vmem_limit_bytes=51 << 20),
        cost_estimate=pl.CostEstimate(
            flops=60 * 24 * width, bytes_accessed=16 * height * width, transcendentals=0
        ),
        name="load",
    )(starts, drive)
    mid = width // 2
    packed = mid * 7 // 4
    sent_l, ends_l = compute(
        functools.partial(inner_kernel, half, 0), [(8, packed), (48, mid)], (own, other, held, mine)
    )
    here_l = routed(sent_l, stage_swap(0))
    sent_r, ends_r, edge = compute(
        functools.partial(inner_kernel, half, 1),
        [(8, packed), (48, mid), (8, width * 9 // 4)],
        (own, other, held, after(mine, sent_l)),
    )
    here_r = routed(sent_r, stage_swap(0))
    got = routed(edge, outward(groups, rows))
    sent_2, ends_2, delta_own = compute(
        functools.partial(middle_kernel, half),
        [(16, width), (48, width), (half + WIDE, width)],
        (own, other, after(held, sent_r)),
    )
    here_2 = routed(sent_2, stage_swap(0))
    (delta_other,) = compute(
        functools.partial(state_kernel, half), [(half + WIDE, width)], (other, after(held, sent_2))
    )
    keep_8, send_8, frame = compute(
        functools.partial(inner_end, half),
        [(8, width), (8, width), (16, width)],
        (here_l, here_r, held, delta_own, delta_other),
    )
    sent_3, ends_3, state_3 = compute(
        functools.partial(outer_kernel, half),
        [(8, width * 3 // 4), (32, width), (3 * 24, width)],
        (own, other, after(held, frame), got, delta_own, delta_other),
    )
    here_3 = routed(sent_3, stage_swap(0))
    keep_1, send_1 = compute(
        gather_kernel, [(half, width)] * 2, (ends_l, ends_r, ends_2, ends_3, keep_8, send_8)
    )
    back_1 = routed(send_1, partner)
    keep_2, send_2 = compute(
        functools.partial(middle_end, half),
        [(half - 16, width)] * 2,
        (frame, here_2, held, delta_own, after(delta_other, state_3)),
        scratch_shapes=[pltpu.VMEM((half, width), jnp.float32)],
    )
    back_2 = routed(send_2, partner)
    keep_3, send_3 = compute(
        outer_end,
        [(8, width)] * 2,
        (here_2, here_3, after(state_3, keep_2)),
        scratch_shapes=[pltpu.VMEM((24, width), jnp.float32)],
    )
    back_3 = routed(send_3, partner)
    out = written(half, (keep_1, back_1, keep_2, back_2, keep_3), starts.shape)
    return written(half, (back_3,), starts.shape, into=out)


def solution(mesh):
    in_specs = (P(("groups", "tm"), "rows", None), P("rows", None))
    out_specs = P(("groups", "tm"), "rows", None)
    return jax.shard_map(
        on_device, mesh=mesh, in_specs=in_specs, out_specs=out_specs, check_vma=False
    )
```

```python
import functools

import jax
import jax.numpy as jnp
from jax import lax
from jax.experimental import pallas as pl
from jax.experimental.pallas import tpu as pltpu
from jax.sharding import PartitionSpec as P


FINE = 3
WIDE = 8
CUT = 4


diffusion = 2.0
step_fine = 0.1
coarse_step = FINE * step_fine
damping = 1.0 + 4.0 * diffusion * coarse_step

AXES = ("groups", "tm", "rows")


def routed(block, route):
    groups, slices, rows = (lax.axis_size(a) for a in AXES)
    pairs = []
    for g in range(groups):
        for t in range(slices):
            for r in range(rows):
                to_g, to_t, to_r = route(g, t, r)
                source = (g * slices + t) * rows + r
                pairs.append((source, (to_g * slices + to_t) * rows + to_r))
    return lax.ppermute(block, AXES, pairs)


def partner(g, t, r):
    return g, t ^ 1, r


def outward(groups, rows):
    def route(g, t, r):
        to_r = r + 1 if t & 1 else r - 1
        if 0 <= to_r < rows:
            return g, t ^ 1, to_r
        other = g ^ 1
        return (other, t, r) if other < groups else (g, t, r)

    return route


def stage_swap(stage):
    def route(g, t, r):
        chip = t // 2
        if chip == stage:
            return g, t + 2, r
        if chip == stage + 1:
            return g, t - 2, r
        return g, t, r

    return route


def around(v):
    height, width = v.shape
    return (pltpu.roll(v, 1, 0) + pltpu.roll(v, height - 1, 0)) + (
        pltpu.roll(v, 1, 1) + pltpu.roll(v, width - 1, 1)
    )


def fine_of(v, nsum, drive):
    return (
        step_fine * diffusion * nsum
        + v * ((1.0 + step_fine - 4.0 * step_fine * diffusion) - step_fine * (v * v))
        + step_fine * drive
    )


def coarse_of(v, nsum, drive):
    scale = coarse_step / damping
    return (
        scale * diffusion * nsum
        + v * ((1.0 + coarse_step) / damping - scale * (v * v))
        + scale * drive
    )


def compute(kernel, outs, args, **kwargs):
    shapes = [jax.ShapeDtypeStruct(o, jnp.float32) for o in outs]
    vmem = pl.BlockSpec(memory_space=pltpu.VMEM)
    return pl.pallas_call(
        kernel,
        out_shape=shapes,
        in_specs=[vmem] * len(args),
        out_specs=[vmem] * len(outs),
        compiler_params=pltpu.CompilerParams(vmem_limit_bytes=16 << 20),
        **kwargs,
    )(*args)


def same(v):
    return v


def start_of(v, drive, kept=same):
    nsum = around(v)
    coarse = kept(coarse_of(v, nsum, drive))
    fine = kept(fine_of(v, nsum, drive))
    for _ in range(FINE - 1):
        fine = kept(fine_of(fine, around(fine), drive))
    return fine, coarse


def ends_of(first, mine, theirs, drive, kept=same):
    f_a, f_b = picked(first, mine[0], theirs[0])
    g_a, g_b = picked(first, mine[1], theirs[1])
    e_a = g_a + (f_a - g_a)
    e_b = kept(coarse_of(e_a, around(e_a), drive)) + (f_b - g_b)
    return e_a, e_b


def chain(current, d_a, d_b, drive, kept=same):
    e_a = kept(coarse_of(current, around(current), drive)) + d_a
    e_b = kept(coarse_of(e_a, around(e_a), drive)) + d_b
    return e_a, e_b


def picked(first, own, other):
    return jnp.where(first, own, other), jnp.where(first, other, own)


def field(ref, kind, kinds, start, size):
    height = ref.shape[0] // kinds
    return ref.at[pl.ds(pl.multiple_of(kind * height + start, 8), size), :]


def mixed(upper, lower):
    row = lax.broadcasted_iota(jnp.int32, upper.shape, 0)
    return jnp.where(row < CUT, upper, lower)


def sublane(v):
    return lax.broadcasted_iota(jnp.int32, v.shape, 0)


def folded(v):
    width = v.shape[1]
    half, quarter = width // 2, width // 4
    four = mixed(v[:, :half], pltpu.roll(v[:, half:], 4, 0))
    row = sublane(four[:, :quarter])
    two = pltpu.roll(v[:, :quarter], 4, 0)
    for i, shift in ((1, 6), (2, 0), (3, 2)):
        part = v[:, i * quarter : (i + 1) * quarter]
        part = pltpu.roll(part, shift, 0) if shift else part
        two = jnp.where(row < 2 * i, two, part)
    return jnp.concatenate([four, two], axis=1)


def unfolded(v):
    half = v.shape[1] * 2 // 3
    four, two = v[:, :half], v[:, half:]
    low = [pltpu.roll(two, 4, 0), pltpu.roll(two, 2, 0), two, pltpu.roll(two, 6, 0)]
    return mixed(
        jnp.concatenate([four, pltpu.roll(four, 4, 0)], axis=1),
        jnp.concatenate(low, axis=1),
    )


def place():
    t = lax.axis_index("tm")
    return t % 2, t // 2


def at_edge(core):
    r, rows = lax.axis_index("rows"), lax.axis_size("rows")
    return ((core == 0) & (r == 0)) | ((core == 1) & (r == rows - 1))


def inner_row(half, core):
    return pl.multiple_of(8 + (half - 16) * core, 8)


def middle_row(half, core):
    return pl.multiple_of((2 * half - 16) * core, 8)


def outer_row(half, core):
    return pl.multiple_of((2 * half - WIDE) * core, 8)


def load_kernel(half, starts, drive, own, held, inner, sems):
    core, chip = place()
    copies = []
    for i, (row, size) in enumerate(((8, 2 * half - 16), (0, 8), (2 * half - 8, 8))):
        rows = pl.ds(row, size)
        pair = (
            pltpu.make_async_copy(starts.at[0, rows, :], own.at[rows, :], sems.at[2 * i]),
            pltpu.make_async_copy(drive.at[rows, :], held.at[rows, :], sems.at[2 * i + 1]),
        )
        for copy in pair:
            copy.start()
        copies.append(pair)

    for copy in copies[0]:
        copy.wait()

    @pl.when(chip == 0)
    def _():
        rows = pl.ds(inner_row(half, core), half)
        fine, coarse = start_of(own[rows, :], held[rows, :])
        inner[0:half, :] = fine
        inner[half : 2 * half, :] = coarse

    for copy in (*copies[1], *copies[2]):
        copy.wait()


def inner_kernel(half, side, own, other, drive, mine, sent, ends, edge=None):
    core, chip = place()
    first = core == 0
    width = drive.shape[1]
    mid = width // 2

    def columns(ref, rows):
        if side == 0:
            parts = ref[rows, width - 128 :], ref[rows, : mid + 128]
        else:
            parts = ref[rows, mid - 128 :], ref[rows, :128]
        return jnp.concatenate(parts, axis=1)

    @pl.when(chip == 0)
    def _():
        rows = pl.ds(inner_row(half, core), half)
        d = columns(drive, rows)
        theirs = start_of(columns(other, rows), d)
        known = columns(mine, pl.ds(0, half)), columns(mine, pl.ds(half, half))
        e_a, e_b = ends_of(first, known, theirs, d)
        e_a, e_b = e_a[:, 128:-128], e_b[:, 128:-128]
        frame = pltpu.roll(e_b, half - CUT, 0)
        count = half // 8 - 2
        whole = [
            jnp.where(first, frame[8 * i : 8 * i + 8], frame[8 * i + 8 : 8 * i + 16])
            for i in range(count)
        ]
        part = jnp.where(
            first, frame[8 * count : 8 * count + 8], pltpu.roll(frame[:8], 6, 0)
        )
        sent[...] = jnp.concatenate([*whole, folded(part)], axis=1)
        ends[0:half, :] = e_a
        ends[half : 2 * half, :] = e_b

    if edge is not None:
        rows = pl.ds(outer_row(half, core), 8)
        a, b = picked(first, own[rows, :], other[rows, :])
        fields = (jnp.where(first, v, pltpu.roll(v, 6, 0)) for v in (a, b, drive[rows, :]))
        edge[...] = jnp.concatenate([folded(v) for v in fields], axis=1)


def middle_kernel(half, own, other, drive, sent, ends, delta):
    core, chip = place()
    first = core == 0

    @pl.when(chip == 0)
    def _():
        rows = pl.ds(middle_row(half, core), 16)
        d = drive[rows, :]
        mine, theirs = start_of(own[rows, :], d), start_of(other[rows, :], d)
        e_a, e_b = ends_of(first, mine, theirs, d)
        sent[...] = pltpu.roll(e_b, 16 - CUT, 0)[:8]
        ends[0:16, :] = e_a
        ends[16:32, :] = e_b

    @pl.when(chip > 0)
    def _():
        rows = receiver_rows(half, core)
        fine, coarse = start_of(own[rows, :], drive[rows, :])
        delta[...] = fine - coarse


def receiver_rows(half, core):
    return pl.ds(pl.multiple_of((half - WIDE) * core, 8), half + WIDE)


def state_kernel(half, other, drive, theirs):
    core, chip = place()

    @pl.when(chip > 0)
    def _():
        rows = receiver_rows(half, core)
        fine, coarse = start_of(other[rows, :], drive[rows, :])
        theirs[...] = fine - coarse


def outer_window(half, own, other, drive, got):
    core, _ = place()
    first = core == 0
    rows = pl.ds(outer_row(half, core), 8)
    a, b = picked(first, own[rows, :], other[rows, :])
    near = (a, b, drive[rows, :])
    size = got.shape[1] // 3
    far = [unfolded(got[:, i * size : (i + 1) * size]) for i in range(3)]
    far = [jnp.where(first, pltpu.roll(v, 2, 0), v) for v in far]
    upper = [jnp.where(first, f, n) for f, n in zip(far, near)]
    lower = [jnp.where(first, n, f) for f, n in zip(far, near)]
    a, b, d = (jnp.concatenate(p) for p in zip(upper, lower))
    inside = ~(at_edge(core) & (sublane(a) // 8 == core))

    def kept(v):
        return jnp.where(inside, v, 0.0)

    return kept(a), kept(b), d, kept


def outer_kernel(half, own, other, drive, got, mine, theirs, sent, ends, state):
    core, chip = place()
    first = core == 0
    a, b, d, kept = outer_window(half, own, other, drive, got)
    (f_a, g_a), (f_b, g_b) = start_of(a, d, kept), start_of(b, d, kept)

    @pl.when(chip == 0)
    def _():
        e_a = g_a + (f_a - g_a)
        e_b = kept(coarse_of(e_a, around(e_a), d)) + (f_b - g_b)
        frame = pltpu.roll(e_b, 16 - CUT, 0)[:8]
        sent[...] = folded(jnp.where(first, pltpu.roll(frame, 6, 0), frame))
        ends[0:16, :] = e_a
        ends[16:32, :] = e_b

    @pl.when(chip > 0)
    def _():
        rows = pl.ds(pl.multiple_of((half - WIDE) * core, 8), 16)
        before = picked(first, mine[rows, :], theirs[rows, :])
        d_rows = pl.ds(pl.multiple_of((2 * half - 16) * core, 8), 16)
        fields = zip((f_a - g_a, f_b - g_b, d), (*before, drive[d_rows, :]))
        for kind, (v, near) in enumerate(fields):
            top = jnp.where(first, v[:8], near[:8])
            mid = jnp.where(first, mixed(v[8:], near[:8]), mixed(near[8:], v[:8]))
            low = jnp.where(first, near[8:], v[8:])
            state[24 * kind : 24 * kind + 24, :] = jnp.concatenate([top, mid, low])


def inner_end(half, left, right, drive, mine, theirs, keep, send, frame):
    core, chip = place()
    first = core == 0

    @pl.when(chip > 0)
    def _():
        count = half // 8 - 2
        mid = left.shape[1] * 4 // (4 * count + 3)
        parts = left[...], right[...]

        def across(begin, end, change=same):
            return jnp.concatenate([change(p[:, begin:end]) for p in parts], axis=1)

        whole = [across(i * mid, i * mid + mid) for i in range(count)]
        part = across(count * mid, left.shape[1], unfolded)
        upper = [*whole, part]
        lower = [pltpu.roll(part, 2, 0), *whole]
        rows = jnp.concatenate([jnp.where(first, u, v) for u, v in zip(upper, lower)])
        frame[...] = rows
        current = pltpu.roll(jnp.concatenate([rows, rows[:8]]), CUT, 0)
        into = pl.ds(pl.multiple_of(8 * (1 - core), 8), half)
        d_a, d_b = picked(first, mine[into, :], theirs[into, :])
        d = drive[pl.ds(inner_row(half, core), half), :]
        e_a, e_b = chain(current, d_a, d_b, d)
        put_ends(first, e_a[8 : half - 8], e_b[8 : half - 8], keep, send)


def gather_kernel(half, ends_left, ends_right, middle, outer, near_keep, near_send, keep, send):
    core, chip = place()
    first = core == 0
    near = half - 16

    @pl.when(chip == 0)
    def _():
        def rows(kind, begin, size):
            into = pl.ds(half * kind + begin, size)
            return jnp.concatenate([ends_left[into, :], ends_right[into, :]], axis=1)

        def known(kind):
            two = [field(middle, kind, 2, 8 * i, 8)[...] for i in range(2)]
            last = [field(outer, kind, 2, 8 * i, 8)[...] for i in range(2)]
            beside = [rows(kind, 0, 8), rows(kind, half - 8, 8)]
            return jnp.concatenate(
                [
                    rows(kind, 8, near),
                    jnp.where(first, mixed(two[1], beside[0]), mixed(beside[1], two[0])),
                    jnp.where(first, mixed(last[1], two[0]), mixed(two[1], last[0])),
                ]
            )

        put_ends(first, known(0), known(1), keep, send)

    @pl.when(chip > 0)
    def _():
        keep[0:near, :] = near_keep[...]
        send[0:near, :] = near_send[...]


def put_ends(first, e_a, e_b, keep, send):
    kept, sent = picked(first, e_a, e_b)
    keep[...] = kept
    send[...] = sent


def middle_end(half, inner, middle, drive, mine, theirs, keep, send, current):
    core, chip = place()
    first = core == 0
    last = inner.shape[0] - 16

    @pl.when((chip > 0) & first)
    def _():
        current[...] = pltpu.roll(jnp.concatenate([middle[...], inner[0:16, :]]), CUT, 0)

    @pl.when((chip > 0) & (core == 1))
    def _():
        rows = jnp.concatenate([inner[last : last + 16, :], middle[...]])
        current[...] = pltpu.roll(rows, 24 - CUT, 0)

    @pl.when(chip > 0)
    def _():
        rows = pl.ds(pl.multiple_of((half - 16) * core, 8), 24)
        d_a, d_b = picked(first, mine[rows, :], theirs[rows, :])
        d = drive[pl.ds(pl.multiple_of((2 * half - 24) * core, 8), 24), :]
        e_a, e_b = chain(current[...], d_a, d_b, d)
        put_ends(first, e_a[8:16], e_b[8:16], keep, send)


def outer_end(inner, middle, outer, state, keep, send, current):
    core, chip = place()
    first = core == 0
    last = inner.shape[0] - 8

    @pl.when((chip > 0) & first)
    def _():
        part = pltpu.roll(unfolded(outer[...]), 2, 0)
        rows = jnp.concatenate([part, middle[...], inner[0:8, :]])
        current[...] = pltpu.roll(rows, CUT, 0)

    @pl.when((chip > 0) & (core == 1))
    def _():
        rows = jnp.concatenate([inner[last : last + 8, :], middle[...], unfolded(outer[...])])
        current[...] = pltpu.roll(rows, 24 - CUT, 0)

    @pl.when(chip > 0)
    def _():
        d_a, d_b, d = (field(state, kind, 3, 0, 24)[...] for kind in range(3))
        inside = ~(at_edge(core) & (sublane(d) // 8 == 2 * core))
        e_a = coarse_of(current[...], around(current[...]), d) + d_a
        e_a = jnp.where(inside, e_a, 0.0)
        mid = e_a[8:16]
        width = mid.shape[1]
        beside = pltpu.roll(mid, 1, 1) + pltpu.roll(mid, width - 1, 1)
        upright = pltpu.roll(e_a, 1, 0)[8:16] + pltpu.roll(e_a, 23, 0)[8:16]
        e_b = coarse_of(mid, upright + beside, d[8:16]) + d_b[8:16]
        put_ends(first, mid, e_b, keep, send)


def write_kernel(half, last, *refs):
    pieces, out, sems = refs[: 1 if last else 5], refs[-2], refs[-1]
    core, chip = place()

    def copy_all(order):
        copies = []
        for i, (mine, part, source, begin, size) in enumerate(order):
            upper = (16, 8, 0)[part]
            lower = (half, 2 * half - 16, 2 * half - 8)[part]
            row = pl.multiple_of(jnp.where((core == 0) == mine, upper, lower), 8)
            copy = pltpu.make_async_copy(
                pieces[source].at[pl.ds(begin, size), :],
                out.at[0, pl.ds(row, size), :],
                sems.at[i],
            )
            copy.start()
            copies.append(copy)
        for copy in copies:
            copy.wait()

    if last:

        @pl.when(chip > 0)
        def _():
            copy_all(((False, 2, 0, 0, 8),))

    else:
        near = half - 16

        @pl.when(chip == 0)
        def _():
            parts = ((0, 0, near), (1, near, 8), (2, near + 8, 8))
            copy_all(
                [(mine, part, source, *rows) for mine, source in ((True, 0), (False, 1)) for part, *rows in parts]
            )

        @pl.when(chip > 0)
        def _():
            copy_all(
                (
                    (True, 0, 0, 0, near),
                    (False, 0, 1, 0, near),
                    (True, 1, 2, 0, 8),
                    (False, 1, 3, 0, 8),
                    (True, 2, 4, 0, 8),
                )
            )


def written(half, pieces, shape, into=None):
    vmem, anywhere = pl.BlockSpec(memory_space=pltpu.VMEM), pl.BlockSpec(memory_space=pl.ANY)
    extra = () if into is None else (into,)
    return pl.pallas_call(
        functools.partial(write_kernel, half, into is not None),
        out_shape=jax.ShapeDtypeStruct(shape, jnp.float32),
        in_specs=[vmem] * len(pieces) + [anywhere] * len(extra),
        out_specs=anywhere,
        input_output_aliases={len(pieces): 0} if extra else {},
        scratch_shapes=[pltpu.SemaphoreType.DMA((6,))],
        compiler_params=pltpu.CompilerParams(vmem_limit_bytes=16 << 20),
    )(*pieces, *extra)


def after(value, earlier):
    return lax.optimization_barrier((value, earlier))[0]


def masked_update(update, v, drive, inside):
    wide = (
        jnp.roll(v, 1, axis=0) + jnp.roll(v, -1, axis=0)
    ) + (jnp.roll(v, 1, axis=1) + jnp.roll(v, -1, axis=1))
    return jnp.where(inside, update(v, wide, drive), 0.0)


def long_chain(own, drive):
    height = own.shape[0]
    half = height // 2
    groups, slices, rows = (lax.axis_size(a) for a in AXES)
    t, r = lax.axis_index("tm"), lax.axis_index("rows")
    core, chip = t % 2, t // 2
    first = core == 0
    away = outward(groups, rows)

    def cut(field, start, size):
        return lax.dynamic_slice_in_dim(field, start, size, axis=0)

    other = routed(own, partner)
    s_a, s_b = picked(first, own, other)
    edge = core * (height - WIDE)
    got = routed(jnp.concatenate([cut(f, edge, WIDE) for f in (s_a, s_b, drive)]), away)

    def sided(body, outer, inner):
        return jnp.where(
            first,
            jnp.concatenate([outer, body, inner]),
            jnp.concatenate([inner, body, outer]),
        )

    def window(field, place):
        body = cut(field, core * half, half)
        inner = cut(field, jnp.where(first, half, half - WIDE), WIDE)
        return sided(body, got[place * WIDE : (place + 1) * WIDE], inner)

    w_a, w_b, w_d = (window(f, i) for i, f in enumerate((s_a, s_b, drive)))
    row = lax.broadcasted_iota(jnp.int32, (half + 2 * WIDE, 1), 0)
    row = row + r * height + core * half - WIDE
    inside = (row >= 0) & (row < rows * height)
    w_a, w_b = jnp.where(inside, w_a, 0.0), jnp.where(inside, w_b, 0.0)

    def delta(v):
        fine = v
        for _ in range(FINE):
            fine = masked_update(fine_of, fine, w_d, inside)
        return fine - masked_update(coarse_of, v, w_d, inside)

    d_a, d_b = delta(w_a), delta(w_b)

    def both(v):
        e_a = masked_update(coarse_of, v, w_d, inside) + d_a
        return e_a, masked_update(coarse_of, e_a, w_d, inside) + d_b

    def extended(v):
        last = WIDE + half - 2
        inner = routed(cut(v, jnp.where(first, last, WIDE), 2), partner)
        outer = routed(cut(v, jnp.where(first, WIDE, last), 2), away)
        return sided(v[WIDE : WIDE + half], outer, inner)

    e_a, e_b = both(w_a)
    for stage in range(slices // 2 - 1):
        moved = e_b[WIDE - 2 : WIDE + half + 2] if stage == 0 else extended(e_b)
        arrived = routed(moved, stage_swap(stage))
        current = jnp.pad(arrived, ((WIDE - 2, WIDE - 2), (0, 0)))
        n_a, n_b = both(jnp.where(inside, current, 0.0))
        here = chip == stage + 1
        e_a, e_b = jnp.where(here, n_a, e_a), jnp.where(here, n_b, e_b)

    kept, sent = picked(first, e_a[WIDE : WIDE + half], e_b[WIDE : WIDE + half])
    back = routed(sent, partner)
    return jnp.concatenate(picked(first, kept, back))[None]


def on_device(starts, drive):
    own = starts[0]
    if lax.axis_size("tm") != 4:
        return long_chain(own, drive)
    return two_chips(starts, drive)


def two_chips(starts, drive):
    _, height, width = starts.shape
    half = height // 2
    groups, rows = lax.axis_size("groups"), lax.axis_size("rows")
    vmem = pl.BlockSpec(memory_space=pltpu.VMEM)

    other = routed(starts[0], partner)
    own, held, mine = pl.pallas_call(
        functools.partial(load_kernel, half),
        out_shape=[
            jax.ShapeDtypeStruct((size, width), jnp.float32) for size in (height, height, height)
        ],
        in_specs=[pl.BlockSpec(memory_space=pltpu.HBM)] * 2,
        out_specs=[vmem] * 3,
        scratch_shapes=[pltpu.SemaphoreType.DMA((6,))],
        compiler_params=pltpu.CompilerParams(vmem_limit_bytes=50 << 20),
        cost_estimate=pl.CostEstimate(
            flops=60 * 24 * width, bytes_accessed=16 * height * width, transcendentals=0
        ),
        name="load",
    )(starts, drive)
    mid = width // 2
    packed = mid * (half // 8 - 2) + mid * 3 // 4
    sent_l, ends_l = compute(
        functools.partial(inner_kernel, half, 0),
        [(8, packed), (height, mid)],
        (own, other, held, mine),
    )
    here_l = routed(sent_l, stage_swap(0))
    sent_r, ends_r, edge = compute(
        functools.partial(inner_kernel, half, 1),
        [(8, packed), (height, mid), (8, width * 9 // 4)],
        (own, other, held, after(mine, sent_l)),
    )
    here_r = routed(sent_r, stage_swap(0))
    got = routed(edge, outward(groups, rows))
    sent_2, ends_2, delta_own = compute(
        functools.partial(middle_kernel, half),
        [(8, width), (32, width), (half + WIDE, width)],
        (own, other, after(held, sent_r)),
    )
    here_2 = routed(sent_2, stage_swap(0))
    (delta_other,) = compute(
        functools.partial(state_kernel, half), [(half + WIDE, width)], (other, after(held, sent_2))
    )
    sent_3, ends_3, state_3 = compute(
        functools.partial(outer_kernel, half),
        [(8, width * 3 // 4), (32, width), (3 * 24, width)],
        (own, other, held, got, delta_own, delta_other),
    )
    here_3 = routed(sent_3, stage_swap(0))
    near_keep, near_send, frame = compute(
        functools.partial(inner_end, half),
        [(half - 16, width), (half - 16, width), (half - 8, width)],
        (here_l, here_r, held, delta_own, after(delta_other, sent_3)),
    )
    keep_1, send_1 = compute(
        functools.partial(gather_kernel, half),
        [(half, width)] * 2,
        (ends_l, ends_r, ends_2, ends_3, near_keep, near_send),
    )
    back_1 = routed(send_1, partner)
    keep_2, send_2 = compute(
        functools.partial(middle_end, half),
        [(8, width)] * 2,
        (frame, here_2, held, delta_own, after(delta_other, state_3)),
        scratch_shapes=[pltpu.VMEM((24, width), jnp.float32)],
    )
    back_2 = routed(send_2, partner)
    keep_3, send_3 = compute(
        outer_end,
        [(8, width)] * 2,
        (frame, here_2, here_3, after(state_3, keep_2)),
        scratch_shapes=[pltpu.VMEM((24, width), jnp.float32)],
    )
    back_3 = routed(send_3, partner)
    out = written(half, (keep_1, back_1, keep_2, back_2, keep_3), starts.shape)
    return written(half, (back_3,), starts.shape, into=out)


def solution(mesh):
    in_specs = (P(("groups", "tm"), "rows", None), P("rows", None))
    out_specs = P(("groups", "tm"), "rows", None)
    return jax.shard_map(
        on_device, mesh=mesh, in_specs=in_specs, out_specs=out_specs, check_vma=False
    )
```

```python
import functools

import jax
import jax.numpy as jnp
from jax import lax
from jax.experimental import pallas as pl
from jax.experimental.pallas import tpu as pltpu
from jax.sharding import PartitionSpec as P


FINE = 3
WIDE = 8
CUT = 4


diffusion = 2.0
step_fine = 0.1
coarse_step = FINE * step_fine
damping = 1.0 + 4.0 * diffusion * coarse_step

AXES = ("groups", "tm", "rows")


def routed(block, route):
    groups, slices, rows = (lax.axis_size(a) for a in AXES)
    pairs = []
    for g in range(groups):
        for t in range(slices):
            for r in range(rows):
                to_g, to_t, to_r = route(g, t, r)
                source = (g * slices + t) * rows + r
                pairs.append((source, (to_g * slices + to_t) * rows + to_r))
    return lax.ppermute(block, AXES, pairs)


def partner(g, t, r):
    return g, t ^ 1, r


def outward(groups, rows):
    def route(g, t, r):
        to_r = r + 1 if t & 1 else r - 1
        if 0 <= to_r < rows:
            return g, t ^ 1, to_r
        other = g ^ 1
        return (other, t, r) if other < groups else (g, t, r)

    return route


def stage_swap(stage):
    def route(g, t, r):
        chip = t // 2
        if chip == stage:
            return g, t + 2, r
        if chip == stage + 1:
            return g, t - 2, r
        return g, t, r

    return route


def around(v):
    height, width = v.shape
    return (pltpu.roll(v, 1, 0) + pltpu.roll(v, height - 1, 0)) + (
        pltpu.roll(v, 1, 1) + pltpu.roll(v, width - 1, 1)
    )


def fine_of(v, nsum, drive):
    return (
        step_fine * diffusion * nsum
        + v * ((1.0 + step_fine - 4.0 * step_fine * diffusion) - step_fine * (v * v))
        + step_fine * drive
    )


def coarse_of(v, nsum, drive):
    scale = coarse_step / damping
    return (
        scale * diffusion * nsum
        + v * ((1.0 + coarse_step) / damping - scale * (v * v))
        + scale * drive
    )


def compute(kernel, outs, args, **kwargs):
    shapes = [jax.ShapeDtypeStruct(o, jnp.float32) for o in outs]
    vmem = pl.BlockSpec(memory_space=pltpu.VMEM)
    return pl.pallas_call(
        kernel,
        out_shape=shapes,
        in_specs=[vmem] * len(args),
        out_specs=[vmem] * len(outs),
        compiler_params=pltpu.CompilerParams(vmem_limit_bytes=16 << 20),
        **kwargs,
    )(*args)


def same(v):
    return v


def start_of(v, drive, kept=same):
    nsum = around(v)
    coarse = kept(coarse_of(v, nsum, drive))
    fine = kept(fine_of(v, nsum, drive))
    for _ in range(FINE - 1):
        fine = kept(fine_of(fine, around(fine), drive))
    return fine, coarse


def ends_of(first, mine, theirs, drive, kept=same):
    f_a, f_b = picked(first, mine[0], theirs[0])
    g_a, g_b = picked(first, mine[1], theirs[1])
    e_a = g_a + (f_a - g_a)
    e_b = kept(coarse_of(e_a, around(e_a), drive)) + (f_b - g_b)
    return e_a, e_b


def chain(current, d_a, d_b, drive, kept=same):
    e_a = kept(coarse_of(current, around(current), drive)) + d_a
    e_b = kept(coarse_of(e_a, around(e_a), drive)) + d_b
    return e_a, e_b


def picked(first, own, other):
    return jnp.where(first, own, other), jnp.where(first, other, own)


def field(ref, kind, kinds, start, size):
    height = ref.shape[0] // kinds
    return ref.at[pl.ds(pl.multiple_of(kind * height + start, 8), size), :]


def mixed(upper, lower):
    row = lax.broadcasted_iota(jnp.int32, upper.shape, 0)
    return jnp.where(row < CUT, upper, lower)


def sublane(v):
    return lax.broadcasted_iota(jnp.int32, v.shape, 0)


def folded(v):
    width = v.shape[1]
    half, quarter = width // 2, width // 4
    four = mixed(v[:, :half], pltpu.roll(v[:, half:], 4, 0))
    row = sublane(four[:, :quarter])
    two = pltpu.roll(v[:, :quarter], 4, 0)
    for i, shift in ((1, 6), (2, 0), (3, 2)):
        part = v[:, i * quarter : (i + 1) * quarter]
        part = pltpu.roll(part, shift, 0) if shift else part
        two = jnp.where(row < 2 * i, two, part)
    return jnp.concatenate([four, two], axis=1)


def unfolded(v):
    half = v.shape[1] * 2 // 3
    four, two = v[:, :half], v[:, half:]
    low = [pltpu.roll(two, 4, 0), pltpu.roll(two, 2, 0), two, pltpu.roll(two, 6, 0)]
    return mixed(
        jnp.concatenate([four, pltpu.roll(four, 4, 0)], axis=1),
        jnp.concatenate(low, axis=1),
    )


def place():
    t = lax.axis_index("tm")
    return t % 2, t // 2


def at_edge(core):
    r, rows = lax.axis_index("rows"), lax.axis_size("rows")
    return ((core == 0) & (r == 0)) | ((core == 1) & (r == rows - 1))


def inner_row(half, core):
    return pl.multiple_of(8 + (half - 16) * core, 8)


def middle_row(half, core):
    return pl.multiple_of((2 * half - 16) * core, 8)


def outer_row(half, core):
    return pl.multiple_of((2 * half - WIDE) * core, 8)


def load_kernel(half, starts, drive, own, held, inner, sems):
    core, chip = place()
    copies = []
    for i, (row, size) in enumerate(((8, 2 * half - 16), (0, 8), (2 * half - 8, 8))):
        rows = pl.ds(row, size)
        pair = (
            pltpu.make_async_copy(starts.at[0, rows, :], own.at[rows, :], sems.at[2 * i]),
            pltpu.make_async_copy(drive.at[rows, :], held.at[rows, :], sems.at[2 * i + 1]),
        )
        for copy in pair:
            copy.start()
        copies.append(pair)

    for copy in copies[0]:
        copy.wait()

    @pl.when(chip == 0)
    def _():
        rows = pl.ds(inner_row(half, core), half)
        fine, coarse = start_of(own[rows, :], held[rows, :])
        inner[0:half, :] = fine
        inner[half : 2 * half, :] = coarse

    for copy in (*copies[1], *copies[2]):
        copy.wait()


def inner_kernel(half, side, own, other, drive, mine, sent, ends, edge=None):
    core, chip = place()
    first = core == 0
    width = drive.shape[1]
    mid = width // 2

    def columns(ref, rows):
        if side == 0:
            parts = ref[rows, width - 128 :], ref[rows, : mid + 128]
        else:
            parts = ref[rows, mid - 128 :], ref[rows, :128]
        return jnp.concatenate(parts, axis=1)

    @pl.when(chip == 0)
    def _():
        rows = pl.ds(inner_row(half, core), half)
        d = columns(drive, rows)
        theirs = start_of(columns(other, rows), d)
        known = columns(mine, pl.ds(0, half)), columns(mine, pl.ds(half, half))
        e_a, e_b = ends_of(first, known, theirs, d)
        e_a, e_b = e_a[:, 128:-128], e_b[:, 128:-128]
        frame = pltpu.roll(e_b, half - CUT, 0)
        count = half // 8 - 2
        whole = [
            jnp.where(first, frame[8 * i : 8 * i + 8], frame[8 * i + 8 : 8 * i + 16])
            for i in range(count)
        ]
        part = jnp.where(
            first, frame[8 * count : 8 * count + 8], pltpu.roll(frame[:8], 6, 0)
        )
        sent[...] = jnp.concatenate([*whole, folded(part)], axis=1)
        ends[0:half, :] = e_a
        ends[half : 2 * half, :] = e_b

    if edge is not None:
        rows = pl.ds(outer_row(half, core), 8)
        a, b = picked(first, own[rows, :], other[rows, :])
        fields = (jnp.where(first, v, pltpu.roll(v, 6, 0)) for v in (a, b, drive[rows, :]))
        edge[...] = jnp.concatenate([folded(v) for v in fields], axis=1)


def middle_kernel(half, own, other, drive, sent, ends, delta):
    core, chip = place()
    first = core == 0

    @pl.when(chip == 0)
    def _():
        rows = pl.ds(middle_row(half, core), 16)
        d = drive[rows, :]
        mine, theirs = start_of(own[rows, :], d), start_of(other[rows, :], d)
        e_a, e_b = ends_of(first, mine, theirs, d)
        sent[...] = pltpu.roll(e_b, 16 - CUT, 0)[:8]
        ends[0:16, :] = e_a
        ends[16:32, :] = e_b

    @pl.when(chip > 0)
    def _():
        rows = receiver_rows(half, core)
        fine, coarse = start_of(own[rows, :], drive[rows, :])
        delta[...] = fine - coarse


def receiver_rows(half, core):
    return pl.ds(pl.multiple_of((half - WIDE) * core, 8), half + WIDE)


def state_kernel(half, other, drive, theirs):
    core, chip = place()

    @pl.when(chip > 0)
    def _():
        rows = receiver_rows(half, core)
        fine, coarse = start_of(other[rows, :], drive[rows, :])
        theirs[...] = fine - coarse


def outer_window(half, own, other, drive, got):
    core, _ = place()
    first = core == 0
    rows = pl.ds(outer_row(half, core), 8)
    a, b = picked(first, own[rows, :], other[rows, :])
    near = (a, b, drive[rows, :])
    size = got.shape[1] // 3
    far = [unfolded(got[:, i * size : (i + 1) * size]) for i in range(3)]
    far = [jnp.where(first, pltpu.roll(v, 2, 0), v) for v in far]
    upper = [jnp.where(first, f, n) for f, n in zip(far, near)]
    lower = [jnp.where(first, n, f) for f, n in zip(far, near)]
    a, b, d = (jnp.concatenate(p) for p in zip(upper, lower))
    inside = ~(at_edge(core) & (sublane(a) // 8 == core))

    def kept(v):
        return jnp.where(inside, v, 0.0)

    return kept(a), kept(b), d, kept


def outer_kernel(half, own, other, drive, got, sent, ends):
    core, chip = place()
    first = core == 0
    a, b, d, kept = outer_window(half, own, other, drive, got)
    f_a, g_a = start_of(a, d, kept)

    @pl.when(chip == 0)
    def _():
        f_b, g_b = start_of(b, d, kept)
        e_a = g_a + (f_a - g_a)
        e_b = kept(coarse_of(e_a, around(e_a), d)) + (f_b - g_b)
        frame = pltpu.roll(e_b, 16 - CUT, 0)[:8]
        sent[...] = folded(jnp.where(first, pltpu.roll(frame, 6, 0), frame))
        ends[0:16, :] = e_a
        ends[16:32, :] = e_b

    @pl.when(chip > 0)
    def _():
        ends[0:16, :] = f_a - g_a


def outer_state_kernel(half, own, other, drive, got, mine, theirs, ends, state):
    core, chip = place()
    first = core == 0

    @pl.when(chip > 0)
    def _():
        _, b, d, kept = outer_window(half, own, other, drive, got)
        f_b, g_b = start_of(b, d, kept)
        rows = pl.ds(pl.multiple_of((half - WIDE) * core, 8), 16)
        before = picked(first, mine[rows, :], theirs[rows, :])
        d_rows = pl.ds(pl.multiple_of((2 * half - 16) * core, 8), 16)
        fields = zip((ends[0:16, :], f_b - g_b, d), (*before, drive[d_rows, :]))
        for kind, (v, near) in enumerate(fields):
            top = jnp.where(first, v[:8], near[:8])
            mid = jnp.where(first, mixed(v[8:], near[:8]), mixed(near[8:], v[:8]))
            low = jnp.where(first, near[8:], v[8:])
            state[24 * kind : 24 * kind + 24, :] = jnp.concatenate([top, mid, low])


def near_end(
    half,
    left,
    right,
    middle,
    drive,
    mine,
    theirs,
    ends_left,
    ends_right,
    ends_middle,
    ends_outer,
    keep,
    send,
    frame,
):
    core, chip = place()
    first = core == 0

    def put(begin, e_a, e_b):
        kept, sent = picked(first, e_a, e_b)
        keep[pl.ds(begin, kept.shape[0]), :] = kept
        send[pl.ds(begin, kept.shape[0]), :] = sent

    @pl.when(chip == 0)
    def _():
        def rows(kind, begin, size):
            into = pl.ds(half * kind + begin, size)
            return jnp.concatenate([ends_left[into, :], ends_right[into, :]], axis=1)

        def known(kind):
            two = [field(ends_middle, kind, 2, 8 * i, 8)[...] for i in range(2)]
            last = [field(ends_outer, kind, 2, 8 * i, 8)[...] for i in range(2)]
            inner = rows(kind, 8, half - 16)
            upper = jnp.concatenate([mixed(two[1], rows(kind, 0, 8)), inner])
            lower = jnp.concatenate([inner, mixed(rows(kind, half - 8, 8), two[0])])
            edge = jnp.where(first, mixed(last[1], two[0]), mixed(two[1], last[0]))
            return jnp.concatenate([jnp.where(first, upper, lower), edge])

        put(0, known(0), known(1))

    @pl.when(chip > 0)
    def _():
        count = half // 8 - 2
        mid = left.shape[1] * 4 // (4 * count + 3)
        parts = left[...], right[...]

        def across(begin, end, change=same):
            return jnp.concatenate([change(p[:, begin:end]) for p in parts], axis=1)

        whole = [across(i * mid, i * mid + mid) for i in range(count)]
        part = across(count * mid, left.shape[1], unfolded)
        beside = middle[...]
        upper = [beside, *whole, part]
        lower = [pltpu.roll(part, 2, 0), *whole, beside]
        rows = [jnp.where(first, u, v) for u, v in zip(upper, lower)]
        frame[0:8, :] = jnp.where(first, rows[0], rows[-2])
        frame[8:16, :] = jnp.where(first, rows[1], rows[-1])
        current = pltpu.roll(jnp.concatenate([*rows, rows[0]]), CUT, 0)
        d_a, d_b = picked(first, mine[...], theirs[...])
        e_a, e_b = chain(current, d_a, d_b, drive[receiver_rows(half, core), :])
        put(0, e_a[8:half], e_b[8:half])


def put_ends(first, e_a, e_b, keep, send):
    kept, sent = picked(first, e_a, e_b)
    keep[...] = kept
    send[...] = sent


def outer_end(frame, outer, state, keep, send, current):
    core, chip = place()
    first = core == 0

    @pl.when((chip > 0) & first)
    def _():
        part = pltpu.roll(unfolded(outer[...]), 2, 0)
        current[...] = pltpu.roll(jnp.concatenate([part, frame[...]]), CUT, 0)

    @pl.when((chip > 0) & (core == 1))
    def _():
        rows = jnp.concatenate([frame[...], unfolded(outer[...])])
        current[...] = pltpu.roll(rows, 24 - CUT, 0)

    @pl.when(chip > 0)
    def _():
        d_a, d_b, d = (field(state, kind, 3, 0, 24)[...] for kind in range(3))
        inside = ~(at_edge(core) & (sublane(d) // 8 == 2 * core))
        e_a = coarse_of(current[...], around(current[...]), d) + d_a
        e_a = jnp.where(inside, e_a, 0.0)
        mid = e_a[8:16]
        width = mid.shape[1]
        beside = pltpu.roll(mid, 1, 1) + pltpu.roll(mid, width - 1, 1)
        upright = pltpu.roll(e_a, 1, 0)[8:16] + pltpu.roll(e_a, 23, 0)[8:16]
        e_b = coarse_of(mid, upright + beside, d[8:16]) + d_b[8:16]
        put_ends(first, mid, e_b, keep, send)


def write_kernel(half, last, *refs):
    pieces, out, sems = refs[: 1 if last else 3], refs[-2], refs[-1]
    core, chip = place()
    near = half - 8

    def copy_all(order):
        copies = []
        for i, (mine, part, source, begin) in enumerate(order):
            size = (near, 8)[part]
            upper, lower = ((8, half), (0, 2 * half - 8))[part]
            row = pl.multiple_of(jnp.where((core == 0) == mine, upper, lower), 8)
            copy = pltpu.make_async_copy(
                pieces[source].at[pl.ds(begin, size), :],
                out.at[0, pl.ds(row, size), :],
                sems.at[i],
            )
            copy.start()
            copies.append(copy)
        for copy in copies:
            copy.wait()

    if last:

        @pl.when(chip > 0)
        def _():
            copy_all(((False, 1, 0, 0),))

    else:

        @pl.when(chip == 0)
        def _():
            copy_all(((True, 0, 0, 0), (False, 0, 1, 0), (True, 1, 0, near), (False, 1, 1, near)))

        @pl.when(chip > 0)
        def _():
            copy_all(((True, 0, 0, 0), (False, 0, 1, 0), (True, 1, 2, 0)))


def written(half, pieces, shape, into=None):
    vmem, anywhere = pl.BlockSpec(memory_space=pltpu.VMEM), pl.BlockSpec(memory_space=pl.ANY)
    extra = () if into is None else (into,)
    return pl.pallas_call(
        functools.partial(write_kernel, half, into is not None),
        out_shape=jax.ShapeDtypeStruct(shape, jnp.float32),
        in_specs=[vmem] * len(pieces) + [anywhere] * len(extra),
        out_specs=anywhere,
        input_output_aliases={len(pieces): 0} if extra else {},
        scratch_shapes=[pltpu.SemaphoreType.DMA((6,))],
        compiler_params=pltpu.CompilerParams(vmem_limit_bytes=16 << 20),
    )(*pieces, *extra)


def after(value, earlier):
    return lax.optimization_barrier((value, earlier))[0]


def masked_update(update, v, drive, inside):
    wide = (
        jnp.roll(v, 1, axis=0) + jnp.roll(v, -1, axis=0)
    ) + (jnp.roll(v, 1, axis=1) + jnp.roll(v, -1, axis=1))
    return jnp.where(inside, update(v, wide, drive), 0.0)


def long_chain(own, drive):
    height = own.shape[0]
    half = height // 2
    groups, slices, rows = (lax.axis_size(a) for a in AXES)
    t, r = lax.axis_index("tm"), lax.axis_index("rows")
    core, chip = t % 2, t // 2
    first = core == 0
    away = outward(groups, rows)

    def cut(field, start, size):
        return lax.dynamic_slice_in_dim(field, start, size, axis=0)

    other = routed(own, partner)
    s_a, s_b = picked(first, own, other)
    edge = core * (height - WIDE)
    got = routed(jnp.concatenate([cut(f, edge, WIDE) for f in (s_a, s_b, drive)]), away)

    def sided(body, outer, inner):
        return jnp.where(
            first,
            jnp.concatenate([outer, body, inner]),
            jnp.concatenate([inner, body, outer]),
        )

    def window(field, place):
        body = cut(field, core * half, half)
        inner = cut(field, jnp.where(first, half, half - WIDE), WIDE)
        return sided(body, got[place * WIDE : (place + 1) * WIDE], inner)

    w_a, w_b, w_d = (window(f, i) for i, f in enumerate((s_a, s_b, drive)))
    row = lax.broadcasted_iota(jnp.int32, (half + 2 * WIDE, 1), 0)
    row = row + r * height + core * half - WIDE
    inside = (row >= 0) & (row < rows * height)
    w_a, w_b = jnp.where(inside, w_a, 0.0), jnp.where(inside, w_b, 0.0)

    def delta(v):
        fine = v
        for _ in range(FINE):
            fine = masked_update(fine_of, fine, w_d, inside)
        return fine - masked_update(coarse_of, v, w_d, inside)

    d_a, d_b = delta(w_a), delta(w_b)

    def both(v):
        e_a = masked_update(coarse_of, v, w_d, inside) + d_a
        return e_a, masked_update(coarse_of, e_a, w_d, inside) + d_b

    def extended(v):
        last = WIDE + half - 2
        inner = routed(cut(v, jnp.where(first, last, WIDE), 2), partner)
        outer = routed(cut(v, jnp.where(first, WIDE, last), 2), away)
        return sided(v[WIDE : WIDE + half], outer, inner)

    e_a, e_b = both(w_a)
    for stage in range(slices // 2 - 1):
        moved = e_b[WIDE - 2 : WIDE + half + 2] if stage == 0 else extended(e_b)
        arrived = routed(moved, stage_swap(stage))
        current = jnp.pad(arrived, ((WIDE - 2, WIDE - 2), (0, 0)))
        n_a, n_b = both(jnp.where(inside, current, 0.0))
        here = chip == stage + 1
        e_a, e_b = jnp.where(here, n_a, e_a), jnp.where(here, n_b, e_b)

    kept, sent = picked(first, e_a[WIDE : WIDE + half], e_b[WIDE : WIDE + half])
    back = routed(sent, partner)
    return jnp.concatenate(picked(first, kept, back))[None]


def on_device(starts, drive):
    own = starts[0]
    if lax.axis_size("tm") != 4:
        return long_chain(own, drive)
    return two_chips(starts, drive)


def two_chips(starts, drive):
    _, height, width = starts.shape
    half = height // 2
    groups, rows = lax.axis_size("groups"), lax.axis_size("rows")
    vmem = pl.BlockSpec(memory_space=pltpu.VMEM)

    other = routed(starts[0], partner)
    own, held, mine = pl.pallas_call(
        functools.partial(load_kernel, half),
        out_shape=[
            jax.ShapeDtypeStruct((size, width), jnp.float32) for size in (height, height, height)
        ],
        in_specs=[pl.BlockSpec(memory_space=pltpu.HBM)] * 2,
        out_specs=[vmem] * 3,
        scratch_shapes=[pltpu.SemaphoreType.DMA((6,))],
        compiler_params=pltpu.CompilerParams(vmem_limit_bytes=50 << 20),
        cost_estimate=pl.CostEstimate(
            flops=60 * 24 * width, bytes_accessed=16 * height * width, transcendentals=0
        ),
        name="load",
    )(starts, drive)
    mid = width // 2
    packed = mid * (half // 8 - 2) + mid * 3 // 4
    sent_l, ends_l = compute(
        functools.partial(inner_kernel, half, 0),
        [(8, packed), (height, mid)],
        (own, other, held, mine),
    )
    here_l = routed(sent_l, stage_swap(0))
    sent_r, ends_r, edge = compute(
        functools.partial(inner_kernel, half, 1),
        [(8, packed), (height, mid), (8, width * 9 // 4)],
        (own, other, held, after(mine, sent_l)),
    )
    here_r = routed(sent_r, stage_swap(0))
    got = routed(edge, outward(groups, rows))
    sent_2, ends_2, delta_own = compute(
        functools.partial(middle_kernel, half),
        [(8, width), (32, width), (half + WIDE, width)],
        (own, other, after(held, sent_r)),
    )
    here_2 = routed(sent_2, stage_swap(0))
    (delta_other,) = compute(
        functools.partial(state_kernel, half),
        [(half + WIDE, width)],
        (other, after(held, sent_2)),
    )
    sent_3, ends_3 = compute(
        functools.partial(outer_kernel, half),
        [(8, width * 3 // 4), (32, width)],
        (own, other, after(held, delta_other), got),
    )
    here_3 = routed(sent_3, stage_swap(0))
    (state_3,) = compute(
        functools.partial(outer_state_kernel, half),
        [(3 * 24, width)],
        (own, other, held, got, delta_own, delta_other, ends_3),
    )
    keep_1, send_1, frame = compute(
        functools.partial(near_end, half),
        [(half, width), (half, width), (16, width)],
        (
            here_l,
            here_r,
            here_2,
            held,
            delta_own,
            after(delta_other, state_3),
            ends_l,
            ends_r,
            ends_2,
            ends_3,
        ),
    )
    back_1 = routed(send_1, partner)
    keep_3, send_3 = compute(
        outer_end,
        [(8, width)] * 2,
        (frame, here_3, state_3),
        scratch_shapes=[pltpu.VMEM((24, width), jnp.float32)],
    )
    back_3 = routed(send_3, partner)
    out = written(half, (keep_1, back_1, keep_3), starts.shape)
    return written(half, (back_3,), starts.shape, into=out)


def solution(mesh):
    in_specs = (P(("groups", "tm"), "rows", None), P("rows", None))
    out_specs = P(("groups", "tm"), "rows", None)
    return jax.shard_map(
        on_device, mesh=mesh, in_specs=in_specs, out_specs=out_specs, check_vma=False
    )
```

```python
import functools

import jax
import jax.numpy as jnp
from jax import lax
from jax.experimental import pallas as pl
from jax.experimental.pallas import tpu as pltpu
from jax.sharding import PartitionSpec as P


FINE = 3
WIDE = 8
CUT = 4


diffusion = 2.0
step_fine = 0.1
coarse_step = FINE * step_fine
damping = 1.0 + 4.0 * diffusion * coarse_step

AXES = ("groups", "tm", "rows")


def routed(block, route):
    groups, slices, rows = (lax.axis_size(a) for a in AXES)
    pairs = []
    for g in range(groups):
        for t in range(slices):
            for r in range(rows):
                to_g, to_t, to_r = route(g, t, r)
                source = (g * slices + t) * rows + r
                pairs.append((source, (to_g * slices + to_t) * rows + to_r))
    return lax.ppermute(block, AXES, pairs)


def partner(g, t, r):
    return g, t ^ 1, r


def outward(groups, rows):
    def route(g, t, r):
        to_r = r + 1 if t & 1 else r - 1
        if 0 <= to_r < rows:
            return g, t ^ 1, to_r
        other = g ^ 1
        return (other, t, r) if other < groups else (g, t, r)

    return route


def stage_swap(stage):
    def route(g, t, r):
        chip = t // 2
        if chip == stage:
            return g, t + 2, r
        if chip == stage + 1:
            return g, t - 2, r
        return g, t, r

    return route


def around(v):
    height, width = v.shape
    return (pltpu.roll(v, 1, 0) + pltpu.roll(v, height - 1, 0)) + (
        pltpu.roll(v, 1, 1) + pltpu.roll(v, width - 1, 1)
    )


def fine_of(v, nsum, drive):
    return (
        step_fine * diffusion * nsum
        + v * ((1.0 + step_fine - 4.0 * step_fine * diffusion) - step_fine * (v * v))
        + step_fine * drive
    )


def coarse_of(v, nsum, drive):
    scale = coarse_step / damping
    return (
        scale * diffusion * nsum
        + v * ((1.0 + coarse_step) / damping - scale * (v * v))
        + scale * drive
    )


def compute(kernel, outs, args, **kwargs):
    shapes = [jax.ShapeDtypeStruct(o, jnp.float32) for o in outs]
    vmem = pl.BlockSpec(memory_space=pltpu.VMEM)
    return pl.pallas_call(
        kernel,
        out_shape=shapes,
        in_specs=[vmem] * len(args),
        out_specs=[vmem] * len(outs),
        compiler_params=pltpu.CompilerParams(vmem_limit_bytes=16 << 20),
        **kwargs,
    )(*args)


def same(v):
    return v


def start_of(v, drive, kept=same):
    nsum = around(v)
    coarse = kept(coarse_of(v, nsum, drive))
    fine = kept(fine_of(v, nsum, drive))
    for _ in range(FINE - 1):
        fine = kept(fine_of(fine, around(fine), drive))
    return fine, coarse


def ends_of(first, mine, theirs, drive, kept=same):
    f_a, f_b = picked(first, mine[0], theirs[0])
    g_a, g_b = picked(first, mine[1], theirs[1])
    e_a = g_a + (f_a - g_a)
    e_b = kept(coarse_of(e_a, around(e_a), drive)) + (f_b - g_b)
    return e_a, e_b


def chain(current, d_a, d_b, drive, kept=same):
    e_a = kept(coarse_of(current, around(current), drive)) + d_a
    e_b = kept(coarse_of(e_a, around(e_a), drive)) + d_b
    return e_a, e_b


def picked(first, own, other):
    return jnp.where(first, own, other), jnp.where(first, other, own)


def field(ref, kind, kinds, start, size):
    height = ref.shape[0] // kinds
    return ref.at[pl.ds(pl.multiple_of(kind * height + start, 8), size), :]


def mixed(upper, lower):
    row = lax.broadcasted_iota(jnp.int32, upper.shape, 0)
    return jnp.where(row < CUT, upper, lower)


def sublane(v):
    return lax.broadcasted_iota(jnp.int32, v.shape, 0)


def folded(v):
    width = v.shape[1]
    half, quarter = width // 2, width // 4
    four = mixed(v[:, :half], pltpu.roll(v[:, half:], 4, 0))
    row = sublane(four[:, :quarter])
    two = pltpu.roll(v[:, :quarter], 4, 0)
    for i, shift in ((1, 6), (2, 0), (3, 2)):
        part = v[:, i * quarter : (i + 1) * quarter]
        part = pltpu.roll(part, shift, 0) if shift else part
        two = jnp.where(row < 2 * i, two, part)
    return jnp.concatenate([four, two], axis=1)


def unfolded(v):
    half = v.shape[1] * 2 // 3
    four, two = v[:, :half], v[:, half:]
    low = [pltpu.roll(two, 4, 0), pltpu.roll(two, 2, 0), two, pltpu.roll(two, 6, 0)]
    return mixed(
        jnp.concatenate([four, pltpu.roll(four, 4, 0)], axis=1),
        jnp.concatenate(low, axis=1),
    )


def place():
    t = lax.axis_index("tm")
    return t % 2, t // 2


def at_edge(core):
    r, rows = lax.axis_index("rows"), lax.axis_size("rows")
    return ((core == 0) & (r == 0)) | ((core == 1) & (r == rows - 1))


def inner_row(half, core):
    return pl.multiple_of(8 + (half - 16) * core, 8)


def middle_row(half, core):
    return pl.multiple_of((2 * half - 16) * core, 8)


def outer_row(half, core):
    return pl.multiple_of((2 * half - WIDE) * core, 8)


def load_kernel(half, starts, drive, own, held, inner, sems):
    core, chip = place()
    copies = []
    for i, (row, size) in enumerate(((8, 2 * half - 16), (0, 8), (2 * half - 8, 8))):
        rows = pl.ds(row, size)
        pair = (
            pltpu.make_async_copy(starts.at[0, rows, :], own.at[rows, :], sems.at[2 * i]),
            pltpu.make_async_copy(drive.at[rows, :], held.at[rows, :], sems.at[2 * i + 1]),
        )
        for copy in pair:
            copy.start()
        copies.append(pair)

    for copy in copies[0]:
        copy.wait()

    @pl.when(chip == 0)
    def _():
        rows = pl.ds(inner_row(half, core), half)
        fine, coarse = start_of(own[rows, :], held[rows, :])
        inner[0:half, :] = fine
        inner[half : 2 * half, :] = coarse

    for copy in (*copies[1], *copies[2]):
        copy.wait()


def inner_kernel(half, side, own, other, drive, mine, sent, ends, edge=None):
    core, chip = place()
    first = core == 0
    width = drive.shape[1]
    mid = width // 2

    def columns(ref, rows):
        if side == 0:
            parts = ref[rows, width - 128 :], ref[rows, : mid + 128]
        else:
            parts = ref[rows, mid - 128 :], ref[rows, :128]
        return jnp.concatenate(parts, axis=1)

    @pl.when(chip == 0)
    def _():
        rows = pl.ds(inner_row(half, core), half)
        d = columns(drive, rows)
        theirs = start_of(columns(other, rows), d)
        known = columns(mine, pl.ds(0, half)), columns(mine, pl.ds(half, half))
        e_a, e_b = ends_of(first, known, theirs, d)
        e_a, e_b = e_a[:, 128:-128], e_b[:, 128:-128]
        frame = pltpu.roll(e_b, half - CUT, 0)
        count = half // 8 - 2
        whole = [
            jnp.where(first, frame[8 * i : 8 * i + 8], frame[8 * i + 8 : 8 * i + 16])
            for i in range(count)
        ]
        part = jnp.where(
            first, frame[8 * count : 8 * count + 8], pltpu.roll(frame[:8], 6, 0)
        )
        sent[...] = jnp.concatenate([*whole, folded(part)], axis=1)
        ends[0:half, :] = e_a
        ends[half : 2 * half, :] = e_b

    if edge is not None:
        rows = pl.ds(outer_row(half, core), 8)
        a, b = picked(first, own[rows, :], other[rows, :])
        fields = (jnp.where(first, v, pltpu.roll(v, 6, 0)) for v in (a, b, drive[rows, :]))
        edge[...] = jnp.concatenate([folded(v) for v in fields], axis=1)


def middle_kernel(half, own, other, drive, sent, ends, delta):
    core, chip = place()
    first = core == 0

    @pl.when(chip == 0)
    def _():
        rows = pl.ds(middle_row(half, core), 16)
        d = drive[rows, :]
        mine, theirs = start_of(own[rows, :], d), start_of(other[rows, :], d)
        e_a, e_b = ends_of(first, mine, theirs, d)
        sent[...] = pltpu.roll(e_b, 16 - CUT, 0)[:8]
        ends[0:16, :] = e_a
        ends[16:32, :] = e_b

    @pl.when(chip > 0)
    def _():
        rows = receiver_rows(half, core)
        fine, coarse = start_of(own[rows, :], drive[rows, :])
        delta[...] = fine - coarse


def receiver_rows(half, core):
    return pl.ds(pl.multiple_of((half - WIDE) * core, 8), half + WIDE)


def state_kernel(half, other, drive, theirs):
    core, chip = place()

    @pl.when(chip > 0)
    def _():
        rows = receiver_rows(half, core)
        fine, coarse = start_of(other[rows, :], drive[rows, :])
        theirs[...] = fine - coarse


def outer_window(half, own, other, drive, got):
    core, _ = place()
    first = core == 0
    rows = pl.ds(outer_row(half, core), 8)
    a, b = picked(first, own[rows, :], other[rows, :])
    near = (a, b, drive[rows, :])
    size = got.shape[1] // 3
    far = [unfolded(got[:, i * size : (i + 1) * size]) for i in range(3)]
    far = [jnp.where(first, pltpu.roll(v, 2, 0), v) for v in far]
    upper = [jnp.where(first, f, n) for f, n in zip(far, near)]
    lower = [jnp.where(first, n, f) for f, n in zip(far, near)]
    a, b, d = (jnp.concatenate(p) for p in zip(upper, lower))
    inside = ~(at_edge(core) & (sublane(a) // 8 == core))

    def kept(v):
        return jnp.where(inside, v, 0.0)

    return kept(a), kept(b), d, kept


def outer_kernel(half, own, other, drive, got, sent, ends):
    core, chip = place()
    first = core == 0
    a, b, d, kept = outer_window(half, own, other, drive, got)
    f_a, g_a = start_of(a, d, kept)

    @pl.when(chip == 0)
    def _():
        f_b, g_b = start_of(b, d, kept)
        e_a = g_a + (f_a - g_a)
        e_b = kept(coarse_of(e_a, around(e_a), d)) + (f_b - g_b)
        frame = pltpu.roll(e_b, 16 - CUT, 0)[:8]
        sent[...] = folded(jnp.where(first, pltpu.roll(frame, 6, 0), frame))
        ends[0:16, :] = e_a
        ends[16:32, :] = e_b

    @pl.when(chip > 0)
    def _():
        ends[0:16, :] = f_a - g_a


def outer_state_kernel(half, own, other, drive, got, mine, theirs, ends, state):
    core, chip = place()
    first = core == 0

    @pl.when(chip > 0)
    def _():
        _, b, d, kept = outer_window(half, own, other, drive, got)
        f_b, g_b = start_of(b, d, kept)
        rows = pl.ds(pl.multiple_of((half - WIDE) * core, 8), 16)
        before = picked(first, mine[rows, :], theirs[rows, :])
        d_rows = pl.ds(pl.multiple_of((2 * half - 16) * core, 8), 16)
        fields = zip((ends[0:16, :], f_b - g_b, d), (*before, drive[d_rows, :]))
        for kind, (v, near) in enumerate(fields):
            top = jnp.where(first, v[:8], near[:8])
            mid = jnp.where(first, mixed(v[8:], near[:8]), mixed(near[8:], v[:8]))
            low = jnp.where(first, near[8:], v[8:])
            state[24 * kind : 24 * kind + 24, :] = jnp.concatenate([top, mid, low])


def inner_end(half, left, right, drive, mine, theirs, keep, send, frame):
    core, chip = place()
    first = core == 0

    @pl.when(chip > 0)
    def _():
        count = half // 8 - 2
        mid = left.shape[1] * 4 // (4 * count + 3)
        parts = left[...], right[...]

        def across(begin, end, change=same):
            return jnp.concatenate([change(p[:, begin:end]) for p in parts], axis=1)

        whole = [across(i * mid, i * mid + mid) for i in range(count)]
        part = across(count * mid, left.shape[1], unfolded)
        upper = [*whole, part]
        lower = [pltpu.roll(part, 2, 0), *whole]
        rows = jnp.concatenate([jnp.where(first, u, v) for u, v in zip(upper, lower)])
        frame[...] = rows
        current = pltpu.roll(jnp.concatenate([rows, rows[:8]]), CUT, 0)
        into = pl.ds(pl.multiple_of(8 * (1 - core), 8), half)
        d_a, d_b = picked(first, mine[into, :], theirs[into, :])
        d = drive[pl.ds(inner_row(half, core), half), :]
        e_a, e_b = chain(current, d_a, d_b, d)
        put_ends(first, e_a[8 : half - 8], e_b[8 : half - 8], keep, send)


def gather_kernel(half, ends_left, ends_right, middle, outer, near_keep, near_send, keep, send):
    core, chip = place()
    first = core == 0
    near = half - 16

    @pl.when(chip == 0)
    def _():
        def rows(kind, begin, size):
            into = pl.ds(half * kind + begin, size)
            return jnp.concatenate([ends_left[into, :], ends_right[into, :]], axis=1)

        def known(kind):
            two = [field(middle, kind, 2, 8 * i, 8)[...] for i in range(2)]
            last = [field(outer, kind, 2, 8 * i, 8)[...] for i in range(2)]
            beside = [rows(kind, 0, 8), rows(kind, half - 8, 8)]
            return jnp.concatenate(
                [
                    rows(kind, 8, near),
                    jnp.where(first, mixed(two[1], beside[0]), mixed(beside[1], two[0])),
                    jnp.where(first, mixed(last[1], two[0]), mixed(two[1], last[0])),
                ]
            )

        put_ends(first, known(0), known(1), keep, send)

    @pl.when(chip > 0)
    def _():
        keep[0:near, :] = near_keep[...]
        send[0:near, :] = near_send[...]


def put_ends(first, e_a, e_b, keep, send):
    kept, sent = picked(first, e_a, e_b)
    keep[...] = kept
    send[...] = sent


def middle_end(half, inner, middle, drive, mine, theirs, keep, send, current):
    core, chip = place()
    first = core == 0
    last = inner.shape[0] - 16

    @pl.when((chip > 0) & first)
    def _():
        current[...] = pltpu.roll(jnp.concatenate([middle[...], inner[0:16, :]]), CUT, 0)

    @pl.when((chip > 0) & (core == 1))
    def _():
        rows = jnp.concatenate([inner[last : last + 16, :], middle[...]])
        current[...] = pltpu.roll(rows, 24 - CUT, 0)

    @pl.when(chip > 0)
    def _():
        rows = pl.ds(pl.multiple_of((half - 16) * core, 8), 24)
        d_a, d_b = picked(first, mine[rows, :], theirs[rows, :])
        d = drive[pl.ds(pl.multiple_of((2 * half - 24) * core, 8), 24), :]
        e_a, e_b = chain(current[...], d_a, d_b, d)
        put_ends(first, e_a[8:16], e_b[8:16], keep, send)


def outer_end(inner, middle, outer, state, keep, send, current):
    core, chip = place()
    first = core == 0
    last = inner.shape[0] - 8

    @pl.when((chip > 0) & first)
    def _():
        part = pltpu.roll(unfolded(outer[...]), 2, 0)
        rows = jnp.concatenate([part, middle[...], inner[0:8, :]])
        current[...] = pltpu.roll(rows, CUT, 0)

    @pl.when((chip > 0) & (core == 1))
    def _():
        rows = jnp.concatenate([inner[last : last + 8, :], middle[...], unfolded(outer[...])])
        current[...] = pltpu.roll(rows, 24 - CUT, 0)

    @pl.when(chip > 0)
    def _():
        d_a, d_b, d = (field(state, kind, 3, 0, 24)[...] for kind in range(3))
        inside = ~(at_edge(core) & (sublane(d) // 8 == 2 * core))
        e_a = coarse_of(current[...], around(current[...]), d) + d_a
        e_a = jnp.where(inside, e_a, 0.0)
        mid = e_a[8:16]
        width = mid.shape[1]
        beside = pltpu.roll(mid, 1, 1) + pltpu.roll(mid, width - 1, 1)
        upright = pltpu.roll(e_a, 1, 0)[8:16] + pltpu.roll(e_a, 23, 0)[8:16]
        e_b = coarse_of(mid, upright + beside, d[8:16]) + d_b[8:16]
        put_ends(first, mid, e_b, keep, send)


def write_kernel(half, last, *refs):
    pieces, out, sems = refs[: 1 if last else 5], refs[-2], refs[-1]
    core, chip = place()

    def copy_all(order):
        copies = []
        for i, (mine, part, source, begin, size) in enumerate(order):
            upper = (16, 8, 0)[part]
            lower = (half, 2 * half - 16, 2 * half - 8)[part]
            row = pl.multiple_of(jnp.where((core == 0) == mine, upper, lower), 8)
            copy = pltpu.make_async_copy(
                pieces[source].at[pl.ds(begin, size), :],
                out.at[0, pl.ds(row, size), :],
                sems.at[i],
            )
            copy.start()
            copies.append(copy)
        for copy in copies:
            copy.wait()

    if last:

        @pl.when(chip > 0)
        def _():
            copy_all(((False, 2, 0, 0, 8),))

    else:
        near = half - 16

        @pl.when(chip == 0)
        def _():
            parts = ((0, 0, near), (1, near, 8), (2, near + 8, 8))
            copy_all(
                [(mine, part, source, *rows) for mine, source in ((True, 0), (False, 1)) for part, *rows in parts]
            )

        @pl.when(chip > 0)
        def _():
            copy_all(
                (
                    (True, 0, 0, 0, near),
                    (False, 0, 1, 0, near),
                    (True, 1, 2, 0, 8),
                    (False, 1, 3, 0, 8),
                    (True, 2, 4, 0, 8),
                )
            )


def written(half, pieces, shape, into=None):
    vmem, anywhere = pl.BlockSpec(memory_space=pltpu.VMEM), pl.BlockSpec(memory_space=pl.ANY)
    extra = () if into is None else (into,)
    return pl.pallas_call(
        functools.partial(write_kernel, half, into is not None),
        out_shape=jax.ShapeDtypeStruct(shape, jnp.float32),
        in_specs=[vmem] * len(pieces) + [anywhere] * len(extra),
        out_specs=anywhere,
        input_output_aliases={len(pieces): 0} if extra else {},
        scratch_shapes=[pltpu.SemaphoreType.DMA((6,))],
        compiler_params=pltpu.CompilerParams(vmem_limit_bytes=16 << 20),
    )(*pieces, *extra)


def after(value, earlier):
    return lax.optimization_barrier((value, earlier))[0]


def masked_update(update, v, drive, inside):
    wide = (
        jnp.roll(v, 1, axis=0) + jnp.roll(v, -1, axis=0)
    ) + (jnp.roll(v, 1, axis=1) + jnp.roll(v, -1, axis=1))
    return jnp.where(inside, update(v, wide, drive), 0.0)


def long_chain(own, drive):
    height = own.shape[0]
    half = height // 2
    groups, slices, rows = (lax.axis_size(a) for a in AXES)
    t, r = lax.axis_index("tm"), lax.axis_index("rows")
    core, chip = t % 2, t // 2
    first = core == 0
    away = outward(groups, rows)

    def cut(field, start, size):
        return lax.dynamic_slice_in_dim(field, start, size, axis=0)

    other = routed(own, partner)
    s_a, s_b = picked(first, own, other)
    edge = core * (height - WIDE)
    got = routed(jnp.concatenate([cut(f, edge, WIDE) for f in (s_a, s_b, drive)]), away)

    def sided(body, outer, inner):
        return jnp.where(
            first,
            jnp.concatenate([outer, body, inner]),
            jnp.concatenate([inner, body, outer]),
        )

    def window(field, place):
        body = cut(field, core * half, half)
        inner = cut(field, jnp.where(first, half, half - WIDE), WIDE)
        return sided(body, got[place * WIDE : (place + 1) * WIDE], inner)

    w_a, w_b, w_d = (window(f, i) for i, f in enumerate((s_a, s_b, drive)))
    row = lax.broadcasted_iota(jnp.int32, (half + 2 * WIDE, 1), 0)
    row = row + r * height + core * half - WIDE
    inside = (row >= 0) & (row < rows * height)
    w_a, w_b = jnp.where(inside, w_a, 0.0), jnp.where(inside, w_b, 0.0)

    def delta(v):
        fine = v
        for _ in range(FINE):
            fine = masked_update(fine_of, fine, w_d, inside)
        return fine - masked_update(coarse_of, v, w_d, inside)

    d_a, d_b = delta(w_a), delta(w_b)

    def both(v):
        e_a = masked_update(coarse_of, v, w_d, inside) + d_a
        return e_a, masked_update(coarse_of, e_a, w_d, inside) + d_b

    def extended(v):
        last = WIDE + half - 2
        inner = routed(cut(v, jnp.where(first, last, WIDE), 2), partner)
        outer = routed(cut(v, jnp.where(first, WIDE, last), 2), away)
        return sided(v[WIDE : WIDE + half], outer, inner)

    e_a, e_b = both(w_a)
    for stage in range(slices // 2 - 1):
        moved = e_b[WIDE - 2 : WIDE + half + 2] if stage == 0 else extended(e_b)
        arrived = routed(moved, stage_swap(stage))
        current = jnp.pad(arrived, ((WIDE - 2, WIDE - 2), (0, 0)))
        n_a, n_b = both(jnp.where(inside, current, 0.0))
        here = chip == stage + 1
        e_a, e_b = jnp.where(here, n_a, e_a), jnp.where(here, n_b, e_b)

    kept, sent = picked(first, e_a[WIDE : WIDE + half], e_b[WIDE : WIDE + half])
    back = routed(sent, partner)
    return jnp.concatenate(picked(first, kept, back))[None]


def on_device(starts, drive):
    own = starts[0]
    if lax.axis_size("tm") != 4:
        return long_chain(own, drive)
    return two_chips(starts, drive)


def two_chips(starts, drive):
    _, height, width = starts.shape
    half = height // 2
    groups, rows = lax.axis_size("groups"), lax.axis_size("rows")
    vmem = pl.BlockSpec(memory_space=pltpu.VMEM)

    other = routed(starts[0], partner)
    own, held, mine = pl.pallas_call(
        functools.partial(load_kernel, half),
        out_shape=[
            jax.ShapeDtypeStruct((size, width), jnp.float32) for size in (height, height, height)
        ],
        in_specs=[pl.BlockSpec(memory_space=pltpu.HBM)] * 2,
        out_specs=[vmem] * 3,
        scratch_shapes=[pltpu.SemaphoreType.DMA((6,))],
        compiler_params=pltpu.CompilerParams(vmem_limit_bytes=50 << 20),
        cost_estimate=pl.CostEstimate(
            flops=60 * 24 * width, bytes_accessed=16 * height * width, transcendentals=0
        ),
        name="load",
    )(starts, drive)
    mid = width // 2
    packed = mid * (half // 8 - 2) + mid * 3 // 4
    sent_l, ends_l = compute(
        functools.partial(inner_kernel, half, 0),
        [(8, packed), (height, mid)],
        (own, other, held, mine),
    )
    here_l = routed(sent_l, stage_swap(0))
    sent_r, ends_r, edge = compute(
        functools.partial(inner_kernel, half, 1),
        [(8, packed), (height, mid), (8, width * 9 // 4)],
        (own, other, held, after(mine, sent_l)),
    )
    here_r = routed(sent_r, stage_swap(0))
    got = routed(edge, outward(groups, rows))
    sent_2, ends_2, delta_own = compute(
        functools.partial(middle_kernel, half),
        [(8, width), (32, width), (half + WIDE, width)],
        (own, other, after(held, sent_r)),
    )
    here_2 = routed(sent_2, stage_swap(0))
    (delta_other,) = compute(
        functools.partial(state_kernel, half), [(half + WIDE, width)], (other, after(held, sent_2))
    )
    sent_3, ends_3 = compute(
        functools.partial(outer_kernel, half),
        [(8, width * 3 // 4), (32, width)],
        (own, other, after(held, delta_other), got),
    )
    here_3 = routed(sent_3, stage_swap(0))
    (state_3,) = compute(
        functools.partial(outer_state_kernel, half),
        [(3 * 24, width)],
        (own, other, held, got, delta_own, delta_other, ends_3),
    )
    near_keep, near_send, frame = compute(
        functools.partial(inner_end, half),
        [(half - 16, width), (half - 16, width), (half - 8, width)],
        (here_l, here_r, held, delta_own, after(delta_other, state_3)),
    )
    keep_1, send_1 = compute(
        functools.partial(gather_kernel, half),
        [(half, width)] * 2,
        (ends_l, ends_r, ends_2, ends_3, near_keep, near_send),
    )
    back_1 = routed(send_1, partner)
    keep_2, send_2 = compute(
        functools.partial(middle_end, half),
        [(8, width)] * 2,
        (frame, here_2, held, delta_own, delta_other),
        scratch_shapes=[pltpu.VMEM((24, width), jnp.float32)],
    )
    back_2 = routed(send_2, partner)
    keep_3, send_3 = compute(
        outer_end,
        [(8, width)] * 2,
        (frame, here_2, here_3, after(state_3, keep_2)),
        scratch_shapes=[pltpu.VMEM((24, width), jnp.float32)],
    )
    back_3 = routed(send_3, partner)
    out = written(half, (keep_1, back_1, keep_2, back_2, keep_3), starts.shape)
    return written(half, (back_3,), starts.shape, into=out)


def solution(mesh):
    in_specs = (P(("groups", "tm"), "rows", None), P("rows", None))
    out_specs = P(("groups", "tm"), "rows", None)
    return jax.shard_map(
        on_device, mesh=mesh, in_specs=in_specs, out_specs=out_specs, check_vma=False
    )
```

```python
import functools

import jax
import jax.numpy as jnp
from jax import lax
from jax.experimental import pallas as pl
from jax.experimental.pallas import tpu as pltpu
from jax.sharding import PartitionSpec as P


FINE = 3
WIDE = 8
CUT = 4


diffusion = 2.0
step_fine = 0.1
coarse_step = FINE * step_fine
damping = 1.0 + 4.0 * diffusion * coarse_step

AXES = ("groups", "tm", "rows")


def routed(block, route):
    groups, slices, rows = (lax.axis_size(a) for a in AXES)
    pairs = []
    for g in range(groups):
        for t in range(slices):
            for r in range(rows):
                to_g, to_t, to_r = route(g, t, r)
                source = (g * slices + t) * rows + r
                pairs.append((source, (to_g * slices + to_t) * rows + to_r))
    return lax.ppermute(block, AXES, pairs)


def partner(g, t, r):
    return g, t ^ 1, r


def outward(groups, rows):
    def route(g, t, r):
        to_r = r + 1 if t & 1 else r - 1
        if 0 <= to_r < rows:
            return g, t ^ 1, to_r
        other = g ^ 1
        return (other, t, r) if other < groups else (g, t, r)

    return route


def stage_swap(stage):
    def route(g, t, r):
        chip = t // 2
        if chip == stage:
            return g, t + 2, r
        if chip == stage + 1:
            return g, t - 2, r
        return g, t, r

    return route


def around(v):
    height, width = v.shape
    return (pltpu.roll(v, 1, 0) + pltpu.roll(v, height - 1, 0)) + (
        pltpu.roll(v, 1, 1) + pltpu.roll(v, width - 1, 1)
    )


def fine_of(v, nsum, drive):
    return (
        step_fine * diffusion * nsum
        + v * ((1.0 + step_fine - 4.0 * step_fine * diffusion) - step_fine * (v * v))
        + step_fine * drive
    )


def coarse_of(v, nsum, drive):
    scale = coarse_step / damping
    return (
        scale * diffusion * nsum
        + v * ((1.0 + coarse_step) / damping - scale * (v * v))
        + scale * drive
    )


def compute(kernel, outs, args, **kwargs):
    shapes = [jax.ShapeDtypeStruct(o, jnp.float32) for o in outs]
    vmem = pl.BlockSpec(memory_space=pltpu.VMEM)
    return pl.pallas_call(
        kernel,
        out_shape=shapes,
        in_specs=[vmem] * len(args),
        out_specs=[vmem] * len(outs),
        compiler_params=pltpu.CompilerParams(vmem_limit_bytes=16 << 20),
        **kwargs,
    )(*args)


def same(v):
    return v


def start_of(v, drive, kept=same):
    nsum = around(v)
    coarse = kept(coarse_of(v, nsum, drive))
    fine = kept(fine_of(v, nsum, drive))
    for _ in range(FINE - 1):
        fine = kept(fine_of(fine, around(fine), drive))
    return fine, coarse


def ends_of(first, mine, theirs, drive, kept=same):
    f_a, f_b = picked(first, mine[0], theirs[0])
    g_a, g_b = picked(first, mine[1], theirs[1])
    e_a = g_a + (f_a - g_a)
    e_b = kept(coarse_of(e_a, around(e_a), drive)) + (f_b - g_b)
    return e_a, e_b


def chain(current, d_a, d_b, drive, kept=same):
    e_a = kept(coarse_of(current, around(current), drive)) + d_a
    e_b = kept(coarse_of(e_a, around(e_a), drive)) + d_b
    return e_a, e_b


def picked(first, own, other):
    return jnp.where(first, own, other), jnp.where(first, other, own)


def field(ref, kind, kinds, start, size):
    height = ref.shape[0] // kinds
    return ref.at[pl.ds(pl.multiple_of(kind * height + start, 8), size), :]


def mixed(upper, lower):
    row = lax.broadcasted_iota(jnp.int32, upper.shape, 0)
    return jnp.where(row < CUT, upper, lower)


def sublane(v):
    return lax.broadcasted_iota(jnp.int32, v.shape, 0)


def folded(v):
    width = v.shape[1]
    half, quarter = width // 2, width // 4
    four = mixed(v[:, :half], pltpu.roll(v[:, half:], 4, 0))
    row = sublane(four[:, :quarter])
    two = pltpu.roll(v[:, :quarter], 4, 0)
    for i, shift in ((1, 6), (2, 0), (3, 2)):
        part = v[:, i * quarter : (i + 1) * quarter]
        part = pltpu.roll(part, shift, 0) if shift else part
        two = jnp.where(row < 2 * i, two, part)
    return jnp.concatenate([four, two], axis=1)


def unfolded(v):
    half = v.shape[1] * 2 // 3
    four, two = v[:, :half], v[:, half:]
    low = [pltpu.roll(two, 4, 0), pltpu.roll(two, 2, 0), two, pltpu.roll(two, 6, 0)]
    return mixed(
        jnp.concatenate([four, pltpu.roll(four, 4, 0)], axis=1),
        jnp.concatenate(low, axis=1),
    )


def halved(v):
    half = v.shape[1] // 2
    return mixed(v[:, :half], pltpu.roll(v[:, half:], 4, 0))


def unhalved(v):
    return jnp.concatenate([v, pltpu.roll(v, 4, 0)], axis=1)


def place():
    t = lax.axis_index("tm")
    return t % 2, t // 2


def at_edge(core):
    r, rows = lax.axis_index("rows"), lax.axis_size("rows")
    return ((core == 0) & (r == 0)) | ((core == 1) & (r == rows - 1))


def inner_row(half, core):
    return pl.multiple_of(8 + (half - 16) * core, 8)


def middle_row(half, core):
    return pl.multiple_of((2 * half - 16) * core, 8)


def outer_row(half, core):
    return pl.multiple_of((2 * half - WIDE) * core, 8)


def load_kernel(half, starts, drive, own, held, inner, sems):
    core, chip = place()
    copies = []
    for i, (row, size) in enumerate(((8, 2 * half - 16), (0, 8), (2 * half - 8, 8))):
        rows = pl.ds(row, size)
        pair = (
            pltpu.make_async_copy(starts.at[0, rows, :], own.at[rows, :], sems.at[2 * i]),
            pltpu.make_async_copy(drive.at[rows, :], held.at[rows, :], sems.at[2 * i + 1]),
        )
        for copy in pair:
            copy.start()
        copies.append(pair)

    for copy in copies[0]:
        copy.wait()

    @pl.when(chip == 0)
    def _():
        rows = pl.ds(inner_row(half, core), half)
        fine, coarse = start_of(own[rows, :], held[rows, :])
        inner[0:half, :] = fine
        inner[half : 2 * half, :] = coarse

    for copy in (*copies[1], *copies[2]):
        copy.wait()


def inner_kernel(half, side, own, other, drive, mine, sent, ends, edge=None):
    core, chip = place()
    first = core == 0
    width = drive.shape[1]
    mid = width // 2

    def columns(ref, rows):
        if side == 0:
            parts = ref[rows, width - 128 :], ref[rows, : mid + 128]
        else:
            parts = ref[rows, mid - 128 :], ref[rows, :128]
        return jnp.concatenate(parts, axis=1)

    @pl.when(chip == 0)
    def _():
        rows = pl.ds(inner_row(half, core), half)
        d = columns(drive, rows)
        theirs = start_of(columns(other, rows), d)
        known = columns(mine, pl.ds(0, half)), columns(mine, pl.ds(half, half))
        e_a, e_b = ends_of(first, known, theirs, d)
        e_a, e_b = e_a[:, 128:-128], e_b[:, 128:-128]
        frame = pltpu.roll(e_b, half - CUT, 0)
        count = half // 8 - 2
        whole = [
            jnp.where(first, frame[8 * i : 8 * i + 8], frame[8 * i + 8 : 8 * i + 16])
            for i in range(count)
        ]
        part = jnp.where(
            first, frame[8 * count : 8 * count + 8], pltpu.roll(frame[:8], 4, 0)
        )
        sent[...] = jnp.concatenate([*whole, halved(part)], axis=1)
        ends[0:half, :] = e_a
        ends[half : 2 * half, :] = e_b

    if edge is not None:
        rows = pl.ds(outer_row(half, core), 8)
        a, b = picked(first, own[rows, :], other[rows, :])
        fields = (jnp.where(first, v, pltpu.roll(v, 6, 0)) for v in (a, b, drive[rows, :]))
        edge[...] = jnp.concatenate([folded(v) for v in fields], axis=1)


def middle_kernel(half, own, other, drive, sent, ends, delta):
    core, chip = place()
    first = core == 0

    @pl.when(chip == 0)
    def _():
        rows = pl.ds(middle_row(half, core), 16)
        d = drive[rows, :]
        mine, theirs = start_of(own[rows, :], d), start_of(other[rows, :], d)
        e_a, e_b = ends_of(first, mine, theirs, d)
        sent[...] = pltpu.roll(e_b, 16 - CUT, 0)[:8]
        ends[0:16, :] = e_a
        ends[16:32, :] = e_b

    @pl.when(chip > 0)
    def _():
        rows = receiver_rows(half, core)
        fine, coarse = start_of(own[rows, :], drive[rows, :])
        delta[...] = fine - coarse


def receiver_rows(half, core):
    return pl.ds(pl.multiple_of((half - WIDE) * core, 8), half + WIDE)


def state_kernel(half, other, drive, theirs):
    core, chip = place()

    @pl.when(chip > 0)
    def _():
        rows = receiver_rows(half, core)
        fine, coarse = start_of(other[rows, :], drive[rows, :])
        theirs[...] = fine - coarse


def outer_window(half, own, other, drive, got):
    core, _ = place()
    first = core == 0
    rows = pl.ds(outer_row(half, core), 8)
    a, b = picked(first, own[rows, :], other[rows, :])
    near = (a, b, drive[rows, :])
    size = got.shape[1] // 3
    far = [unfolded(got[:, i * size : (i + 1) * size]) for i in range(3)]
    far = [jnp.where(first, pltpu.roll(v, 2, 0), v) for v in far]
    upper = [jnp.where(first, f, n) for f, n in zip(far, near)]
    lower = [jnp.where(first, n, f) for f, n in zip(far, near)]
    a, b, d = (jnp.concatenate(p) for p in zip(upper, lower))
    inside = ~(at_edge(core) & (sublane(a) // 8 == core))

    def kept(v):
        return jnp.where(inside, v, 0.0)

    return kept(a), kept(b), d, kept


def outer_kernel(half, own, other, drive, got, sent, ends):
    core, chip = place()
    first = core == 0
    a, b, d, kept = outer_window(half, own, other, drive, got)
    f_a, g_a = start_of(a, d, kept)

    @pl.when(chip == 0)
    def _():
        f_b, g_b = start_of(b, d, kept)
        e_a = g_a + (f_a - g_a)
        e_b = kept(coarse_of(e_a, around(e_a), d)) + (f_b - g_b)
        frame = pltpu.roll(e_b, 16 - CUT, 0)[:8]
        sent[...] = folded(jnp.where(first, pltpu.roll(frame, 6, 0), frame))
        ends[0:16, :] = e_a
        ends[16:32, :] = e_b

    @pl.when(chip > 0)
    def _():
        ends[0:16, :] = f_a - g_a


def outer_state_kernel(half, own, other, drive, got, mine, theirs, ends, state):
    core, chip = place()
    first = core == 0

    @pl.when(chip > 0)
    def _():
        _, b, d, kept = outer_window(half, own, other, drive, got)
        f_b, g_b = start_of(b, d, kept)
        rows = pl.ds(pl.multiple_of((half - WIDE) * core, 8), 16)
        before = picked(first, mine[rows, :], theirs[rows, :])
        d_rows = pl.ds(pl.multiple_of((2 * half - 16) * core, 8), 16)
        fields = zip((ends[0:16, :], f_b - g_b, d), (*before, drive[d_rows, :]))
        for kind, (v, near) in enumerate(fields):
            top = jnp.where(first, v[:8], near[:8])
            mid = jnp.where(first, mixed(v[8:], near[:8]), mixed(near[8:], v[:8]))
            low = jnp.where(first, near[8:], v[8:])
            state[24 * kind : 24 * kind + 24, :] = jnp.concatenate([top, mid, low])


def boundary_kernel(left, right, rows):
    size = rows.shape[1] // 2
    start = left.shape[1] - size
    rows[:, :size] = left[:, start:]
    rows[:, size:] = right[:, start:]


def inner_end(half, left, right, beyond, drive, mine, theirs, keep, send, frame):
    core, chip = place()
    first = core == 0

    @pl.when(chip > 0)
    def _():
        count = half // 8 - 2
        mid = left.shape[1] * 2 // (2 * count + 1)
        parts = left[...], right[...]

        def across(begin, end, change=same):
            return jnp.concatenate([change(p[:, begin:end]) for p in parts], axis=1)

        whole = [across(i * mid, i * mid + mid) for i in range(count)]
        near = across(count * mid, left.shape[1], unhalved)
        far = [beyond[:, : mid // 2], beyond[:, mid // 2 :]]
        far = jnp.concatenate([unhalved(v) for v in far], axis=1)
        top, low = picked(first, near, far)
        part = mixed(top, pltpu.roll(low, 4, 0))
        upper = [*whole, part]
        lower = [part, *whole]
        rows = jnp.concatenate([jnp.where(first, u, v) for u, v in zip(upper, lower)])
        frame[...] = rows
        current = pltpu.roll(jnp.concatenate([rows, rows[:8]]), CUT, 0)
        into = pl.ds(pl.multiple_of(8 * (1 - core), 8), half)
        d_a, d_b = picked(first, mine[into, :], theirs[into, :])
        d = drive[pl.ds(inner_row(half, core), half), :]
        e_a, e_b = chain(current, d_a, d_b, d)
        put_ends(first, e_a[8 : half - 8], e_b[8 : half - 8], keep, send)


def gather_kernel(half, ends_left, ends_right, middle, outer, near_keep, near_send, keep, send):
    core, chip = place()
    first = core == 0
    near = half - 16

    @pl.when(chip == 0)
    def _():
        def rows(kind, begin, size):
            into = pl.ds(half * kind + begin, size)
            return jnp.concatenate([ends_left[into, :], ends_right[into, :]], axis=1)

        def known(kind):
            two = [field(middle, kind, 2, 8 * i, 8)[...] for i in range(2)]
            last = [field(outer, kind, 2, 8 * i, 8)[...] for i in range(2)]
            beside = [rows(kind, 0, 8), rows(kind, half - 8, 8)]
            return jnp.concatenate(
                [
                    rows(kind, 8, near),
                    jnp.where(first, mixed(two[1], beside[0]), mixed(beside[1], two[0])),
                    jnp.where(first, mixed(last[1], two[0]), mixed(two[1], last[0])),
                ]
            )

        put_ends(first, known(0), known(1), keep, send)

    @pl.when(chip > 0)
    def _():
        keep[0:near, :] = near_keep[...]
        send[0:near, :] = near_send[...]


def put_ends(first, e_a, e_b, keep, send):
    kept, sent = picked(first, e_a, e_b)
    keep[...] = kept
    send[...] = sent


def middle_end(half, inner, middle, drive, mine, theirs, keep, send, current):
    core, chip = place()
    first = core == 0
    last = inner.shape[0] - 16

    @pl.when((chip > 0) & first)
    def _():
        current[...] = pltpu.roll(jnp.concatenate([middle[...], inner[0:16, :]]), CUT, 0)

    @pl.when((chip > 0) & (core == 1))
    def _():
        rows = jnp.concatenate([inner[last : last + 16, :], middle[...]])
        current[...] = pltpu.roll(rows, 24 - CUT, 0)

    @pl.when(chip > 0)
    def _():
        rows = pl.ds(pl.multiple_of((half - 16) * core, 8), 24)
        d_a, d_b = picked(first, mine[rows, :], theirs[rows, :])
        d = drive[pl.ds(pl.multiple_of((2 * half - 24) * core, 8), 24), :]
        e_a, e_b = chain(current[...], d_a, d_b, d)
        put_ends(first, e_a[8:16], e_b[8:16], keep, send)


def outer_end(inner, middle, outer, state, keep, send, current):
    core, chip = place()
    first = core == 0
    last = inner.shape[0] - 8

    @pl.when((chip > 0) & first)
    def _():
        part = pltpu.roll(unfolded(outer[...]), 2, 0)
        rows = jnp.concatenate([part, middle[...], inner[0:8, :]])
        current[...] = pltpu.roll(rows, CUT, 0)

    @pl.when((chip > 0) & (core == 1))
    def _():
        rows = jnp.concatenate([inner[last : last + 8, :], middle[...], unfolded(outer[...])])
        current[...] = pltpu.roll(rows, 24 - CUT, 0)

    @pl.when(chip > 0)
    def _():
        d_a, d_b, d = (field(state, kind, 3, 0, 24)[...] for kind in range(3))
        inside = ~(at_edge(core) & (sublane(d) // 8 == 2 * core))
        e_a = coarse_of(current[...], around(current[...]), d) + d_a
        e_a = jnp.where(inside, e_a, 0.0)
        mid = e_a[8:16]
        width = mid.shape[1]
        beside = pltpu.roll(mid, 1, 1) + pltpu.roll(mid, width - 1, 1)
        upright = pltpu.roll(e_a, 1, 0)[8:16] + pltpu.roll(e_a, 23, 0)[8:16]
        e_b = coarse_of(mid, upright + beside, d[8:16]) + d_b[8:16]
        put_ends(first, mid, e_b, keep, send)


def write_kernel(half, last, *refs):
    pieces, out, sems = refs[: 1 if last else 5], refs[-2], refs[-1]
    core, chip = place()

    def copy_all(order):
        copies = []
        for i, (mine, part, source, begin, size) in enumerate(order):
            upper = (16, 8, 0)[part]
            lower = (half, 2 * half - 16, 2 * half - 8)[part]
            row = pl.multiple_of(jnp.where((core == 0) == mine, upper, lower), 8)
            copy = pltpu.make_async_copy(
                pieces[source].at[pl.ds(begin, size), :],
                out.at[0, pl.ds(row, size), :],
                sems.at[i],
            )
            copy.start()
            copies.append(copy)
        for copy in copies:
            copy.wait()

    if last:

        @pl.when(chip > 0)
        def _():
            copy_all(((False, 2, 0, 0, 8),))

    else:
        near = half - 16

        @pl.when(chip == 0)
        def _():
            parts = ((0, 0, near), (1, near, 8), (2, near + 8, 8))
            copy_all(
                [(mine, part, source, *rows) for mine, source in ((True, 0), (False, 1)) for part, *rows in parts]
            )

        @pl.when(chip > 0)
        def _():
            copy_all(
                (
                    (True, 0, 0, 0, near),
                    (False, 0, 1, 0, near),
                    (True, 1, 2, 0, 8),
                    (False, 1, 3, 0, 8),
                    (True, 2, 4, 0, 8),
                )
            )


def written(half, pieces, shape, into=None):
    vmem, anywhere = pl.BlockSpec(memory_space=pltpu.VMEM), pl.BlockSpec(memory_space=pl.ANY)
    extra = () if into is None else (into,)
    return pl.pallas_call(
        functools.partial(write_kernel, half, into is not None),
        out_shape=jax.ShapeDtypeStruct(shape, jnp.float32),
        in_specs=[vmem] * len(pieces) + [anywhere] * len(extra),
        out_specs=anywhere,
        input_output_aliases={len(pieces): 0} if extra else {},
        scratch_shapes=[pltpu.SemaphoreType.DMA((6,))],
        compiler_params=pltpu.CompilerParams(vmem_limit_bytes=16 << 20),
    )(*pieces, *extra)


def after(value, earlier):
    return lax.optimization_barrier((value, earlier))[0]


def masked_update(update, v, drive, inside):
    wide = (
        jnp.roll(v, 1, axis=0) + jnp.roll(v, -1, axis=0)
    ) + (jnp.roll(v, 1, axis=1) + jnp.roll(v, -1, axis=1))
    return jnp.where(inside, update(v, wide, drive), 0.0)


def long_chain(own, drive):
    height = own.shape[0]
    half = height // 2
    groups, slices, rows = (lax.axis_size(a) for a in AXES)
    t, r = lax.axis_index("tm"), lax.axis_index("rows")
    core, chip = t % 2, t // 2
    first = core == 0
    away = outward(groups, rows)

    def cut(field, start, size):
        return lax.dynamic_slice_in_dim(field, start, size, axis=0)

    other = routed(own, partner)
    s_a, s_b = picked(first, own, other)
    edge = core * (height - WIDE)
    got = routed(jnp.concatenate([cut(f, edge, WIDE) for f in (s_a, s_b, drive)]), away)

    def sided(body, outer, inner):
        return jnp.where(
            first,
            jnp.concatenate([outer, body, inner]),
            jnp.concatenate([inner, body, outer]),
        )

    def window(field, place):
        body = cut(field, core * half, half)
        inner = cut(field, jnp.where(first, half, half - WIDE), WIDE)
        return sided(body, got[place * WIDE : (place + 1) * WIDE], inner)

    w_a, w_b, w_d = (window(f, i) for i, f in enumerate((s_a, s_b, drive)))
    row = lax.broadcasted_iota(jnp.int32, (half + 2 * WIDE, 1), 0)
    row = row + r * height + core * half - WIDE
    inside = (row >= 0) & (row < rows * height)
    w_a, w_b = jnp.where(inside, w_a, 0.0), jnp.where(inside, w_b, 0.0)

    def delta(v):
        fine = v
        for _ in range(FINE):
            fine = masked_update(fine_of, fine, w_d, inside)
        return fine - masked_update(coarse_of, v, w_d, inside)

    d_a, d_b = delta(w_a), delta(w_b)

    def both(v):
        e_a = masked_update(coarse_of, v, w_d, inside) + d_a
        return e_a, masked_update(coarse_of, e_a, w_d, inside) + d_b

    def extended(v):
        last = WIDE + half - 2
        inner = routed(cut(v, jnp.where(first, last, WIDE), 2), partner)
        outer = routed(cut(v, jnp.where(first, WIDE, last), 2), away)
        return sided(v[WIDE : WIDE + half], outer, inner)

    e_a, e_b = both(w_a)
    for stage in range(slices // 2 - 1):
        moved = e_b[WIDE - 2 : WIDE + half + 2] if stage == 0 else extended(e_b)
        arrived = routed(moved, stage_swap(stage))
        current = jnp.pad(arrived, ((WIDE - 2, WIDE - 2), (0, 0)))
        n_a, n_b = both(jnp.where(inside, current, 0.0))
        here = chip == stage + 1
        e_a, e_b = jnp.where(here, n_a, e_a), jnp.where(here, n_b, e_b)

    kept, sent = picked(first, e_a[WIDE : WIDE + half], e_b[WIDE : WIDE + half])
    back = routed(sent, partner)
    return jnp.concatenate(picked(first, kept, back))[None]


def on_device(starts, drive):
    own = starts[0]
    if lax.axis_size("tm") != 4:
        return long_chain(own, drive)
    return two_chips(starts, drive)


def two_chips(starts, drive):
    _, height, width = starts.shape
    half = height // 2
    groups, rows = lax.axis_size("groups"), lax.axis_size("rows")
    vmem = pl.BlockSpec(memory_space=pltpu.VMEM)

    other = routed(starts[0], partner)
    own, held, mine = pl.pallas_call(
        functools.partial(load_kernel, half),
        out_shape=[
            jax.ShapeDtypeStruct((size, width), jnp.float32) for size in (height, height, height)
        ],
        in_specs=[pl.BlockSpec(memory_space=pltpu.HBM)] * 2,
        out_specs=[vmem] * 3,
        scratch_shapes=[pltpu.SemaphoreType.DMA((6,))],
        compiler_params=pltpu.CompilerParams(vmem_limit_bytes=50 << 20),
        cost_estimate=pl.CostEstimate(
            flops=60 * 24 * width, bytes_accessed=16 * height * width, transcendentals=0
        ),
        name="load",
    )(starts, drive)
    mid = width // 2
    packed = mid * (half // 8 - 2) + mid // 2
    sent_l, ends_l = compute(
        functools.partial(inner_kernel, half, 0),
        [(8, packed), (height, mid)],
        (own, other, held, mine),
    )
    here_l = routed(sent_l, stage_swap(0))
    sent_r, ends_r, edge = compute(
        functools.partial(inner_kernel, half, 1),
        [(8, packed), (height, mid), (8, width * 9 // 4)],
        (own, other, held, after(mine, sent_l)),
    )
    here_r = routed(sent_r, stage_swap(0))
    got = routed(edge, outward(groups, rows))
    sent_2, ends_2, delta_own = compute(
        functools.partial(middle_kernel, half),
        [(8, width), (32, width), (half + WIDE, width)],
        (own, other, after(held, sent_r)),
    )
    here_2 = routed(sent_2, stage_swap(0))
    (delta_other,) = compute(
        functools.partial(state_kernel, half), [(half + WIDE, width)], (other, after(held, sent_2))
    )
    sent_3, ends_3 = compute(
        functools.partial(outer_kernel, half),
        [(8, width * 3 // 4), (32, width)],
        (own, other, after(held, delta_other), got),
    )
    here_3 = routed(sent_3, stage_swap(0))
    (rows_1,) = compute(boundary_kernel, [(8, mid)], (here_l, after(here_r, sent_3)))
    beyond = routed(rows_1, partner)
    (state_3,) = compute(
        functools.partial(outer_state_kernel, half),
        [(3 * 24, width)],
        (own, other, held, got, delta_own, delta_other, ends_3),
    )
    near_keep, near_send, frame = compute(
        functools.partial(inner_end, half),
        [(half - 16, width), (half - 16, width), (half - 8, width)],
        (here_l, here_r, beyond, held, delta_own, after(delta_other, state_3)),
    )
    keep_1, send_1 = compute(
        functools.partial(gather_kernel, half),
        [(half, width)] * 2,
        (ends_l, ends_r, ends_2, ends_3, near_keep, near_send),
    )
    back_1 = routed(send_1, partner)
    keep_2, send_2 = compute(
        functools.partial(middle_end, half),
        [(8, width)] * 2,
        (frame, here_2, held, delta_own, delta_other),
        scratch_shapes=[pltpu.VMEM((24, width), jnp.float32)],
    )
    back_2 = routed(send_2, partner)
    keep_3, send_3 = compute(
        outer_end,
        [(8, width)] * 2,
        (frame, here_2, here_3, after(state_3, keep_2)),
        scratch_shapes=[pltpu.VMEM((24, width), jnp.float32)],
    )
    back_3 = routed(send_3, partner)
    out = written(half, (keep_1, back_1, keep_2, back_2, keep_3), starts.shape)
    return written(half, (back_3,), starts.shape, into=out)


def solution(mesh):
    in_specs = (P(("groups", "tm"), "rows", None), P("rows", None))
    out_specs = P(("groups", "tm"), "rows", None)
    return jax.shard_map(
        on_device, mesh=mesh, in_specs=in_specs, out_specs=out_specs, check_vma=False
    )
```

```python
import functools

import jax
import jax.numpy as jnp
from jax import lax
from jax.experimental import pallas as pl
from jax.experimental.pallas import tpu as pltpu
from jax.sharding import PartitionSpec as P


FINE = 3
WIDE = 8
CUT = 4


diffusion = 2.0
step_fine = 0.1
coarse_step = FINE * step_fine
damping = 1.0 + 4.0 * diffusion * coarse_step

AXES = ("groups", "tm", "rows")


def routed(block, route):
    groups, slices, rows = (lax.axis_size(a) for a in AXES)
    pairs = []
    for g in range(groups):
        for t in range(slices):
            for r in range(rows):
                target = route(g, t, r)
                if target is not None:
                    to_g, to_t, to_r = target
                    source = (g * slices + t) * rows + r
                    pairs.append((source, (to_g * slices + to_t) * rows + to_r))
    return lax.ppermute(block, AXES, pairs)


def partner(g, t, r):
    return g, t ^ 1, r


def outward(groups, rows):
    def route(g, t, r):
        to_r = r + 1 if t & 1 else r - 1
        if 0 <= to_r < rows:
            return g, t ^ 1, to_r
        other = g ^ 1
        return (other, t, r) if other < groups else (g, t, r)

    return route


def stage_swap(stage):
    def route(g, t, r):
        chip = t // 2
        if chip == stage:
            return g, t + 2, r
        if chip == stage + 1:
            return g, t - 2, r
        return g, t, r

    return route


def stage_send(stage):
    def route(g, t, r):
        return (g, t + 2, r) if t // 2 == stage else None

    return route


def around(v):
    height, width = v.shape
    return (pltpu.roll(v, 1, 0) + pltpu.roll(v, height - 1, 0)) + (
        pltpu.roll(v, 1, 1) + pltpu.roll(v, width - 1, 1)
    )


def fine_of(v, nsum, drive):
    return (
        step_fine * diffusion * nsum
        + v * ((1.0 + step_fine - 4.0 * step_fine * diffusion) - step_fine * (v * v))
        + step_fine * drive
    )


def coarse_of(v, nsum, drive):
    scale = coarse_step / damping
    return (
        scale * diffusion * nsum
        + v * ((1.0 + coarse_step) / damping - scale * (v * v))
        + scale * drive
    )


def compute(kernel, outs, args, **kwargs):
    shapes = [jax.ShapeDtypeStruct(o, jnp.float32) for o in outs]
    vmem = pl.BlockSpec(memory_space=pltpu.VMEM)
    return pl.pallas_call(
        kernel,
        out_shape=shapes,
        in_specs=[vmem] * len(args),
        out_specs=[vmem] * len(outs),
        compiler_params=pltpu.CompilerParams(vmem_limit_bytes=16 << 20),
        **kwargs,
    )(*args)


def same(v):
    return v


def start_of(v, drive, kept=same):
    nsum = around(v)
    coarse = kept(coarse_of(v, nsum, drive))
    fine = kept(fine_of(v, nsum, drive))
    for _ in range(FINE - 1):
        fine = kept(fine_of(fine, around(fine), drive))
    return fine, coarse


def ends_of(first, mine, theirs, drive, kept=same):
    f_a, f_b = picked(first, mine[0], theirs[0])
    g_a, g_b = picked(first, mine[1], theirs[1])
    e_a = g_a + (f_a - g_a)
    e_b = kept(coarse_of(e_a, around(e_a), drive)) + (f_b - g_b)
    return e_a, e_b


def chain(current, d_a, d_b, drive, kept=same):
    e_a = kept(coarse_of(current, around(current), drive)) + d_a
    e_b = kept(coarse_of(e_a, around(e_a), drive)) + d_b
    return e_a, e_b


def picked(first, own, other):
    return jnp.where(first, own, other), jnp.where(first, other, own)


def field(ref, kind, kinds, start, size):
    height = ref.shape[0] // kinds
    return ref.at[pl.ds(pl.multiple_of(kind * height + start, 8), size), :]


def mixed(upper, lower):
    row = lax.broadcasted_iota(jnp.int32, upper.shape, 0)
    return jnp.where(row < CUT, upper, lower)


def sublane(v):
    return lax.broadcasted_iota(jnp.int32, v.shape, 0)


def folded(v):
    width = v.shape[1]
    half, quarter = width // 2, width // 4
    four = mixed(v[:, :half], pltpu.roll(v[:, half:], 4, 0))
    row = sublane(four[:, :quarter])
    two = pltpu.roll(v[:, :quarter], 4, 0)
    for i, shift in ((1, 6), (2, 0), (3, 2)):
        part = v[:, i * quarter : (i + 1) * quarter]
        part = pltpu.roll(part, shift, 0) if shift else part
        two = jnp.where(row < 2 * i, two, part)
    return jnp.concatenate([four, two], axis=1)


def unfolded(v):
    half = v.shape[1] * 2 // 3
    four, two = v[:, :half], v[:, half:]
    low = [pltpu.roll(two, 4, 0), pltpu.roll(two, 2, 0), two, pltpu.roll(two, 6, 0)]
    return mixed(
        jnp.concatenate([four, pltpu.roll(four, 4, 0)], axis=1),
        jnp.concatenate(low, axis=1),
    )


def halved(v):
    half = v.shape[1] // 2
    return mixed(v[:, :half], pltpu.roll(v[:, half:], 4, 0))


def unhalved(v):
    return jnp.concatenate([v, pltpu.roll(v, 4, 0)], axis=1)


def place():
    t = lax.axis_index("tm")
    return t % 2, t // 2


def at_edge(core):
    r, rows = lax.axis_index("rows"), lax.axis_size("rows")
    return ((core == 0) & (r == 0)) | ((core == 1) & (r == rows - 1))


def inner_row(half, core):
    return pl.multiple_of(8 + (half - 16) * core, 8)


def middle_row(half, core):
    return pl.multiple_of((2 * half - 16) * core, 8)


def outer_row(half, core):
    return pl.multiple_of((2 * half - WIDE) * core, 8)


def load_kernel(half, starts, drive, own, held, inner, sems):
    core, chip = place()
    copies = []
    for i, (row, size) in enumerate(((8, 2 * half - 16), (0, 8), (2 * half - 8, 8))):
        rows = pl.ds(row, size)
        pair = (
            pltpu.make_async_copy(starts.at[0, rows, :], own.at[rows, :], sems.at[2 * i]),
            pltpu.make_async_copy(drive.at[rows, :], held.at[rows, :], sems.at[2 * i + 1]),
        )
        for copy in pair:
            copy.start()
        copies.append(pair)

    for copy in copies[0]:
        copy.wait()

    @pl.when(chip == 0)
    def _():
        rows = pl.ds(inner_row(half, core), half)
        fine, coarse = start_of(own[rows, :], held[rows, :])
        inner[0:half, :] = fine
        inner[half : 2 * half, :] = coarse

    for copy in (*copies[1], *copies[2]):
        copy.wait()


def inner_kernel(half, side, own, other, drive, mine, sent, ends, edge=None):
    core, chip = place()
    first = core == 0
    width = drive.shape[1]
    mid = width // 2

    def columns(ref, rows):
        if side == 0:
            parts = ref[rows, width - 128 :], ref[rows, : mid + 128]
        else:
            parts = ref[rows, mid - 128 :], ref[rows, :128]
        return jnp.concatenate(parts, axis=1)

    @pl.when(chip == 0)
    def _():
        rows = pl.ds(inner_row(half, core), half)
        d = columns(drive, rows)
        theirs = start_of(columns(other, rows), d)
        known = columns(mine, pl.ds(0, half)), columns(mine, pl.ds(half, half))
        e_a, e_b = ends_of(first, known, theirs, d)
        e_a, e_b = e_a[:, 128:-128], e_b[:, 128:-128]
        frame = pltpu.roll(e_b, half - CUT, 0)
        count = half // 8 - 2
        whole = [
            jnp.where(first, frame[8 * i : 8 * i + 8], frame[8 * i + 8 : 8 * i + 16])
            for i in range(count)
        ]
        part = jnp.where(
            first, frame[8 * count : 8 * count + 8], pltpu.roll(frame[:8], 4, 0)
        )
        sent[...] = jnp.concatenate([*whole, halved(part)], axis=1)
        ends[0:half, :] = e_a
        ends[half : 2 * half, :] = e_b

    if edge is not None:
        rows = pl.ds(outer_row(half, core), 8)
        a, b = picked(first, own[rows, :], other[rows, :])
        fields = (jnp.where(first, v, pltpu.roll(v, 6, 0)) for v in (a, b, drive[rows, :]))
        edge[...] = jnp.concatenate([folded(v) for v in fields], axis=1)


def middle_kernel(half, own, other, drive, sent, ends):
    core, chip = place()
    first = core == 0

    @pl.when(chip == 0)
    def _():
        rows = pl.ds(middle_row(half, core), 16)
        d = drive[rows, :]
        mine, theirs = start_of(own[rows, :], d), start_of(other[rows, :], d)
        e_a, e_b = ends_of(first, mine, theirs, d)
        sent[...] = pltpu.roll(e_b, 16 - CUT, 0)[:8]
        ends[0:16, :] = e_a
        ends[16:32, :] = e_b


def receiver_rows(half, core):
    return pl.ds(pl.multiple_of((half - WIDE) * core, 8), half + WIDE)


def state_kernel(half, own, other, drive, mine, theirs):
    core, chip = place()

    @pl.when(chip > 0)
    def _():
        rows = receiver_rows(half, core)
        for ref, delta in ((own, mine), (other, theirs)):
            fine, coarse = start_of(ref[rows, :], drive[rows, :])
            delta[...] = fine - coarse


def outer_window(half, own, other, drive, got):
    core, _ = place()
    first = core == 0
    rows = pl.ds(outer_row(half, core), 8)
    a, b = picked(first, own[rows, :], other[rows, :])
    near = (a, b, drive[rows, :])
    size = got.shape[1] // 3
    far = [unfolded(got[:, i * size : (i + 1) * size]) for i in range(3)]
    far = [jnp.where(first, pltpu.roll(v, 2, 0), v) for v in far]
    upper = [jnp.where(first, f, n) for f, n in zip(far, near)]
    lower = [jnp.where(first, n, f) for f, n in zip(far, near)]
    a, b, d = (jnp.concatenate(p) for p in zip(upper, lower))
    inside = ~(at_edge(core) & (sublane(a) // 8 == core))

    def kept(v):
        return jnp.where(inside, v, 0.0)

    return kept(a), kept(b), d, kept


def outer_kernel(half, own, other, drive, got, sent, ends):
    core, chip = place()
    first = core == 0
    a, b, d, kept = outer_window(half, own, other, drive, got)
    f_a, g_a = start_of(a, d, kept)

    @pl.when(chip == 0)
    def _():
        f_b, g_b = start_of(b, d, kept)
        e_a = g_a + (f_a - g_a)
        e_b = kept(coarse_of(e_a, around(e_a), d)) + (f_b - g_b)
        frame = pltpu.roll(e_b, 16 - CUT, 0)[:8]
        sent[...] = folded(jnp.where(first, pltpu.roll(frame, 6, 0), frame))
        ends[0:16, :] = e_a
        ends[16:32, :] = e_b

    @pl.when(chip > 0)
    def _():
        ends[0:16, :] = f_a - g_a


def outer_state_kernel(half, own, other, drive, got, mine, theirs, ends, state):
    core, chip = place()
    first = core == 0

    @pl.when(chip > 0)
    def _():
        _, b, d, kept = outer_window(half, own, other, drive, got)
        f_b, g_b = start_of(b, d, kept)
        rows = pl.ds(pl.multiple_of((half - WIDE) * core, 8), 16)
        before = picked(first, mine[rows, :], theirs[rows, :])
        d_rows = pl.ds(pl.multiple_of((2 * half - 16) * core, 8), 16)
        fields = zip((ends[0:16, :], f_b - g_b, d), (*before, drive[d_rows, :]))
        for kind, (v, near) in enumerate(fields):
            top = jnp.where(first, v[:8], near[:8])
            mid = jnp.where(first, mixed(v[8:], near[:8]), mixed(near[8:], v[:8]))
            low = jnp.where(first, near[8:], v[8:])
            state[24 * kind : 24 * kind + 24, :] = jnp.concatenate([top, mid, low])


def boundary_kernel(left, right, rows):
    size = rows.shape[1] // 2
    start = left.shape[1] - size
    rows[:, :size] = left[:, start:]
    rows[:, size:] = right[:, start:]


def inner_end(half, left, right, beyond, drive, mine, theirs, keep, send, frame):
    core, chip = place()
    first = core == 0

    @pl.when(chip > 0)
    def _():
        count = half // 8 - 2
        mid = left.shape[1] * 2 // (2 * count + 1)
        parts = left[...], right[...]

        def across(begin, end, change=same):
            return jnp.concatenate([change(p[:, begin:end]) for p in parts], axis=1)

        whole = [across(i * mid, i * mid + mid) for i in range(count)]
        near = across(count * mid, left.shape[1], unhalved)
        far = [beyond[:, : mid // 2], beyond[:, mid // 2 :]]
        far = jnp.concatenate([unhalved(v) for v in far], axis=1)
        top, low = picked(first, near, far)
        part = mixed(top, pltpu.roll(low, 4, 0))
        upper = [*whole, part]
        lower = [part, *whole]
        rows = jnp.concatenate([jnp.where(first, u, v) for u, v in zip(upper, lower)])
        frame[...] = rows
        current = pltpu.roll(jnp.concatenate([rows, rows[:8]]), CUT, 0)
        into = pl.ds(pl.multiple_of(8 * (1 - core), 8), half)
        d_a, d_b = picked(first, mine[into, :], theirs[into, :])
        d = drive[pl.ds(inner_row(half, core), half), :]
        e_a, e_b = chain(current, d_a, d_b, d)
        put_ends(first, e_a[8 : half - 8], e_b[8 : half - 8], keep, send)


def gather_kernel(half, ends_left, ends_right, middle, outer, near_keep, near_send, keep, send):
    core, chip = place()
    first = core == 0
    near = half - 16

    @pl.when(chip == 0)
    def _():
        def rows(kind, begin, size):
            into = pl.ds(half * kind + begin, size)
            return jnp.concatenate([ends_left[into, :], ends_right[into, :]], axis=1)

        def known(kind):
            two = [field(middle, kind, 2, 8 * i, 8)[...] for i in range(2)]
            last = [field(outer, kind, 2, 8 * i, 8)[...] for i in range(2)]
            beside = [rows(kind, 0, 8), rows(kind, half - 8, 8)]
            return jnp.concatenate(
                [
                    rows(kind, 8, near),
                    jnp.where(first, mixed(two[1], beside[0]), mixed(beside[1], two[0])),
                    jnp.where(first, mixed(last[1], two[0]), mixed(two[1], last[0])),
                ]
            )

        put_ends(first, known(0), known(1), keep, send)

    @pl.when(chip > 0)
    def _():
        keep[0:near, :] = near_keep[...]
        send[0:near, :] = near_send[...]


def put_ends(first, e_a, e_b, keep, send):
    kept, sent = picked(first, e_a, e_b)
    keep[...] = kept
    send[...] = sent


def middle_end(half, inner, middle, drive, mine, theirs, keep, send, current):
    core, chip = place()
    first = core == 0
    last = inner.shape[0] - 16

    @pl.when((chip > 0) & first)
    def _():
        current[...] = pltpu.roll(jnp.concatenate([middle[...], inner[0:16, :]]), CUT, 0)

    @pl.when((chip > 0) & (core == 1))
    def _():
        rows = jnp.concatenate([inner[last : last + 16, :], middle[...]])
        current[...] = pltpu.roll(rows, 24 - CUT, 0)

    @pl.when(chip > 0)
    def _():
        rows = pl.ds(pl.multiple_of((half - 16) * core, 8), 24)
        d_a, d_b = picked(first, mine[rows, :], theirs[rows, :])
        d = drive[pl.ds(pl.multiple_of((2 * half - 24) * core, 8), 24), :]
        e_a, e_b = chain(current[...], d_a, d_b, d)
        put_ends(first, e_a[8:16], e_b[8:16], keep, send)


def outer_end(inner, middle, outer, state, keep, send, current):
    core, chip = place()
    first = core == 0
    last = inner.shape[0] - 8

    @pl.when((chip > 0) & first)
    def _():
        part = pltpu.roll(unfolded(outer[...]), 2, 0)
        rows = jnp.concatenate([part, middle[...], inner[0:8, :]])
        current[...] = pltpu.roll(rows, CUT, 0)

    @pl.when((chip > 0) & (core == 1))
    def _():
        rows = jnp.concatenate([inner[last : last + 8, :], middle[...], unfolded(outer[...])])
        current[...] = pltpu.roll(rows, 24 - CUT, 0)

    @pl.when(chip > 0)
    def _():
        d_a, d_b, d = (field(state, kind, 3, 0, 24)[...] for kind in range(3))
        inside = ~(at_edge(core) & (sublane(d) // 8 == 2 * core))
        e_a = coarse_of(current[...], around(current[...]), d) + d_a
        e_a = jnp.where(inside, e_a, 0.0)
        mid = e_a[8:16]
        width = mid.shape[1]
        beside = pltpu.roll(mid, 1, 1) + pltpu.roll(mid, width - 1, 1)
        upright = pltpu.roll(e_a, 1, 0)[8:16] + pltpu.roll(e_a, 23, 0)[8:16]
        e_b = coarse_of(mid, upright + beside, d[8:16]) + d_b[8:16]
        put_ends(first, mid, e_b, keep, send)


def write_kernel(half, last, *refs):
    pieces, out, sems = refs[: 1 if last else 5], refs[-2], refs[-1]
    core, chip = place()

    def copy_all(order):
        copies = []
        for i, (mine, part, source, begin, size) in enumerate(order):
            upper = (16, 8, 0)[part]
            lower = (half, 2 * half - 16, 2 * half - 8)[part]
            row = pl.multiple_of(jnp.where((core == 0) == mine, upper, lower), 8)
            copy = pltpu.make_async_copy(
                pieces[source].at[pl.ds(begin, size), :],
                out.at[0, pl.ds(row, size), :],
                sems.at[i],
            )
            copy.start()
            copies.append(copy)
        for copy in copies:
            copy.wait()

    if last:

        @pl.when(chip > 0)
        def _():
            copy_all(((False, 2, 0, 0, 8),))

    else:
        near = half - 16

        @pl.when(chip == 0)
        def _():
            parts = ((0, 0, near), (1, near, 8), (2, near + 8, 8))
            copy_all(
                [(mine, part, source, *rows) for mine, source in ((True, 0), (False, 1)) for part, *rows in parts]
            )

        @pl.when(chip > 0)
        def _():
            copy_all(
                (
                    (True, 0, 0, 0, near),
                    (False, 0, 1, 0, near),
                    (True, 1, 2, 0, 8),
                    (False, 1, 3, 0, 8),
                    (True, 2, 4, 0, 8),
                )
            )


def written(half, pieces, shape, into=None):
    vmem, anywhere = pl.BlockSpec(memory_space=pltpu.VMEM), pl.BlockSpec(memory_space=pl.ANY)
    extra = () if into is None else (into,)
    return pl.pallas_call(
        functools.partial(write_kernel, half, into is not None),
        out_shape=jax.ShapeDtypeStruct(shape, jnp.float32),
        in_specs=[vmem] * len(pieces) + [anywhere] * len(extra),
        out_specs=anywhere,
        input_output_aliases={len(pieces): 0} if extra else {},
        scratch_shapes=[pltpu.SemaphoreType.DMA((6,))],
        compiler_params=pltpu.CompilerParams(vmem_limit_bytes=16 << 20),
    )(*pieces, *extra)


def after(value, earlier):
    return lax.optimization_barrier((value, earlier))[0]


def masked_update(update, v, drive, inside):
    wide = (
        jnp.roll(v, 1, axis=0) + jnp.roll(v, -1, axis=0)
    ) + (jnp.roll(v, 1, axis=1) + jnp.roll(v, -1, axis=1))
    return jnp.where(inside, update(v, wide, drive), 0.0)


def long_chain(own, drive):
    height = own.shape[0]
    half = height // 2
    groups, slices, rows = (lax.axis_size(a) for a in AXES)
    t, r = lax.axis_index("tm"), lax.axis_index("rows")
    core, chip = t % 2, t // 2
    first = core == 0
    away = outward(groups, rows)

    def cut(field, start, size):
        return lax.dynamic_slice_in_dim(field, start, size, axis=0)

    other = routed(own, partner)
    s_a, s_b = picked(first, own, other)
    edge = core * (height - WIDE)
    got = routed(jnp.concatenate([cut(f, edge, WIDE) for f in (s_a, s_b, drive)]), away)

    def sided(body, outer, inner):
        return jnp.where(
            first,
            jnp.concatenate([outer, body, inner]),
            jnp.concatenate([inner, body, outer]),
        )

    def window(field, place):
        body = cut(field, core * half, half)
        inner = cut(field, jnp.where(first, half, half - WIDE), WIDE)
        return sided(body, got[place * WIDE : (place + 1) * WIDE], inner)

    w_a, w_b, w_d = (window(f, i) for i, f in enumerate((s_a, s_b, drive)))
    row = lax.broadcasted_iota(jnp.int32, (half + 2 * WIDE, 1), 0)
    row = row + r * height + core * half - WIDE
    inside = (row >= 0) & (row < rows * height)
    w_a, w_b = jnp.where(inside, w_a, 0.0), jnp.where(inside, w_b, 0.0)

    def delta(v):
        fine = v
        for _ in range(FINE):
            fine = masked_update(fine_of, fine, w_d, inside)
        return fine - masked_update(coarse_of, v, w_d, inside)

    d_a, d_b = delta(w_a), delta(w_b)

    def both(v):
        e_a = masked_update(coarse_of, v, w_d, inside) + d_a
        return e_a, masked_update(coarse_of, e_a, w_d, inside) + d_b

    def extended(v):
        last = WIDE + half - 2
        inner = routed(cut(v, jnp.where(first, last, WIDE), 2), partner)
        outer = routed(cut(v, jnp.where(first, WIDE, last), 2), away)
        return sided(v[WIDE : WIDE + half], outer, inner)

    e_a, e_b = both(w_a)
    for stage in range(slices // 2 - 1):
        moved = e_b[WIDE - 2 : WIDE + half + 2] if stage == 0 else extended(e_b)
        arrived = routed(moved, stage_swap(stage))
        current = jnp.pad(arrived, ((WIDE - 2, WIDE - 2), (0, 0)))
        n_a, n_b = both(jnp.where(inside, current, 0.0))
        here = chip == stage + 1
        e_a, e_b = jnp.where(here, n_a, e_a), jnp.where(here, n_b, e_b)

    kept, sent = picked(first, e_a[WIDE : WIDE + half], e_b[WIDE : WIDE + half])
    back = routed(sent, partner)
    return jnp.concatenate(picked(first, kept, back))[None]


def on_device(starts, drive):
    own = starts[0]
    if lax.axis_size("tm") != 4:
        return long_chain(own, drive)
    return two_chips(starts, drive)


def two_chips(starts, drive):
    _, height, width = starts.shape
    half = height // 2
    groups, rows = lax.axis_size("groups"), lax.axis_size("rows")
    vmem = pl.BlockSpec(memory_space=pltpu.VMEM)

    other = routed(starts[0], partner)
    own, held, mine = pl.pallas_call(
        functools.partial(load_kernel, half),
        out_shape=[
            jax.ShapeDtypeStruct((size, width), jnp.float32) for size in (height, height, height)
        ],
        in_specs=[pl.BlockSpec(memory_space=pltpu.HBM)] * 2,
        out_specs=[vmem] * 3,
        scratch_shapes=[pltpu.SemaphoreType.DMA((6,))],
        compiler_params=pltpu.CompilerParams(vmem_limit_bytes=50 << 20),
        cost_estimate=pl.CostEstimate(
            flops=60 * 24 * width, bytes_accessed=16 * height * width, transcendentals=0
        ),
        name="load",
    )(starts, drive)
    mid = width // 2
    packed = mid * (half // 8 - 2) + mid // 2
    sent_l, ends_l = compute(
        functools.partial(inner_kernel, half, 0),
        [(8, packed), (height, mid)],
        (own, other, held, mine),
    )
    here_l = routed(sent_l, stage_swap(0))
    sent_r, ends_r, edge = compute(
        functools.partial(inner_kernel, half, 1),
        [(8, packed), (height, mid), (8, width * 9 // 4)],
        (own, other, held, after(mine, sent_l)),
    )
    here_r = routed(sent_r, stage_swap(0))
    got = routed(edge, outward(groups, rows))
    sent_2, ends_2 = compute(
        functools.partial(middle_kernel, half),
        [(8, width), (32, width)],
        (own, other, after(held, sent_r)),
    )
    here_2 = routed(sent_2, stage_send(0))
    delta_own, delta_other = compute(
        functools.partial(state_kernel, half),
        [(half + WIDE, width)] * 2,
        (own, other, after(held, sent_2)),
    )
    sent_3, ends_3 = compute(
        functools.partial(outer_kernel, half),
        [(8, width * 3 // 4), (32, width)],
        (own, other, after(held, delta_other), got),
    )
    here_3 = routed(sent_3, stage_swap(0))
    (rows_1,) = compute(boundary_kernel, [(8, mid)], (here_l, after(here_r, sent_3)))
    beyond = routed(rows_1, partner)
    (state_3,) = compute(
        functools.partial(outer_state_kernel, half),
        [(3 * 24, width)],
        (own, other, held, got, delta_own, delta_other, ends_3),
    )
    near_keep, near_send, frame = compute(
        functools.partial(inner_end, half),
        [(half - 16, width), (half - 16, width), (half - 8, width)],
        (here_l, here_r, beyond, held, delta_own, after(delta_other, state_3)),
    )
    keep_1, send_1 = compute(
        functools.partial(gather_kernel, half),
        [(half, width)] * 2,
        (ends_l, ends_r, ends_2, ends_3, near_keep, near_send),
    )
    back_1 = routed(send_1, partner)
    keep_2, send_2 = compute(
        functools.partial(middle_end, half),
        [(8, width)] * 2,
        (frame, here_2, held, delta_own, delta_other),
        scratch_shapes=[pltpu.VMEM((24, width), jnp.float32)],
    )
    back_2 = routed(send_2, partner)
    keep_3, send_3 = compute(
        outer_end,
        [(8, width)] * 2,
        (frame, here_2, here_3, after(state_3, keep_2)),
        scratch_shapes=[pltpu.VMEM((24, width), jnp.float32)],
    )
    back_3 = routed(send_3, partner)
    out = written(half, (keep_1, back_1, keep_2, back_2, keep_3), starts.shape)
    return written(half, (back_3,), starts.shape, into=out)


def solution(mesh):
    in_specs = (P(("groups", "tm"), "rows", None), P("rows", None))
    out_specs = P(("groups", "tm"), "rows", None)
    return jax.shard_map(
        on_device, mesh=mesh, in_specs=in_specs, out_specs=out_specs, check_vma=False
    )
```

```python
import functools

import jax
import jax.numpy as jnp
from jax import lax
from jax.experimental import pallas as pl
from jax.experimental.pallas import tpu as pltpu
from jax.sharding import PartitionSpec as P


FINE = 3
WIDE = 8
CUT = 4


diffusion = 2.0
step_fine = 0.1
coarse_step = FINE * step_fine
damping = 1.0 + 4.0 * diffusion * coarse_step

AXES = ("groups", "tm", "rows")


def routed(block, route):
    groups, slices, rows = (lax.axis_size(a) for a in AXES)
    pairs = []
    for g in range(groups):
        for t in range(slices):
            for r in range(rows):
                target = route(g, t, r)
                if target is not None:
                    to_g, to_t, to_r = target
                    source = (g * slices + t) * rows + r
                    pairs.append((source, (to_g * slices + to_t) * rows + to_r))
    return lax.ppermute(block, AXES, pairs)


def partner(g, t, r):
    return g, t ^ 1, r


def outward(groups, rows):
    def route(g, t, r):
        to_r = r + 1 if t & 1 else r - 1
        if 0 <= to_r < rows:
            return g, t ^ 1, to_r
        other = g ^ 1
        return (other, t, r) if other < groups else (g, t, r)

    return route


def stage_swap(stage):
    def route(g, t, r):
        chip = t // 2
        if chip == stage:
            return g, t + 2, r
        if chip == stage + 1:
            return g, t - 2, r
        return g, t, r

    return route


def stage_send(stage):
    def route(g, t, r):
        return (g, t + 2, r) if t // 2 == stage else None

    return route


def around(v):
    height, width = v.shape
    return (pltpu.roll(v, 1, 0) + pltpu.roll(v, height - 1, 0)) + (
        pltpu.roll(v, 1, 1) + pltpu.roll(v, width - 1, 1)
    )


def fine_of(v, nsum, drive):
    return (
        step_fine * diffusion * nsum
        + v * ((1.0 + step_fine - 4.0 * step_fine * diffusion) - step_fine * (v * v))
        + step_fine * drive
    )


def coarse_of(v, nsum, drive):
    scale = coarse_step / damping
    return (
        scale * diffusion * nsum
        + v * ((1.0 + coarse_step) / damping - scale * (v * v))
        + scale * drive
    )


def compute(kernel, outs, args, **kwargs):
    shapes = [jax.ShapeDtypeStruct(o, jnp.float32) for o in outs]
    vmem = pl.BlockSpec(memory_space=pltpu.VMEM)
    return pl.pallas_call(
        kernel,
        out_shape=shapes,
        in_specs=[vmem] * len(args),
        out_specs=[vmem] * len(outs),
        compiler_params=pltpu.CompilerParams(vmem_limit_bytes=16 << 20),
        **kwargs,
    )(*args)


def same(v):
    return v


def start_of(v, drive, kept=same):
    nsum = around(v)
    coarse = kept(coarse_of(v, nsum, drive))
    fine = kept(fine_of(v, nsum, drive))
    for _ in range(FINE - 1):
        fine = kept(fine_of(fine, around(fine), drive))
    return fine, coarse


def ends_of(first, mine, theirs, drive, kept=same):
    f_a, f_b = picked(first, mine[0], theirs[0])
    g_a, g_b = picked(first, mine[1], theirs[1])
    e_a = g_a + (f_a - g_a)
    e_b = kept(coarse_of(e_a, around(e_a), drive)) + (f_b - g_b)
    return e_a, e_b


def chain(current, d_a, d_b, drive, kept=same):
    e_a = kept(coarse_of(current, around(current), drive)) + d_a
    e_b = kept(coarse_of(e_a, around(e_a), drive)) + d_b
    return e_a, e_b


def picked(first, own, other):
    return jnp.where(first, own, other), jnp.where(first, other, own)


def field(ref, kind, kinds, start, size):
    height = ref.shape[0] // kinds
    return ref.at[pl.ds(pl.multiple_of(kind * height + start, 8), size), :]


def mixed(upper, lower):
    row = lax.broadcasted_iota(jnp.int32, upper.shape, 0)
    return jnp.where(row < CUT, upper, lower)


def sublane(v):
    return lax.broadcasted_iota(jnp.int32, v.shape, 0)


def folded(v):
    width = v.shape[1]
    half, quarter = width // 2, width // 4
    four = mixed(v[:, :half], pltpu.roll(v[:, half:], 4, 0))
    row = sublane(four[:, :quarter])
    two = pltpu.roll(v[:, :quarter], 4, 0)
    for i, shift in ((1, 6), (2, 0), (3, 2)):
        part = v[:, i * quarter : (i + 1) * quarter]
        part = pltpu.roll(part, shift, 0) if shift else part
        two = jnp.where(row < 2 * i, two, part)
    return jnp.concatenate([four, two], axis=1)


def unfolded(v):
    half = v.shape[1] * 2 // 3
    four, two = v[:, :half], v[:, half:]
    low = [pltpu.roll(two, 4, 0), pltpu.roll(two, 2, 0), two, pltpu.roll(two, 6, 0)]
    return mixed(
        jnp.concatenate([four, pltpu.roll(four, 4, 0)], axis=1),
        jnp.concatenate(low, axis=1),
    )


def halved(v):
    half = v.shape[1] // 2
    return mixed(v[:, :half], pltpu.roll(v[:, half:], 4, 0))


def unhalved(v):
    return jnp.concatenate([v, pltpu.roll(v, 4, 0)], axis=1)


def place():
    t = lax.axis_index("tm")
    return t % 2, t // 2


def at_edge(core):
    r, rows = lax.axis_index("rows"), lax.axis_size("rows")
    return ((core == 0) & (r == 0)) | ((core == 1) & (r == rows - 1))


def inner_row(half, core):
    return pl.multiple_of(8 + (half - 16) * core, 8)


def middle_row(half, core):
    return pl.multiple_of((2 * half - 16) * core, 8)


def outer_row(half, core):
    return pl.multiple_of((2 * half - WIDE) * core, 8)


def load_kernel(half, starts, drive, own, held, inner, sems):
    core, chip = place()
    copies = []
    for i, (row, size) in enumerate(((8, 2 * half - 16), (0, 8), (2 * half - 8, 8))):
        rows = pl.ds(row, size)
        pair = (
            pltpu.make_async_copy(starts.at[0, rows, :], own.at[rows, :], sems.at[2 * i]),
            pltpu.make_async_copy(drive.at[rows, :], held.at[rows, :], sems.at[2 * i + 1]),
        )
        for copy in pair:
            copy.start()
        copies.append(pair)

    for copy in copies[0]:
        copy.wait()

    @pl.when(chip == 0)
    def _():
        rows = pl.ds(inner_row(half, core), half)
        fine, coarse = start_of(own[rows, :], held[rows, :])
        inner[0:half, :] = fine
        inner[half : 2 * half, :] = coarse

    for copy in (*copies[1], *copies[2]):
        copy.wait()


def inner_kernel(half, side, own, other, drive, mine, sent, ends, edge=None):
    core, chip = place()
    first = core == 0
    width = drive.shape[1]
    mid = width // 2

    def columns(ref, rows):
        if side == 0:
            parts = ref[rows, width - 128 :], ref[rows, : mid + 128]
        else:
            parts = ref[rows, mid - 128 :], ref[rows, :128]
        return jnp.concatenate(parts, axis=1)

    @pl.when(chip == 0)
    def _():
        rows = pl.ds(inner_row(half, core), half)
        d = columns(drive, rows)
        theirs = start_of(columns(other, rows), d)
        known = columns(mine, pl.ds(0, half)), columns(mine, pl.ds(half, half))
        e_a, e_b = ends_of(first, known, theirs, d)
        e_a, e_b = e_a[:, 128:-128], e_b[:, 128:-128]
        frame = pltpu.roll(e_b, half - CUT, 0)
        count = half // 8 - 2
        whole = [
            jnp.where(first, frame[8 * i : 8 * i + 8], frame[8 * i + 8 : 8 * i + 16])
            for i in range(count)
        ]
        part = jnp.where(
            first, frame[8 * count : 8 * count + 8], pltpu.roll(frame[:8], 4, 0)
        )
        sent[...] = jnp.concatenate([*whole, halved(part)], axis=1)
        ends[0:half, :] = e_a
        ends[half : 2 * half, :] = e_b

    if edge is not None:
        rows = pl.ds(outer_row(half, core), 8)
        a, b = picked(first, own[rows, :], other[rows, :])
        fields = (jnp.where(first, v, pltpu.roll(v, 6, 0)) for v in (a, b, drive[rows, :]))
        edge[...] = jnp.concatenate([folded(v) for v in fields], axis=1)


def middle_kernel(half, own, other, drive, sent, ends):
    core, chip = place()
    first = core == 0

    @pl.when(chip == 0)
    def _():
        rows = pl.ds(middle_row(half, core), 16)
        d = drive[rows, :]
        mine, theirs = start_of(own[rows, :], d), start_of(other[rows, :], d)
        e_a, e_b = ends_of(first, mine, theirs, d)
        sent[...] = pltpu.roll(e_b, 16 - CUT, 0)[:8]
        ends[0:16, :] = e_a
        ends[16:32, :] = e_b


def receiver_rows(half, core):
    return pl.ds(pl.multiple_of((half - WIDE) * core, 8), half + WIDE)


def state_kernel(half, own, other, drive, mine, theirs):
    core, chip = place()

    @pl.when(chip > 0)
    def _():
        rows = receiver_rows(half, core)
        for ref, delta in ((own, mine), (other, theirs)):
            fine, coarse = start_of(ref[rows, :], drive[rows, :])
            delta[...] = fine - coarse


def outer_window(half, own, other, drive, got):
    core, _ = place()
    first = core == 0
    rows = pl.ds(outer_row(half, core), 8)
    a, b = picked(first, own[rows, :], other[rows, :])
    near = (a, b, drive[rows, :])
    size = got.shape[1] // 3
    far = [unfolded(got[:, i * size : (i + 1) * size]) for i in range(3)]
    far = [jnp.where(first, pltpu.roll(v, 2, 0), v) for v in far]
    upper = [jnp.where(first, f, n) for f, n in zip(far, near)]
    lower = [jnp.where(first, n, f) for f, n in zip(far, near)]
    a, b, d = (jnp.concatenate(p) for p in zip(upper, lower))
    inside = ~(at_edge(core) & (sublane(a) // 8 == core))

    def kept(v):
        return jnp.where(inside, v, 0.0)

    return kept(a), kept(b), d, kept


def outer_kernel(half, own, other, drive, got, sent, ends):
    core, chip = place()
    first = core == 0

    @pl.when(chip == 0)
    def _():
        a, b, d, kept = outer_window(half, own, other, drive, got)
        (f_a, g_a), (f_b, g_b) = start_of(a, d, kept), start_of(b, d, kept)
        e_a = g_a + (f_a - g_a)
        e_b = kept(coarse_of(e_a, around(e_a), d)) + (f_b - g_b)
        frame = pltpu.roll(e_b, 16 - CUT, 0)[:8]
        sent[...] = folded(jnp.where(first, pltpu.roll(frame, 6, 0), frame))
        ends[0:16, :] = e_a
        ends[16:32, :] = e_b


def outer_state_kernel(half, own, other, drive, got, mine, theirs, state):
    core, chip = place()
    first = core == 0

    @pl.when(chip > 0)
    def _():
        a, b, d, kept = outer_window(half, own, other, drive, got)
        (f_a, g_a), (f_b, g_b) = start_of(a, d, kept), start_of(b, d, kept)
        rows = pl.ds(pl.multiple_of((half - WIDE) * core, 8), 16)
        before = picked(first, mine[rows, :], theirs[rows, :])
        d_rows = pl.ds(pl.multiple_of((2 * half - 16) * core, 8), 16)
        fields = zip((f_a - g_a, f_b - g_b, d), (*before, drive[d_rows, :]))
        for kind, (v, near) in enumerate(fields):
            top = jnp.where(first, v[:8], near[:8])
            mid = jnp.where(first, mixed(v[8:], near[:8]), mixed(near[8:], v[:8]))
            low = jnp.where(first, near[8:], v[8:])
            state[24 * kind : 24 * kind + 24, :] = jnp.concatenate([top, mid, low])


def boundary_kernel(left, right, rows):
    size = rows.shape[1] // 2
    start = left.shape[1] - size
    rows[:, :size] = left[:, start:]
    rows[:, size:] = right[:, start:]


def inner_end(half, left, right, beyond, drive, mine, theirs, keep, send, frame):
    core, chip = place()
    first = core == 0

    @pl.when(chip > 0)
    def _():
        count = half // 8 - 2
        mid = left.shape[1] * 2 // (2 * count + 1)
        parts = left[...], right[...]

        def across(begin, end, change=same):
            return jnp.concatenate([change(p[:, begin:end]) for p in parts], axis=1)

        whole = [across(i * mid, i * mid + mid) for i in range(count)]
        near = across(count * mid, left.shape[1], unhalved)
        far = [beyond[:, : mid // 2], beyond[:, mid // 2 :]]
        far = jnp.concatenate([unhalved(v) for v in far], axis=1)
        top, low = picked(first, near, far)
        part = mixed(top, pltpu.roll(low, 4, 0))
        upper = [*whole, part]
        lower = [part, *whole]
        rows = jnp.concatenate([jnp.where(first, u, v) for u, v in zip(upper, lower)])
        frame[...] = rows
        current = pltpu.roll(jnp.concatenate([rows, rows[:8]]), CUT, 0)
        into = pl.ds(pl.multiple_of(8 * (1 - core), 8), half)
        d_a, d_b = picked(first, mine[into, :], theirs[into, :])
        d = drive[pl.ds(inner_row(half, core), half), :]
        e_a, e_b = chain(current, d_a, d_b, d)
        put_ends(first, e_a[8 : half - 8], e_b[8 : half - 8], keep, send)


def gather_kernel(half, ends_left, ends_right, middle, outer, near_keep, near_send, keep, send):
    core, chip = place()
    first = core == 0
    near = half - 16

    @pl.when(chip == 0)
    def _():
        def rows(kind, begin, size):
            into = pl.ds(half * kind + begin, size)
            return jnp.concatenate([ends_left[into, :], ends_right[into, :]], axis=1)

        def known(kind):
            two = [field(middle, kind, 2, 8 * i, 8)[...] for i in range(2)]
            last = [field(outer, kind, 2, 8 * i, 8)[...] for i in range(2)]
            beside = [rows(kind, 0, 8), rows(kind, half - 8, 8)]
            return jnp.concatenate(
                [
                    rows(kind, 8, near),
                    jnp.where(first, mixed(two[1], beside[0]), mixed(beside[1], two[0])),
                    jnp.where(first, mixed(last[1], two[0]), mixed(two[1], last[0])),
                ]
            )

        put_ends(first, known(0), known(1), keep, send)

    @pl.when(chip > 0)
    def _():
        keep[0:near, :] = near_keep[...]
        send[0:near, :] = near_send[...]


def put_ends(first, e_a, e_b, keep, send):
    kept, sent = picked(first, e_a, e_b)
    keep[...] = kept
    send[...] = sent


def middle_end(half, inner, middle, drive, mine, theirs, keep, send, current):
    core, chip = place()
    first = core == 0
    last = inner.shape[0] - 16

    @pl.when((chip > 0) & first)
    def _():
        current[...] = pltpu.roll(jnp.concatenate([middle[...], inner[0:16, :]]), CUT, 0)

    @pl.when((chip > 0) & (core == 1))
    def _():
        rows = jnp.concatenate([inner[last : last + 16, :], middle[...]])
        current[...] = pltpu.roll(rows, 24 - CUT, 0)

    @pl.when(chip > 0)
    def _():
        rows = pl.ds(pl.multiple_of((half - 16) * core, 8), 24)
        d_a, d_b = picked(first, mine[rows, :], theirs[rows, :])
        d = drive[pl.ds(pl.multiple_of((2 * half - 24) * core, 8), 24), :]
        e_a, e_b = chain(current[...], d_a, d_b, d)
        put_ends(first, e_a[8:16], e_b[8:16], keep, send)


def outer_end(inner, middle, outer, state, keep, send, current):
    core, chip = place()
    first = core == 0
    last = inner.shape[0] - 8

    @pl.when((chip > 0) & first)
    def _():
        part = pltpu.roll(unfolded(outer[...]), 2, 0)
        rows = jnp.concatenate([part, middle[...], inner[0:8, :]])
        current[...] = pltpu.roll(rows, CUT, 0)

    @pl.when((chip > 0) & (core == 1))
    def _():
        rows = jnp.concatenate([inner[last : last + 8, :], middle[...], unfolded(outer[...])])
        current[...] = pltpu.roll(rows, 24 - CUT, 0)

    @pl.when(chip > 0)
    def _():
        d_a, d_b, d = (field(state, kind, 3, 0, 24)[...] for kind in range(3))
        inside = ~(at_edge(core) & (sublane(d) // 8 == 2 * core))
        e_a = coarse_of(current[...], around(current[...]), d) + d_a
        e_a = jnp.where(inside, e_a, 0.0)
        mid = e_a[8:16]
        width = mid.shape[1]
        beside = pltpu.roll(mid, 1, 1) + pltpu.roll(mid, width - 1, 1)
        upright = pltpu.roll(e_a, 1, 0)[8:16] + pltpu.roll(e_a, 23, 0)[8:16]
        e_b = coarse_of(mid, upright + beside, d[8:16]) + d_b[8:16]
        put_ends(first, mid, e_b, keep, send)


def write_kernel(half, last, *refs):
    pieces, out, sems = refs[: 1 if last else 5], refs[-2], refs[-1]
    core, chip = place()

    def copy_all(order):
        copies = []
        for i, (mine, part, source, begin, size) in enumerate(order):
            upper = (16, 8, 0)[part]
            lower = (half, 2 * half - 16, 2 * half - 8)[part]
            row = pl.multiple_of(jnp.where((core == 0) == mine, upper, lower), 8)
            copy = pltpu.make_async_copy(
                pieces[source].at[pl.ds(begin, size), :],
                out.at[0, pl.ds(row, size), :],
                sems.at[i],
            )
            copy.start()
            copies.append(copy)
        for copy in copies:
            copy.wait()

    if last:

        @pl.when(chip > 0)
        def _():
            copy_all(((False, 2, 0, 0, 8),))

    else:
        near = half - 16

        @pl.when(chip == 0)
        def _():
            parts = ((0, 0, near), (1, near, 8), (2, near + 8, 8))
            copy_all(
                [(mine, part, source, *rows) for mine, source in ((True, 0), (False, 1)) for part, *rows in parts]
            )

        @pl.when(chip > 0)
        def _():
            copy_all(
                (
                    (True, 0, 0, 0, near),
                    (False, 0, 1, 0, near),
                    (True, 1, 2, 0, 8),
                    (False, 1, 3, 0, 8),
                    (True, 2, 4, 0, 8),
                )
            )


def written(half, pieces, shape, into=None):
    vmem, anywhere = pl.BlockSpec(memory_space=pltpu.VMEM), pl.BlockSpec(memory_space=pl.ANY)
    extra = () if into is None else (into,)
    return pl.pallas_call(
        functools.partial(write_kernel, half, into is not None),
        out_shape=jax.ShapeDtypeStruct(shape, jnp.float32),
        in_specs=[vmem] * len(pieces) + [anywhere] * len(extra),
        out_specs=anywhere,
        input_output_aliases={len(pieces): 0} if extra else {},
        scratch_shapes=[pltpu.SemaphoreType.DMA((6,))],
        compiler_params=pltpu.CompilerParams(vmem_limit_bytes=16 << 20),
    )(*pieces, *extra)


def after(value, earlier):
    return lax.optimization_barrier((value, earlier))[0]


def masked_update(update, v, drive, inside):
    wide = (
        jnp.roll(v, 1, axis=0) + jnp.roll(v, -1, axis=0)
    ) + (jnp.roll(v, 1, axis=1) + jnp.roll(v, -1, axis=1))
    return jnp.where(inside, update(v, wide, drive), 0.0)


def long_chain(own, drive):
    height = own.shape[0]
    half = height // 2
    groups, slices, rows = (lax.axis_size(a) for a in AXES)
    t, r = lax.axis_index("tm"), lax.axis_index("rows")
    core, chip = t % 2, t // 2
    first = core == 0
    away = outward(groups, rows)

    def cut(field, start, size):
        return lax.dynamic_slice_in_dim(field, start, size, axis=0)

    other = routed(own, partner)
    s_a, s_b = picked(first, own, other)
    edge = core * (height - WIDE)
    got = routed(jnp.concatenate([cut(f, edge, WIDE) for f in (s_a, s_b, drive)]), away)

    def sided(body, outer, inner):
        return jnp.where(
            first,
            jnp.concatenate([outer, body, inner]),
            jnp.concatenate([inner, body, outer]),
        )

    def window(field, place):
        body = cut(field, core * half, half)
        inner = cut(field, jnp.where(first, half, half - WIDE), WIDE)
        return sided(body, got[place * WIDE : (place + 1) * WIDE], inner)

    w_a, w_b, w_d = (window(f, i) for i, f in enumerate((s_a, s_b, drive)))
    row = lax.broadcasted_iota(jnp.int32, (half + 2 * WIDE, 1), 0)
    row = row + r * height + core * half - WIDE
    inside = (row >= 0) & (row < rows * height)
    w_a, w_b = jnp.where(inside, w_a, 0.0), jnp.where(inside, w_b, 0.0)

    def delta(v):
        fine = v
        for _ in range(FINE):
            fine = masked_update(fine_of, fine, w_d, inside)
        return fine - masked_update(coarse_of, v, w_d, inside)

    d_a, d_b = delta(w_a), delta(w_b)

    def both(v):
        e_a = masked_update(coarse_of, v, w_d, inside) + d_a
        return e_a, masked_update(coarse_of, e_a, w_d, inside) + d_b

    def extended(v):
        last = WIDE + half - 2
        inner = routed(cut(v, jnp.where(first, last, WIDE), 2), partner)
        outer = routed(cut(v, jnp.where(first, WIDE, last), 2), away)
        return sided(v[WIDE : WIDE + half], outer, inner)

    e_a, e_b = both(w_a)
    for stage in range(slices // 2 - 1):
        moved = e_b[WIDE - 2 : WIDE + half + 2] if stage == 0 else extended(e_b)
        arrived = routed(moved, stage_swap(stage))
        current = jnp.pad(arrived, ((WIDE - 2, WIDE - 2), (0, 0)))
        n_a, n_b = both(jnp.where(inside, current, 0.0))
        here = chip == stage + 1
        e_a, e_b = jnp.where(here, n_a, e_a), jnp.where(here, n_b, e_b)

    kept, sent = picked(first, e_a[WIDE : WIDE + half], e_b[WIDE : WIDE + half])
    back = routed(sent, partner)
    return jnp.concatenate(picked(first, kept, back))[None]


def on_device(starts, drive):
    own = starts[0]
    if lax.axis_size("tm") != 4:
        return long_chain(own, drive)
    return two_chips(starts, drive)


def two_chips(starts, drive):
    _, height, width = starts.shape
    half = height // 2
    groups, rows = lax.axis_size("groups"), lax.axis_size("rows")
    vmem = pl.BlockSpec(memory_space=pltpu.VMEM)

    other = routed(starts[0], partner)
    own, held, mine = pl.pallas_call(
        functools.partial(load_kernel, half),
        out_shape=[
            jax.ShapeDtypeStruct((size, width), jnp.float32) for size in (height, height, height)
        ],
        in_specs=[pl.BlockSpec(memory_space=pltpu.HBM)] * 2,
        out_specs=[vmem] * 3,
        scratch_shapes=[pltpu.SemaphoreType.DMA((6,))],
        compiler_params=pltpu.CompilerParams(vmem_limit_bytes=50 << 20),
        cost_estimate=pl.CostEstimate(
            flops=60 * 24 * width, bytes_accessed=16 * height * width, transcendentals=0
        ),
        name="load",
    )(starts, drive)
    mid = width // 2
    packed = mid * (half // 8 - 2) + mid // 2
    sent_l, ends_l = compute(
        functools.partial(inner_kernel, half, 0),
        [(8, packed), (height, mid)],
        (own, other, held, mine),
    )
    here_l = routed(sent_l, stage_swap(0))
    sent_r, ends_r, edge = compute(
        functools.partial(inner_kernel, half, 1),
        [(8, packed), (height, mid), (8, width * 9 // 4)],
        (own, other, held, after(mine, sent_l)),
    )
    here_r = routed(sent_r, stage_swap(0))
    got = routed(edge, outward(groups, rows))
    sent_2, ends_2 = compute(
        functools.partial(middle_kernel, half),
        [(8, width), (32, width)],
        (own, other, after(held, sent_r)),
    )
    here_2 = routed(sent_2, stage_send(0))
    delta_own, delta_other = compute(
        functools.partial(state_kernel, half),
        [(half + WIDE, width)] * 2,
        (own, other, after(held, sent_2)),
    )
    sent_3, ends_3 = compute(
        functools.partial(outer_kernel, half),
        [(8, width * 3 // 4), (32, width)],
        (own, other, after(held, delta_other), got),
    )
    here_3 = routed(sent_3, stage_swap(0))
    (rows_1,) = compute(boundary_kernel, [(8, mid)], (here_l, after(here_r, sent_3)))
    beyond = routed(rows_1, partner)
    (state_3,) = compute(
        functools.partial(outer_state_kernel, half),
        [(3 * 24, width)],
        (own, other, held, got, delta_own, delta_other),
    )
    near_keep, near_send, frame = compute(
        functools.partial(inner_end, half),
        [(half - 16, width), (half - 16, width), (half - 8, width)],
        (here_l, here_r, beyond, held, delta_own, after(delta_other, state_3)),
    )
    keep_1, send_1 = compute(
        functools.partial(gather_kernel, half),
        [(half, width)] * 2,
        (ends_l, ends_r, ends_2, ends_3, near_keep, near_send),
    )
    back_1 = routed(send_1, partner)
    keep_2, send_2 = compute(
        functools.partial(middle_end, half),
        [(8, width)] * 2,
        (frame, here_2, held, delta_own, delta_other),
        scratch_shapes=[pltpu.VMEM((24, width), jnp.float32)],
    )
    back_2 = routed(send_2, partner)
    keep_3, send_3 = compute(
        outer_end,
        [(8, width)] * 2,
        (frame, here_2, here_3, after(state_3, keep_2)),
        scratch_shapes=[pltpu.VMEM((24, width), jnp.float32)],
    )
    back_3 = routed(send_3, partner)
    out = written(half, (keep_1, back_1, keep_2, back_2, keep_3), starts.shape)
    return written(half, (back_3,), starts.shape, into=out)


def solution(mesh):
    in_specs = (P(("groups", "tm"), "rows", None), P("rows", None))
    out_specs = P(("groups", "tm"), "rows", None)
    return jax.shard_map(
        on_device, mesh=mesh, in_specs=in_specs, out_specs=out_specs, check_vma=False
    )
```
